32 devices in a mesh: page: 8 (over z, x), seq: 4 (over y, core).
Axes of the slice: x: 2, y: 2, z: 4, core: 2. Of those that a mesh axis runs over, the one named last changes fastest.
Arguments:
- tokens: bfloat16 [16, 512, 1024], P('page', 'seq'), may hold values from -6 to 6
- cells: int32 [16, 512], P('page', 'seq'), may hold values from 0 to 511, as said below
- lengths: int32 [16], P('page'), may hold values from 64 to 512, as said below
- cotangent: bfloat16 [16, 512, 1024], P('page', 'seq'), may hold values from -6 to 6
- w_qkv: float32 [1024, 3072], P(('page', 'seq')), may hold values from -0.1875 to 0.1875
- w_out: float32 [1024, 1024], P(('page', 'seq')), may hold values from -0.75 to 0.75
- w_up: float32 [1024, 4096], P(('page', 'seq')), may hold values from -0.1875 to 0.1875
- w_down: float32 [4096, 1024], P(('page', 'seq')), may hold values from -0.09375 to 0.09375
- biases: float32 [10, 1024], P(None, ('page', 'seq')), may hold values from -3 to 3
- gains: float32 [2, 1024], P(None, ('page', 'seq')), may hold values from 0.5 to 1.5
- cell_bias: float32 [16], replicated, may hold values from 0.5 to 2
Outputs:
- output: bfloat16 [16, 512, 1024], P('page', 'seq')
- grad_tokens: float32 [16, 512, 1024], P('page', 'seq')
- grad_qkv: float32 [1024, 3072], P(('page', 'seq'))
- grad_out: float32 [1024, 1024], P(('page', 'seq'))
- grad_up: float32 [1024, 4096], P(('page', 'seq'))
- grad_down: float32 [4096, 1024], P(('page', 'seq'))
- grad_biases: float32 [10, 1024], P(None, ('page', 'seq'))
- grad_gains: float32 [2, 1024], P(None, ('page', 'seq'))
- grad_cell: float32 [16], replicated
The draws below stay inside these ranges and needn't reach their ends.
Inputs may be any that keep to these rules, and one draw needn't show every extreme that they name: `lengths`: every page has at least 64 valid tokens, and some page is full. `cells`: within a page cell numbers never fall, rise by at most one from token to token, and the first token is in cell 0; some page has every token in a cell of its own.
All inputs are finite; a program needn't handle non-finite values.
Results may differ from the reference program's by a relative error of at most 0.014.
The reference program's roundings to bfloat16 on the way count: a program that leaves them out, or rounds other values in their place, can miss the bound.
Values may be sent and summed in bfloat16 or wider, within the bound.
No kernel may reach another device: no remote copies, remote signals or barrier semaphores. Data moves between devices by JAX's collectives and lax.ppermute only.
A program may use at most 256 MiB of HBM per device.

```python
import math
import jax
import jax.numpy as jnp
from jax import lax

D = 1024
HEADS = 16
FF = 4096
L = 512
PAGES = 16


def draw_lengths(key, part):
    values = jax.random.randint(key, (PAGES,), L // 8, L + 1)
    return values.at[0].set(L).astype(jnp.int32)


def draw_cells(key, part):
    marks = jax.random.randint(key, (PAGES, L), 0, 4)
    marks = marks.at[0].set(0)
    starts = (marks == 0).astype(jnp.int32)
    return (jnp.cumsum(starts, axis=1) - starts[:, :1]).astype(jnp.int32)


def shard_levels(rng, extent, pieces, low, top_value):
    def one(dim, shards_of):
        draws = jax.random.uniform(jax.random.fold_in(jax.random.fold_in(rng, 6), dim), (shards_of,), jnp.float32, low / len(pieces), top_value / len(pieces))
        return jnp.repeat(jnp.exp(draws), extent[dim] // shards_of).reshape((-1,) + (1,) * (len(extent) - dim - 1))

    loudness = one(*pieces[0])
    for cut in pieces[1:]:
        loudness = loudness * one(*cut)
    return loudness


def normal_values(own_key, dims, scale, most, pieces=(), dtype=jnp.bfloat16):
    entries = jax.random.normal(own_key, dims, jnp.float32) * scale
    if len(pieces) > 0:
        entries = shard_levels(own_key, dims, pieces, -0.22, 0.18) * entries
    return jnp.clip(entries, min=-most, max=most).astype(dtype)


def setup_inputs(seed: int = 0) -> dict:
    arg_keys = jax.random.split(jax.random.key(seed), 12)
    tokens = normal_values(arg_keys[0], (PAGES, L, D), 1.0, 6.0, ((0, 8), (1, 4)))
    cells = draw_cells(jax.random.fold_in(arg_keys[11], 71), 0)
    lengths = draw_lengths(jax.random.fold_in(arg_keys[11], 71), 0)
    cotangent = normal_values(arg_keys[3], (PAGES, L, D), 1.0, 6.0, ((0, 8), (1, 4)))
    w_qkv = normal_values(arg_keys[4], (D, 3 * D), D ** -0.5, 0.1875, ((0, 32),), jnp.float32)
    w_out = normal_values(arg_keys[5], (D, D), (D // 16) ** -0.5, 0.75, ((0, 32),), jnp.float32)
    w_up = normal_values(arg_keys[6], (D, FF), D ** -0.5, 0.1875, ((0, 32),), jnp.float32)
    w_down = normal_values(arg_keys[7], (FF, D), FF ** -0.5, 0.09375, ((0, 32),), jnp.float32)
    biases = normal_values(arg_keys[8], (10, D), 0.5, 3.0, ((1, 32),), jnp.float32)
    gains = jnp.clip(1.0 + 0.1 * jax.random.normal(arg_keys[9], (2, D), jnp.float32), 0.5, 1.5)
    cell_bias = jnp.clip(jax.random.uniform(arg_keys[10], (HEADS,), jnp.float32, 0.5, 2.0), 0.5, 2.0)
    return dict(tokens=tokens, cells=cells, lengths=lengths, cotangent=cotangent, w_qkv=w_qkv, w_out=w_out, w_up=w_up, w_down=w_down, biases=biases, gains=gains, cell_bias=cell_bias)


@jax.custom_vjp
def low(v):
    return lax.optimization_barrier(v.astype(jnp.bfloat16)).astype(jnp.float32)

@jax.custom_vjp
def low_back(v):
    return v

def low_keep(v):
    return (low(v), None)

def low_pass(kept, grad):
    return (grad,)

def back_keep(v):
    return (v, None)

def back_low(kept, grad):
    return (low(grad),)
low.defvjp(low_keep, low_pass)
low_back.defvjp(back_keep, back_low)

def product(left, right):
    return jnp.dot(left, right, precision=lax.Precision.HIGHEST)

def layer_norm(values, gain, shift):
    center = values - lax.optimization_barrier(jnp.mean(values, axis=-1, keepdims=True))
    spread = lax.optimization_barrier(jnp.mean(center * center, axis=-1, keepdims=True))
    return center * lax.rsqrt(spread + 1e-05) * gain + shift

def gelu_exact(values):
    return 0.5 * values * (1.0 + jax.scipy.special.erf(values * 0.7071067811865476))

def layer_block(params, page_x, page_cells, page_lens):
    w_proj, w_mix, w_expand, w_reduce, vectors, scales, bias_cell = params
    group_count, slot_count, width_full = page_x.shape
    head_count = bias_cell.shape[0]
    head_depth = width_full // head_count
    bias_qkv = jnp.concatenate([vectors[0], jnp.zeros_like(vectors[0]), vectors[1]])
    projected = low(low_back(product(page_x, w_proj)) + bias_qkv)
    query = projected[..., :width_full].reshape(group_count, slot_count, head_count, head_depth)
    keys = projected[..., width_full:2 * width_full].reshape(group_count, slot_count, head_count, head_depth)
    values = projected[..., 2 * width_full:].reshape(group_count, slot_count, head_count, head_depth)
    raw_scores = low_back(jnp.einsum('gqhe,gkhe->ghqk', query, keys, precision=lax.Precision.HIGHEST) * 0.125)
    same_cell = (page_cells[:, :, None] == page_cells[:, None, :]).astype(jnp.float32)
    key_valid = lax.broadcasted_iota(jnp.int32, (group_count, slot_count), 1) < page_lens[:, None]
    scores = raw_scores + bias_cell[None, :, None, None] * same_cell[:, None]
    scores = jnp.where(key_valid[:, None, None, :], scores, -1e+30)
    weights = low(jax.nn.softmax(scores, axis=-1))
    context = jnp.einsum('ghqk,gkhe->gqhe', weights, values, precision=lax.Precision.HIGHEST)
    context = low(low_back(context.reshape(group_count, slot_count, width_full)))
    attended = low_back(product(context, w_mix)) + vectors[2]
    normed = layer_norm(page_x + attended, scales[0], vectors[4])
    expanded = low_back(product(low(normed), w_expand)) + vectors[6:10].reshape(-1)
    activated = low(gelu_exact(expanded))
    reduced = low_back(product(activated, w_reduce)) + vectors[3]
    return layer_norm(normed + reduced, scales[1], vectors[5])

def reference(tokens, cells, lengths, cotangent, w_qkv, w_out, w_up, w_down, biases, gains, cell_bias):
    page_total = tokens.shape[0]
    group_size = math.gcd(page_total, 8)
    group_total = page_total // group_size

    def forward(masters, flat_x):
        w_proj, w_mix, w_expand, w_reduce, vectors, scales, bias_cell = masters
        params = (low(w_proj), low(w_mix), low(w_expand), low(w_reduce), low(vectors), low(scales), bias_cell)

        def group_step(item):
            return layer_block(params, item[0], item[1], item[2])
        outs = lax.map(jax.checkpoint(group_step), (flat_x.reshape(group_total, group_size, L, D), cells.reshape(group_total, group_size, L), lengths.reshape(group_total, group_size)))
        return outs.reshape(page_total, L, D)
    masters = (w_qkv, w_out, w_up, w_down, biases, gains, cell_bias)
    result, pullback = jax.vjp(forward, masters, tokens.astype(jnp.float32))
    grad_masters, grad_inputs = pullback(cotangent.astype(jnp.float32))
    return (result.astype(jnp.bfloat16), grad_inputs, grad_masters[0], grad_masters[1], grad_masters[2], grad_masters[3], grad_masters[4], grad_masters[5], grad_masters[6])
```

```python
import jax
import jax.numpy as jnp
from jax import lax
from jax.sharding import PartitionSpec as P

LOW = jnp.bfloat16
WIDE = jnp.float32


def layer_norm(values, gain, shift):
    center = values - jnp.mean(values, axis=-1, keepdims=True)
    spread = jnp.mean(center * center, axis=-1, keepdims=True)
    return center * lax.rsqrt(spread + 1e-05) * gain + shift


def gelu_exact(values):
    return 0.5 * values * (1.0 + jax.scipy.special.erf(values * 0.7071067811865476))


def swap(values, axis, count, mask):
    return lax.ppermute(values, axis, [(i, i ^ mask) for i in range(count)])


def bits_of(count):
    return [1 << k for k in range(count.bit_length() - 1)]


def gather_bits(values, axis, count, dim, order):
    index = lax.axis_index(axis)
    done = []
    for mask in order:
        other = swap(values, axis, count, mask)
        place = dim + sum(1 for m in done if m > mask)
        first = ((index // mask) % 2) == 0
        values = jnp.stack(
            [jnp.where(first, values, other), jnp.where(first, other, values)], axis=place
        )
        done.append(mask)
    shape = values.shape
    rest = shape[dim + len(order):]
    return values.reshape(shape[:dim] + (count,) + rest)


def scatter_bits(values, axis, count, dim, order):
    index = lax.axis_index(axis)
    left = sorted(order, reverse=True)
    shape = values.shape
    values = values.reshape(shape[:dim] + (2,) * len(left) + shape[dim + 1:])
    for mask in order:
        at = dim + left.index(mask)
        bit = (index // mask) % 2
        keep = lax.dynamic_index_in_dim(values, bit, at, keepdims=False)
        send = lax.dynamic_index_in_dim(values, 1 - bit, at, keepdims=False)
        values = keep.astype(WIDE) + swap(send.astype(LOW), axis, count, mask).astype(WIDE)
        left.remove(mask)
    return values


def local(counts, tokens, cells, lengths, cotangent, w_qkv, w_out, w_up, w_down, biases, gains, cell_bias):
    pages, seqs = counts
    page_count, row_count, width = tokens.shape
    slots = row_count * seqs
    heads = cell_bias.shape[0]
    depth = width // heads
    heads_here = heads // seqs
    span = heads_here * depth
    flat = page_count * row_count
    rows = w_qkv.shape[0]
    ff_rows = w_down.shape[0]
    ff_here = ff_rows * pages
    seq_index = lax.axis_index("seq")
    high_page = bits_of(pages)[::-1]
    low_page = bits_of(pages)
    high_seq = bits_of(seqs)[::-1]
    low_seq = bits_of(seqs)

    def gather_seq(values, dim):
        return gather_bits(values, "seq", seqs, dim, high_seq)

    def scatter_seq(values, dim):
        return scatter_bits(values, "seq", seqs, dim, low_seq)

    def turn(values):
        return lax.all_to_all(values, "seq", 0, 0)

    part_qkv = w_qkv.astype(LOW).reshape(rows, 3, seqs, span).transpose(2, 0, 1, 3)
    part_qkv = turn(part_qkv.reshape(seqs, rows, 3 * span)).reshape(seqs * rows, 3 * span)
    w_proj = gather_bits(part_qkv, "page", pages, 0, high_page).reshape(width, 3 * span)
    small = jnp.concatenate([biases, gains], axis=0).astype(LOW)
    small_rows = small.shape[0]
    small_pad = -(-small.size // width)
    small_pad = -(-small_pad // 8) * 8
    small_flat = jnp.pad(small.reshape(-1), (0, small_pad * width - small.size)).reshape(small_pad, width)
    both = lax.all_gather(
        jnp.concatenate([w_out.astype(LOW), small_flat], axis=0), ("page", "seq"), axis=0, tiled=False
    )
    w_mix = both[:, :rows].reshape(width, width)
    lanes = small.shape[1]
    vectors = both[:, rows:].reshape(pages * seqs, small_pad * width)[:, : small.size]
    vectors = vectors.reshape(pages * seqs, small_rows, lanes).transpose(1, 0, 2)
    vectors = vectors.reshape(small_rows, width).astype(WIDE)
    scales = vectors[small_rows - 2:]
    part_up = w_up.astype(LOW).reshape(rows, pages, seqs, ff_rows).transpose(2, 0, 1, 3)
    part_up = turn(part_up.reshape(seqs, rows, ff_here)).reshape(seqs * rows, ff_here)
    w_expand = gather_bits(part_up, "page", pages, 0, high_page).reshape(width, ff_here)
    w_reduce = gather_bits(w_down.astype(LOW), "page", pages, 0, high_page).reshape(ff_here, width)
    hidden_bias = vectors[6:10].reshape(pages, seqs, ff_rows)
    hidden_bias = lax.dynamic_index_in_dim(hidden_bias, seq_index, 1, keepdims=False).reshape(ff_here)

    everything = gather_seq(tokens, 1).reshape(page_count * slots, width)
    cells_all = lax.all_gather(cells, "seq", axis=1, tiled=True)
    bias_q = lax.dynamic_slice_in_dim(vectors[0], seq_index * span, span)
    bias_v = lax.dynamic_slice_in_dim(vectors[1], seq_index * span, span)
    bias_qkv = jnp.concatenate([bias_q, jnp.zeros_like(bias_q), bias_v])
    projected = (jnp.dot(everything, w_proj, preferred_element_type=WIDE) + bias_qkv).astype(LOW)
    projected = projected.reshape(page_count, slots, 3, heads_here, depth)
    query, keys, values = projected[:, :, 0], projected[:, :, 1], projected[:, :, 2]
    own_bias = lax.dynamic_slice_in_dim(cell_bias, seq_index * heads_here, heads_here)
    same_cell = (cells_all[:, :, None] == cells_all[:, None, :]).astype(WIDE)
    key_valid = lax.broadcasted_iota(jnp.int32, (page_count, slots), 1) < lengths[:, None]

    def scores_of():
        raw = jnp.einsum("pqhe,pkhe->phqk", query, keys, preferred_element_type=WIDE) * 0.125
        scores = raw + own_bias[None, :, None, None] * same_cell[:, None]
        return jnp.where(key_valid[:, None, None, :], scores, -1e30)

    scores = scores_of()
    peak = jnp.max(scores, axis=-1, keepdims=True)
    exponent = jnp.exp(scores - peak)
    totals = jnp.sum(exponent, axis=-1, keepdims=True)
    log_total = peak + jnp.log(totals)
    weights_low = (exponent / totals).astype(LOW)
    context_here = jnp.einsum("phqk,pkhe->pqhe", weights_low, values, preferred_element_type=WIDE)
    context_here = context_here.astype(LOW).reshape(page_count, seqs, row_count, span)
    context = turn(context_here.transpose(1, 0, 2, 3)).transpose(1, 2, 0, 3).reshape(flat, width)

    inputs_wide = tokens.reshape(flat, width).astype(WIDE)
    attended = jnp.dot(context, w_mix, preferred_element_type=WIDE) + vectors[2]
    normed, norm_first = jax.vjp(layer_norm, inputs_wide + attended, scales[0], vectors[4])
    normed_all = gather_seq(normed.astype(LOW), 0).reshape(seqs * flat, width)
    expanded = jnp.dot(normed_all, w_expand, preferred_element_type=WIDE) + hidden_bias
    activated, gelu_back = jax.vjp(gelu_exact, expanded)
    activated_low = activated.astype(LOW)
    reduced = jnp.dot(activated_low, w_reduce, preferred_element_type=WIDE)
    reduced = scatter_seq(reduced.reshape(seqs, flat, width), 0) + vectors[3]
    output_wide, norm_second = jax.vjp(layer_norm, normed + reduced, scales[1], vectors[5])
    output = output_wide.astype(LOW).reshape(page_count, row_count, width)

    grad_second, grad_gain_two, grad_shift_two = norm_second(cotangent.reshape(flat, width).astype(WIDE))
    second_all = gather_seq(grad_second.astype(LOW), 0).reshape(seqs * flat, width)
    grad_activated = jnp.einsum("td,fd->tf", second_all, w_reduce, preferred_element_type=WIDE)
    grad_expanded = gelu_back(grad_activated)[0]
    expanded_low = grad_expanded.astype(LOW)
    grad_normed = jnp.einsum("tf,df->td", expanded_low, w_expand, preferred_element_type=WIDE)
    grad_normed = grad_second + scatter_seq(grad_normed.reshape(seqs, flat, width), 0)
    grad_reduce = jnp.einsum("tf,td->fd", activated_low, second_all, preferred_element_type=WIDE)
    grad_reduce = scatter_bits(grad_reduce.reshape(pages, ff_rows, width), "page", pages, 0, low_page)
    grad_expand = jnp.einsum("td,tf->df", normed_all, expanded_low, preferred_element_type=WIDE)
    grad_expand = scatter_bits(grad_expand.reshape(pages, seqs * rows, ff_here), "page", pages, 0, low_page)
    grad_expand = turn(grad_expand.astype(LOW).reshape(seqs, rows, ff_here))
    grad_expand = grad_expand.reshape(seqs, rows, pages, ff_rows).transpose(1, 2, 0, 3)
    grad_expand = grad_expand.reshape(rows, seqs * ff_here).astype(WIDE)
    grad_first, grad_gain_one, grad_shift_one = norm_first(grad_normed)
    first_low = grad_first.astype(LOW)
    grad_context = jnp.einsum("td,cd->tc", first_low, w_mix, preferred_element_type=WIDE).astype(LOW)
    grad_context = grad_context.reshape(page_count, row_count, seqs, span).transpose(2, 0, 1, 3)
    grad_context = turn(grad_context).transpose(1, 0, 2, 3).reshape(page_count, slots, heads_here, depth)
    grad_mix = jnp.einsum("tc,td->cd", context, first_low, preferred_element_type=WIDE)
    grad_mix = scatter_bits(grad_mix.reshape(pages, seqs, rows, width), "seq", seqs, 1, low_seq)
    grad_mix = scatter_bits(grad_mix, "page", pages, 0, low_page)

    weights_wide = jnp.exp(scores_of() - log_total)
    weights_low = weights_wide.astype(LOW)
    grad_weights = jnp.einsum("pqhe,pkhe->phqk", grad_context, values, preferred_element_type=WIDE)
    inner = jnp.sum(weights_wide * grad_weights, axis=-1, keepdims=True)
    grad_scores = weights_wide * (grad_weights - inner)
    grad_cell = jnp.sum(grad_scores * same_cell[:, None], axis=(0, 2, 3))
    scores_low = grad_scores.astype(LOW)
    grad_values = jnp.einsum("phqk,pqhe->pkhe", weights_low, grad_context, preferred_element_type=WIDE)
    grad_query = jnp.einsum("phqk,pkhe->pqhe", scores_low, keys, preferred_element_type=WIDE) * 0.125
    grad_keys = jnp.einsum("phqk,pqhe->pkhe", scores_low, query, preferred_element_type=WIDE) * 0.125
    grad_proj_low = jnp.stack([grad_query, grad_keys, grad_values], axis=2).astype(LOW)
    grad_proj_low = grad_proj_low.reshape(page_count * slots, 3 * span)
    grad_proj = jnp.einsum("td,tc->dc", everything, grad_proj_low, preferred_element_type=WIDE)
    grad_proj = scatter_bits(grad_proj.reshape(pages, seqs * rows, 3 * span), "page", pages, 0, low_page)
    grad_proj = turn(grad_proj.astype(LOW).reshape(seqs, rows, 3 * span))
    grad_proj = grad_proj.reshape(seqs, rows, 3, span).transpose(1, 2, 0, 3).reshape(rows, 3 * width)
    grad_proj = grad_proj.astype(WIDE)
    grad_inputs = jnp.einsum("tc,dc->td", grad_proj_low, w_proj, preferred_element_type=WIDE)
    grad_inputs = scatter_seq(grad_inputs.reshape(page_count, seqs, row_count, width), 1)
    grad_inputs = grad_first.reshape(page_count, row_count, width) + grad_inputs

    def place(vector, size):
        blank = jnp.zeros((width,), WIDE)
        return lax.dynamic_update_slice_in_dim(blank, vector, seq_index * size, 0)

    hidden = jnp.sum(grad_expanded, axis=0).reshape(pages, 1, ff_rows)
    hidden = lax.dynamic_update_slice_in_dim(
        jnp.zeros((pages, seqs, ff_rows), WIDE), hidden, seq_index, 1
    ).reshape(4, width)
    head_rows = jnp.stack(
        [
            place(jnp.sum(grad_query, axis=(0, 1)).reshape(span), span),
            place(jnp.sum(grad_values, axis=(0, 1)).reshape(span), span),
            jnp.sum(grad_first, axis=0),
            jnp.sum(grad_second, axis=0),
            grad_shift_one,
            grad_shift_two,
        ]
    )
    table = jnp.concatenate(
        [
            head_rows,
            hidden,
            grad_gain_one[None],
            grad_gain_two[None],
            place(grad_cell, heads_here)[None],
        ],
        axis=0,
    )
    for mask in low_seq:
        table = table + swap(table, "seq", seqs, mask)
    for mask in low_page:
        table = table + swap(table, "page", pages, mask)
    own = lax.axis_index("page") * seqs + seq_index
    mine = lax.dynamic_slice_in_dim(table, own * lanes, lanes, axis=1)
    return (
        output,
        grad_inputs,
        grad_proj,
        grad_mix,
        grad_expand,
        grad_reduce,
        mine[:10],
        mine[10:12],
        table[12, :heads],
    )


def solution(mesh):
    counts = (mesh.shape["page"], mesh.shape["seq"])
    placed = (
        P("page", "seq", None),
        P("page", "seq"),
        P("page"),
        P("page", "seq", None),
        P(("page", "seq"), None),
        P(("page", "seq"), None),
        P(("page", "seq"), None),
        P(("page", "seq"), None),
        P(None, ("page", "seq")),
        P(None, ("page", "seq")),
        P(),
    )

    def step(*args):
        return local(counts, *args)

    return jax.shard_map(
        step,
        mesh=mesh,
        in_specs=placed,
        out_specs=(
            P("page", "seq", None),
            P("page", "seq", None),
            P(("page", "seq"), None),
            P(("page", "seq"), None),
            P(("page", "seq"), None),
            P(("page", "seq"), None),
            P(None, ("page", "seq")),
            P(None, ("page", "seq")),
            P(),
        ),
        check_vma=False,
    )
```

```python
import functools

import jax
import jax.numpy as jnp
from jax import lax
from jax.experimental import pallas as pl
from jax.experimental.pallas import tpu as pltpu
from jax.sharding import PartitionSpec as P

LOW = jnp.bfloat16
WIDE = jnp.float32


def gelu_exact(values):
    return 0.5 * values * (1.0 + lax.erf(values * 0.7071067811865476))


NT = (((1,), (1,)), ((), ()))
TN = (((0,), (0,)), ((), ()))
NN = (((1,), (0,)), ((), ()))
ONCE = pl.Buffered(1)


def mul(left, right, dims=NN):
    return lax.dot_general(left, right, dims, preferred_element_type=WIDE)


def shaped(shape, dtype):
    return pltpu.HBM(shape, dtype)


def kept(shape, dtype):
    return pltpu.VMEM(shape, dtype)


def fixed(shape):
    zeros = (0,) * len(shape)
    return pl.BlockSpec(shape, lambda *_: zeros, pipeline_mode=ONCE)


def scalars():
    return pl.BlockSpec(memory_space=pltpu.SMEM)


def remote():
    return pl.BlockSpec(memory_space=pltpu.HBM)


def outside(values):
    return [pltpu.with_memory_space_constraint(value, pltpu.HBM) for value in values]


def inside(values):
    return [pltpu.with_memory_space_constraint(value, pltpu.VMEM) for value in values]


def near():
    return pl.BlockSpec(memory_space=pltpu.VMEM)


def bring(pairs, sems):
    copies = []
    for source, target in pairs:
        copy = pltpu.make_async_copy(source, target, sems.at[len(copies)])
        copy.start()
        copies.append(copy)
    return copies


def params(megabytes):
    return pltpu.CompilerParams(vmem_limit_bytes=megabytes * 1024 * 1024)


def cost(flops, moved, extra=0):
    return pl.CostEstimate(flops=int(flops), bytes_accessed=int(moved), transcendentals=int(extra))


def swap(values, axis, count, mask):
    return lax.ppermute(values, axis, [(i, i ^ mask) for i in range(count)])


def bits_of(count):
    return [1 << k for k in range(count.bit_length() - 1)]


def gather_near(values, seqs, between=None, wait=()):
    top = bits_of(seqs)[-1]
    far = swap(values, "seq", seqs, top)
    pieces = {0: after(values, *wait) if wait else values}
    for mask in bits_of(top)[::-1]:
        for rel in list(pieces):
            pieces[rel | mask] = swap(pieces[rel], "seq", seqs, mask)
    if between is not None:
        far = after(far, between([pieces[rel] for rel in range(top)]))
    pieces[top] = far
    for mask in bits_of(top)[::-1]:
        for rel in [rel for rel in pieces if rel & top]:
            pieces[rel | mask] = swap(pieces[rel], "seq", seqs, mask)
    return [pieces[rel] for rel in range(seqs)]


def gather_pages(values, pages, hold=None):
    stack, rels = values[None], [0]
    masks = bits_of(pages)[::-1]
    low, high = masks[-1], masks[:-1]
    split = high[-2:]
    for mask in high[:-2]:
        stack = jnp.concatenate([stack, swap(stack, "page", pages, mask)], axis=0)
        rels = rels + [rel | mask for rel in rels]
    found = [(stack, rels)]
    jumps = [0]
    for mask in split:
        jumps = jumps + [jump | mask for jump in jumps]
    for jump in jumps[1:]:
        found.append((swap(stack, "page", pages, jump), [rel ^ jump for rel in rels]))

    def finish(*others):
        first = swap(stack, "page", pages, low)
        more = [(first, [rel ^ low for rel in rels])]
        for array, rels_of in found[1:]:
            array = after(array, first, *others)
            more.append((swap(array, "page", pages, low), [rel ^ low for rel in rels_of]))
        return found + more

    return [array for array, _ in found[1:]], finish


def scatter_first(send, pages):
    return swap(send, "page", pages, 1)


def scatter_rest(keep, got, pages, direct):
    return scatter_last(keep + got.astype(WIDE), pages, 1, direct)


class Sum:
    def __init__(self, total, pages):
        self.pages = pages
        self.total = total
        if pages == 8:
            lows = [self.total[k].astype(LOW) for k in range(1, pages // 2)]
            self.ready = lows[0]
            self.parts = [swap(low, "page", pages, 2 * (k + 1)) for k, low in enumerate(lows)]
        else:
            self.ready = self.total
            self.parts = []

    def arrive(self, *others):
        if self.pages == 8:
            self.parts = [after(part, *others) for part in self.parts]
        else:
            self.parts = []

    def finish(self, *others):
        if self.pages != 8:
            return scatter_last(self.total, self.pages, 1, False)
        final = after(self.total[0], *others)
        for part in self.parts:
            final = final + part.astype(WIDE)
        return final


def scatter_last(total, pages, level, direct):
    left = pages >> level
    mask = 1 << level
    if direct and left == 4:
        lows = [total[k].astype(LOW) for k in range(1, left)]
        parts = [swap(low, "page", pages, 2 * (k + 1)) for k, low in enumerate(lows)]
        final = total[0]
        for part in parts:
            final = final + part.astype(WIDE)
        return final
    while left > 1:
        total = total.reshape((left // 2, 2) + total.shape[1:])
        got = swap(total[:, 1].astype(LOW), "page", pages, mask)
        total = total[:, 0] + got.astype(WIDE)
        left //= 2
        mask *= 2
    return total[0]


def scatter_bits(values, axis, count, dim, order):
    index = lax.axis_index(axis)
    for mask in order:
        shape = values.shape
        values = values.reshape(shape[:dim] + (shape[dim] // 2, 2) + shape[dim + 1 :])
        bit = (index // mask) % 2
        keep = lax.dynamic_index_in_dim(values, bit, dim + 1, keepdims=False)
        send = lax.dynamic_index_in_dim(values, 1 - bit, dim + 1, keepdims=False)
        values = keep.astype(WIDE) + swap(send.astype(LOW), axis, count, mask).astype(WIDE)
    return values


def scatter_start(values, axis, count, dim, mask):
    index = lax.axis_index(axis)
    shape = values.shape
    values = values.reshape(shape[:dim] + (shape[dim] // 2, 2) + shape[dim + 1 :])
    bit = (index // mask) % 2
    keep = lax.dynamic_index_in_dim(values, bit, dim + 1, keepdims=False)
    send = lax.dynamic_index_in_dim(values, 1 - bit, dim + 1, keepdims=False)
    return keep.astype(WIDE), swap(send.astype(LOW), axis, count, mask)


def reorder(pieces, index):
    count = len(pieces)
    out = []
    for k in range(count):
        value = pieces[0]
        for rel in range(1, count):
            value = jnp.where(index ^ k == rel, pieces[rel], value)
        out.append(value)
    return out


def turn(values, seqs, index):
    mine = [lax.dynamic_index_in_dim(values, index ^ rel, 0, keepdims=False) for rel in range(seqs)]
    return [mine[0]] + [swap(mine[rel], "seq", seqs, rel) for rel in range(1, seqs)]


def after(values, *others):
    return lax.optimization_barrier((values, others))[0]


def to_near(values):
    return lax.all_to_all(values, "seq", 0, 0)


def fence(*values):
    return lax.optimization_barrier(values)


def to_all(values):
    return lax.all_to_all(values, ("page", "seq"), 0, 0)


def head_scores(qkv, h, span, depth, bias, same, mask):
    group = (h * depth) // 128
    lanes = lax.broadcasted_iota(jnp.int32, (1, 128), 1)
    mine = (lanes // depth) == (h % (128 // depth))
    q = qkv[:, group * 128 : group * 128 + 128]
    k = qkv[:, span + group * 128 : span + group * 128 + 128]
    raw = mul(jnp.where(mine, q, jnp.zeros_like(q)), k, NT)
    return raw * 0.125 + jnp.where(same, bias, 0.0) + mask, mine, group


def attend(pieces, block, spot, own_bias, inputs, vectors, column, row, mask, heads, depth):
    page_count, rows, width = inputs[0].shape
    seqs = len(inputs)
    slots = seqs * rows
    span = heads * depth
    arrays = [array for array, _ in pieces]
    rels = [rel for _, rel in pieces]
    n_arrays = len(arrays)

    blocks = sum(len(rel) for rel in rels)

    def body(spot_ref, bias_ref, *refs):
        weights = refs[:n_arrays]
        xs = refs[n_arrays : n_arrays + seqs]
        vec_ref, col_ref, row_ref, mask_ref = refs[n_arrays + seqs : n_arrays + seqs + 4]
        qkv_ref, lse_ref, full_ref = refs[n_arrays + seqs + 4 : n_arrays + seqs + 7]
        ctx_ref, x_all, sems = refs[n_arrays + seqs + 7 :]
        seq = spot_ref[1]
        page = spot_ref[0]
        step = pl.program_id(0)

        @pl.when(step == 0)
        def _():
            pairs = [(xs[r], x_all.at[r]) for r in range(seqs)]
            for ref, rel_list in zip(weights, rels):
                for k, rel in enumerate(rel_list):
                    start = pl.multiple_of((page ^ rel) * block, block)
                    for t in range(3):
                        source = ref.at[k, pl.ds(t * block, block), :]
                        pairs.append((source, full_ref.at[pl.ds(start, block), pl.ds(t * span, span)]))
            for copy in bring(pairs, sems):
                copy.wait()

        at_q = pl.multiple_of(spot_ref[1] * span, span)
        row_bias = jnp.concatenate(
            [vec_ref[0:1, pl.ds(at_q, span)], jnp.zeros((1, span), WIDE), vec_ref[1:2, pl.ds(at_q, span)]],
            axis=1,
        )
        for r in range(seqs):
            part = mul(x_all[r, step], full_ref[...]) + row_bias
            qkv_ref[0, r * rows : (r + 1) * rows, :] = part.astype(LOW)
        qkv = qkv_ref[0]
        same = col_ref[0] == row_ref[0]
        key_mask = mask_ref[0]
        lane = lax.broadcasted_iota(jnp.int32, (1, 128), 1)
        lse = jnp.zeros((slots, 128), WIDE)
        context = [None] * (span // 128)
        for h in range(heads):
            scores, mine, group = head_scores(qkv, h, span, depth, bias_ref[h], same, key_mask)
            peak = jnp.max(scores, axis=-1, keepdims=True)
            exponent = jnp.exp(scores - peak)
            total = jnp.sum(exponent, axis=-1, keepdims=True)
            lse = jnp.where(lane == h, peak + jnp.log(total), lse)
            low = (exponent * (1.0 / total)).astype(LOW)
            v = qkv[:, 2 * span + group * 128 : 2 * span + group * 128 + 128]
            out = mul(low, v)
            context[group] = out if context[group] is None else jnp.where(mine, out, context[group])
        lse_ref[0] = lse
        for group, value in enumerate(context):
            value = value.astype(LOW)
            for r in range(seqs):
                ctx_ref[seq ^ r, 0, :, group * 128 : group * 128 + 128] = value[r * rows : (r + 1) * rows]

    def per_page(shape):
        zeros = (0,) * len(shape)
        return pl.BlockSpec((1,) + shape, lambda i: (i,) + zeros)

    flops = page_count * (2 * slots * width * 3 * span + 8 * heads * slots * slots * depth)
    return pl.pallas_call(
        body,
        grid=(page_count,),
        out_shape=[
            kept((page_count, slots, 3 * span), LOW),
            kept((page_count, slots, 128), WIDE),
            kept((width, 3 * span), LOW),
        ]
        + [shaped((seqs, page_count, rows, span), LOW)],
        in_specs=[scalars(), scalars()]
        + [remote()] * (n_arrays + seqs)
        + [fixed(vectors.shape), per_page((slots, 1)), per_page((1, slots)), per_page((1, slots))],
        out_specs=[per_page((slots, 3 * span)), per_page((slots, 128)), fixed((width, 3 * span))]
        + [pl.BlockSpec((seqs, 1, rows, span), lambda i: (0, i, 0, 0))],
        scratch_shapes=[
            pltpu.VMEM((seqs, page_count, rows, width), LOW),
            pltpu.SemaphoreType.DMA((seqs + 3 * blocks,)),
        ],
        compiler_params=params(24),
        cost_estimate=cost(flops, 10 << 20, page_count * heads * slots * slots),
        name="attend",
    )(spot, own_bias, *outside(arrays), *outside(inputs), vectors, column, row, mask)


def attend_back(spot, own_bias, qkv, lse, grads, inputs, column, row, mask, heads, depth, pages):
    page_count, slots, triple = qkv.shape
    span = triple // 3
    seqs = grads.shape[0]
    rows = slots // seqs
    groups = span // 128
    width = inputs[0].shape[2]
    block = width // pages
    tile = 256 if width % 256 == 0 else width

    def body(spot_ref, bias_ref, qkv_ref, lse_ref, *refs):
        grad_ref, x_refs = refs[0], refs[1 : seqs + 1]
        col_ref, row_ref, mask_ref, out_ref, sum_ref, cell_ref, keep, send = refs[seqs + 1 : seqs + 9]
        full, x_all, g_all, sems = refs[seqs + 9 :]
        step = pl.program_id(0)

        @pl.when(step == 0)
        def _():
            pairs = []
            for k in range(seqs):
                start = pl.multiple_of((spot_ref[1] ^ k) * rows, rows)
                pairs.append((grad_ref.at[k], g_all.at[:, pl.ds(start, rows), :]))
            pairs += [(x_refs[r], x_all.at[:, pl.ds(r * rows, rows), :]) for r in range(seqs)]
            for copy in bring(pairs, sems):
                copy.wait()

        page = spot_ref[0]
        qkv = qkv_ref[0]
        same = col_ref[0] == row_ref[0]
        key_mask = mask_ref[0]
        lane = lax.broadcasted_iota(jnp.int32, (1, 128), 1)
        sub = lax.broadcasted_iota(jnp.int32, (128, 1), 0)
        lse = lse_ref[0]
        grad = g_all[step]
        cell = jnp.zeros((1, 128), WIDE)
        dq, dk, dv = [None] * groups, [None] * groups, [None] * groups
        for h in range(heads):
            scores, mine, group = head_scores(qkv, h, span, depth, bias_ref[h], same, key_mask)
            mine_sub = (sub // depth) == (h % (128 // depth))
            at = group * 128
            q = qkv[:, at : at + 128]
            k = qkv[:, span + at : span + at + 128]
            v = qkv[:, 2 * span + at : 2 * span + at + 128]
            g = grad[:, at : at + 128]
            weights = jnp.exp(scores - lse[:, h : h + 1])
            slope = mul(jnp.where(mine, g, jnp.zeros_like(g)), v, NT)
            inner = jnp.sum(weights * slope, axis=-1, keepdims=True)
            ds = weights * (slope - inner)
            same_sum = jnp.sum(jnp.where(same, ds, 0.0), axis=0, keepdims=True)
            cell = jnp.where(lane == h, jnp.sum(same_sum, axis=1, keepdims=True), cell)
            ds_low = ds.astype(LOW)
            part_q = mul(ds_low, k)
            part_k = mul(q, ds_low, TN)
            part_v = mul(g, weights.astype(LOW), TN)
            dq[group] = part_q if dq[group] is None else jnp.where(mine, part_q, dq[group])
            dk[group] = part_k if dk[group] is None else jnp.where(mine_sub, part_k, dk[group])
            dv[group] = part_v if dv[group] is None else jnp.where(mine_sub, part_v, dv[group])
        cell_ref[0] = jnp.broadcast_to(cell, (8, 128))
        for group in range(groups):
            at = group * 128
            value_q = dq[group] * 0.125
            value_v = dv[group].T
            out_ref[0, :, at : at + 128] = value_q.astype(LOW)
            out_ref[0, :, span + at : span + at + 128] = (dk[group] * 0.125).T.astype(LOW)
            out_ref[0, :, 2 * span + at : 2 * span + at + 128] = value_v.astype(LOW)
            sum_ref[0, 0:1, at : at + 128] = jnp.sum(value_q, axis=0, keepdims=True)
            sum_ref[0, 0:1, span + at : span + at + 128] = jnp.sum(value_v, axis=0, keepdims=True)
        grad_proj = out_ref[0]

        @pl.when(step == 0)
        def _():
            for at in range(0, width, tile):
                full[at : at + tile, :] = mul(x_all[step, :, at : at + tile], grad_proj, TN)

        @pl.when(step > 0)
        def _():
            for at in range(0, width, tile):
                full[at : at + tile, :] += mul(x_all[step, :, at : at + tile], grad_proj, TN)

        @pl.when(step == page_count - 1)
        def _():
            for rel in range(pages):
                start = pl.multiple_of((page ^ rel) * block, block)
                value = full[pl.ds(start, block), :]
                if rel % 2 == 0:
                    keep[rel // 2] = value
                else:
                    send[rel // 2] = value.astype(LOW)

    def per_page(shape):
        zeros = (0,) * len(shape)
        return pl.BlockSpec((1,) + shape, lambda i: (i,) + zeros)

    flops = page_count * (20 * heads * slots * slots * depth + 2 * slots * width * triple)
    return pl.pallas_call(
        body,
        grid=(page_count,),
        out_shape=[
            shaped((page_count, slots, triple), LOW),
            shaped((page_count, 8, 2 * span), WIDE),
            shaped((page_count, 8, 128), WIDE),
            shaped((pages // 2, block, triple), WIDE),
            shaped((pages // 2, block, triple), LOW),
        ],
        in_specs=[scalars(), scalars(), per_page((slots, triple)), per_page((slots, 128))]
        + [remote()] * (1 + seqs)
        + [per_page((slots, 1)), per_page((1, slots)), per_page((1, slots))],
        out_specs=[
            per_page((slots, triple)),
            per_page((8, 2 * span)),
            per_page((8, 128)),
            fixed((pages // 2, block, triple)),
            fixed((pages // 2, block, triple)),
        ],
        scratch_shapes=[
            pltpu.VMEM((width, triple), WIDE),
            pltpu.VMEM((page_count, slots, width), LOW),
            pltpu.VMEM((page_count, slots, span), LOW),
            pltpu.SemaphoreType.DMA((2 * seqs,)),
        ],
        compiler_params=params(28),
        cost_estimate=cost(flops, 10 << 20, page_count * heads * slots * slots),
        name="attend_back",
    )(spot, own_bias, *inside([qkv, lse]), *outside([grads]), *outside(inputs), column, row, mask)


def page_order(values, rels, page_index):
    pages = len(rels)
    shape = values.shape
    if rels != sorted(rels):
        values = jnp.stack([values[rels.index(rel)] for rel in range(pages)])
    for bit in bits_of(pages):
        folded = values.reshape((pages // (2 * bit), 2, bit) + shape[1:])
        values = jnp.where((page_index // bit) % 2 == 0, folded, folded[:, ::-1])
    return values.reshape(shape)


def assemble_mix(near_blocks, rels, spot, rows, width):
    seqs = len(near_blocks)
    span = near_blocks[0].shape[2]
    if rows % 16:
        ordered = reorder([array.reshape(len(rels), -1, rows, span) for array in near_blocks], spot[1])
        ordered = jnp.stack([array.transpose(0, 2, 1, 3).reshape(len(rels), rows, width) for array in ordered], axis=1)
        return page_order(ordered, rels, spot[0]).reshape(width, width)

    def body(spot_ref, *refs):
        out, held, sems = refs[-3:]
        page, seq = spot_ref[0], spot_ref[1]
        for copy in bring([(refs[r], held.at[r]) for r in range(seqs)], sems):
            copy.wait()
        for r in range(seqs):
            for k, rel in enumerate(rels):
                start = pl.multiple_of(((page ^ rel) * seqs + (seq ^ r)) * rows, rows)
                for t in range(width // span):
                    out[pl.ds(start, rows), t * span : (t + 1) * span] = held[r, k, t * rows : (t + 1) * rows, :]

    return pl.pallas_call(
        body,
        out_shape=kept((width, width), LOW),
        in_specs=[scalars()] + [remote()] * seqs,
        out_specs=near(),
        scratch_shapes=[pltpu.VMEM((seqs,) + near_blocks[0].shape, LOW), pltpu.SemaphoreType.DMA((seqs,))],
        compiler_params=params(8),
        cost_estimate=cost(0, 4 * width * width),
        name="assemble_mix",
    )(spot, *outside(near_blocks))


def mix(spot, contexts, w_mix, inputs, vectors):
    flat, width = inputs.shape
    seqs = contexts.shape[0]
    span = width // seqs

    def body(spot_ref, *refs):
        c_ref, w_ref, x_ref, vec_ref, wide_ref, low_ref, hat_ref, rstd_ref, c_all, x_here, sems = refs
        copies = bring([(c_ref.at[k], c_all.at[k]) for k in range(seqs)] + [(x_ref, x_here)], sems)
        for copy in copies:
            copy.wait()
        total = x_here[...].astype(WIDE) + vec_ref[2:3, :]
        for k in range(seqs):
            total = total + mul(c_all[k], w_ref[k * span : (k + 1) * span, :])
        center = total - jnp.mean(total, axis=-1, keepdims=True)
        spread = jnp.mean(center * center, axis=-1, keepdims=True)
        rstd = lax.rsqrt(spread + 1e-05)
        hat = center * rstd
        normed = hat * vec_ref[10:11, :] + vec_ref[4:5, :]
        wide_ref[...] = normed
        low_ref[...] = normed.astype(LOW)
        hat_ref[...] = hat
        rstd_ref[...] = jnp.broadcast_to(rstd, (flat, 128))

    return pl.pallas_call(
        body,
        out_shape=[
            kept((flat, width), WIDE),
            shaped((flat, width), LOW),
            kept((flat, width), WIDE),
            kept((flat, 128), WIDE),
        ],
        in_specs=[scalars()] + [remote(), near(), remote(), near()],
        out_specs=[near()] * 4,
        scratch_shapes=[
            pltpu.VMEM((seqs, flat, span), LOW),
            pltpu.VMEM((flat, width), LOW),
            pltpu.SemaphoreType.DMA((seqs + 1,)),
        ],
        compiler_params=params(12),
        cost_estimate=cost(2 * flat * width * width, 8 << 20),
        name="mix",
    )(spot, *outside([contexts]), *inside([w_mix]), *outside([inputs]), vectors)


def second_norm(normed, keep, close, far, vectors, cotangent):
    flat, width = normed.shape

    def body(h_ref, k_ref, n_ref, f_ref, vec_ref, cot_ref, out, wide, low, sums, n_here, f_here, c_here, sems):
        for copy in bring([(n_ref, n_here), (f_ref, f_here), (cot_ref, c_here)], sems):
            copy.wait()
        total = h_ref[...] + (k_ref[...] + n_here[...].astype(WIDE) + f_here[...].astype(WIDE)) + vec_ref[3:4, :]
        center = total - jnp.mean(total, axis=-1, keepdims=True)
        spread = jnp.mean(center * center, axis=-1, keepdims=True)
        rstd = lax.rsqrt(spread + 1e-05)
        hat = center * rstd
        out[...] = (hat * vec_ref[11:12, :] + vec_ref[5:6, :]).astype(LOW)
        cot = c_here[...].astype(WIDE)
        slope = cot * vec_ref[11:12, :]
        first = jnp.mean(slope, axis=-1, keepdims=True)
        second = jnp.mean(slope * hat, axis=-1, keepdims=True)
        grad = rstd * (slope - first - hat * second)
        wide[...] = grad
        low[...] = grad.astype(LOW)
        sums[0:1, :] = jnp.sum(cot * hat, axis=0, keepdims=True)
        sums[1:2, :] = jnp.sum(cot, axis=0, keepdims=True)
        sums[2:3, :] = jnp.sum(grad, axis=0, keepdims=True)

    return pl.pallas_call(
        body,
        out_shape=[
            shaped((flat, width), LOW),
            kept((flat, width), WIDE),
            shaped((flat, width), LOW),
            shaped((8, width), WIDE),
        ],
        in_specs=[near(), near(), remote(), remote(), near(), remote()],
        out_specs=[near()] * 4,
        scratch_shapes=[pltpu.VMEM((flat, width), LOW)] * 3 + [pltpu.SemaphoreType.DMA((3,))],
        compiler_params=params(12),
        cost_estimate=cost(flat * width * 30, 7 << 20),
        name="second_norm",
    )(*inside([normed]), keep, *outside([close, far]), vectors, *outside([cotangent]))


def first_norm_back(spot, grad_second, keep, close, far, hat, rstd, vectors, w_mix, seqs):
    flat, width = grad_second.shape
    span = width // seqs

    def body(spot_ref, d_ref, k_ref, n_ref, f_ref, hat_ref, rstd_ref, vec_ref, w_ref, wide, low, sums, *rest):
        outs, n_here, f_here, sems = rest
        for copy in bring([(n_ref, n_here), (f_ref, f_here)], sems):
            copy.wait()
        grad = d_ref[...] + (k_ref[...] + n_here[...].astype(WIDE) + f_here[...].astype(WIDE))
        hat = hat_ref[...]
        slope = grad * vec_ref[10:11, :]
        first = jnp.mean(slope, axis=-1, keepdims=True)
        second = jnp.mean(slope * hat, axis=-1, keepdims=True)
        result = rstd_ref[:, 0:1] * (slope - first - hat * second)
        wide[...] = result
        result_low = result.astype(LOW)
        low[...] = result_low
        for k in range(seqs):
            outs[k] = mul(result_low, w_ref[k * span : (k + 1) * span, :], NT).astype(LOW)
        sums[0:1, :] = jnp.sum(grad * hat, axis=0, keepdims=True)
        sums[1:2, :] = jnp.sum(grad, axis=0, keepdims=True)
        sums[2:3, :] = jnp.sum(result, axis=0, keepdims=True)

    return pl.pallas_call(
        body,
        out_shape=[shaped((flat, width), WIDE), shaped((flat, width), LOW), shaped((8, width), WIDE)]
        + [shaped((seqs, flat, span), LOW)],
        in_specs=[scalars(), near(), near(), remote(), remote()] + [near()] * 4,
        out_specs=[near()] * 4,
        scratch_shapes=[pltpu.VMEM((flat, width), LOW)] * 2 + [pltpu.SemaphoreType.DMA((2,))],
        compiler_params=params(12),
        cost_estimate=cost(2 * flat * width * width, 8 << 20),
        name="first_norm_back",
    )(spot, *inside([grad_second]), keep, *outside([close, far]), *inside([hat, rstd]), vectors, *inside([w_mix]))


def weight_grad(spot, lefts, rights, pages, split):
    count = len(lefts)
    tokens, height = lefts[0].shape
    width = rights[0].shape[1]
    rows = height // pages
    tile = 256 if height % 256 == 0 else height

    def body(spot_ref, *refs):
        left, right = refs[:count], refs[count : 2 * count]
        outs = refs[2 * count : -4]
        full, l_all, r_all, sems = refs[-4:]
        page = spot_ref[0]
        pairs = []
        for k in range(count):
            pairs.append((left[k], l_all.at[pl.ds(k * tokens, tokens), :]))
            pairs.append((right[k], r_all.at[pl.ds(k * tokens, tokens), :]))
        for copy in bring(pairs, sems):
            copy.wait()
        for at in range(0, height, tile):
            value = mul(l_all[:, at : at + tile], r_all[...], TN)
            if split:
                full[at : at + tile, :] = value
            else:
                outs[0][at : at + tile, :] = value.astype(LOW)
        if split:
            for rel in range(pages):
                start = pl.multiple_of((page ^ rel) * rows, rows)
                value = full[pl.ds(start, rows), :]
                if rel % 2 == 0:
                    outs[0][rel // 2] = value
                else:
                    outs[1][rel // 2] = value.astype(LOW)

    if split:
        outs = [shaped((pages // 2, rows, width), WIDE), shaped((pages // 2, rows, width), LOW)]
    else:
        outs = [shaped((height, width), LOW)]
    return pl.pallas_call(
        body,
        out_shape=outs,
        in_specs=[scalars()] + [remote()] * (2 * count),
        out_specs=[near()] * len(outs),
        scratch_shapes=[
            pltpu.VMEM((height, width) if split else (8, 128), WIDE),
            pltpu.VMEM((count * tokens, height), LOW),
            pltpu.VMEM((count * tokens, width), LOW),
            pltpu.SemaphoreType.DMA((2 * count,)),
        ],
        compiler_params=params(18),
        cost_estimate=cost(2 * count * tokens * height * width, 8 << 20),
        name="weight_grad",
    )(spot, *outside(lefts), *outside(rights))


def input_grad(grad_proj, w_proj, seqs):
    page_count, slots, triple = grad_proj.shape
    width = w_proj.shape[0]
    rows = slots // seqs

    def body(d_ref, w_ref, *outs):
        for rel in range(seqs):
            value = mul(d_ref[0, rel * rows : (rel + 1) * rows, :], w_ref[...], NT)
            outs[rel][0] = value.astype(outs[rel].dtype)

    per = pl.BlockSpec((1, rows, width), lambda i: (i, 0, 0))
    return pl.pallas_call(
        body,
        grid=(page_count,),
        out_shape=[shaped((page_count, rows, width), WIDE if rel % 2 == 0 else LOW) for rel in range(seqs)],
        in_specs=[pl.BlockSpec((1, slots, triple), lambda i: (i, 0, 0)), fixed(w_proj.shape)],
        out_specs=[per] * seqs,
        compiler_params=params(14),
        cost_estimate=cost(2 * page_count * slots * triple * width, 8 << 20),
        name="input_grad",
    )(grad_proj, *inside([w_proj]))


def local(counts, tokens, cells, lengths, cotangent, w_qkv, w_out, w_up, w_down, biases, gains, cell_bias):
    pages, seqs = counts
    page_count, row_count, width = tokens.shape
    slots = row_count * seqs
    heads = cell_bias.shape[0]
    depth = width // heads
    heads_here = heads // seqs
    span = heads_here * depth
    flat = page_count * row_count
    rows = w_qkv.shape[0]
    ff_rows = w_down.shape[0]
    ff_here = ff_rows * pages
    page_index = lax.axis_index("page")
    seq_index = lax.axis_index("seq")
    spot = jnp.stack([page_index, seq_index]).astype(jnp.int32)
    low_page = bits_of(pages)
    low_seq = bits_of(seqs)

    def scatter_near(keeps, sends):
        near_parts = [swap(send, "seq", seqs, 1) for send in sends]
        *result, sent = scatter_far_sent(keeps, near_parts)
        return (*result, sent)

    def scatter_far(keeps, nears):
        return scatter_far_sent(keeps, nears)[:3]

    def scatter_far_sent(totals, nears):
        far = jnp.zeros_like(nears[0])
        mask = 2
        while mask < seqs:
            half = [k for k in range(len(totals)) if (k * 2) & mask]
            ready = [(totals[k] + nears[k].astype(WIDE)).astype(LOW) for k in half]
            moved = [swap(value, "seq", seqs, mask) for value in ready]
            rest = [k for k in range(len(totals)) if not (k * 2) & mask]
            if mask * 2 >= seqs:
                far = moved[0]
                totals, nears = [totals[0]], [nears[0]]
            else:
                totals = [totals[k] + nears[k].astype(WIDE) for k in rest]
                nears = moved
            mask *= 2
        return totals[0], nears[0], far, ready[0]

    def small_table(sums_proj, cells_grad):
        owners = pages * seqs
        here = lax.broadcasted_iota(jnp.int32, (seqs, 1, 1), 0) == seq_index
        sums_proj = jnp.sum(sums_proj[:, 0], axis=0).reshape(2, 1, pages, lanes)

        def own(vector):
            return jnp.where(here, vector, 0.0).reshape(owners, 1, lanes)

        hidden_sum = functools.reduce(jnp.add, totals).reshape(pages, 1, ff_rows)
        hidden_sum = jnp.where(here.reshape(1, seqs, 1), hidden_sum, 0.0)
        hidden_sum = hidden_sum.reshape(-1, owners, lanes).transpose(1, 0, 2)
        cells_grad = jnp.sum(cells_grad[:, 0, :heads_here], axis=0)[None]
        cells_grad = jnp.where(here[:, 0], cells_grad, 0.0).reshape(heads)
        cells_grad = jnp.pad(cells_grad, (0, -heads % lanes)).reshape(1, -1, lanes)

        def row_of(sums, k):
            return sums[k].reshape(owners, 1, lanes)

        return to_all(
            jnp.concatenate(
                [
                    own(sums_proj[0]),
                    own(sums_proj[1]),
                    row_of(sums_one, 2),
                    row_of(sums_two, 2),
                    row_of(sums_one, 1),
                    row_of(sums_two, 1),
                    hidden_sum,
                    row_of(sums_one, 0),
                    row_of(sums_two, 0),
                    jnp.broadcast_to(cells_grad, (owners,) + cells_grad.shape[1:]),
                ],
                axis=1,
            )
        )

    def block_rows(values):
        return values.reshape(values.shape[0], -1, span)

    small = jnp.concatenate([biases, gains], axis=0).astype(LOW)
    small_rows, lanes = small.shape
    digits = jnp.concatenate([cells // 16, cells % 16], axis=0).astype(LOW)
    extra = jnp.concatenate(
        [jnp.pad(small, ((0, 0), (0, span - lanes))), jnp.pad(digits, ((0, 0), (0, span - row_count)))], axis=0
    )
    part_qkv = w_qkv.astype(LOW).reshape(rows, 3, seqs, span).transpose(2, 1, 0, 3)
    part_up = w_up.astype(LOW).reshape(rows, pages, seqs, ff_rows).transpose(2, 0, 1, 3)
    sent = jnp.concatenate(
        [
            part_qkv.reshape(seqs, 3 * rows, span),
            jnp.broadcast_to(extra, (seqs,) + extra.shape),
            part_up.reshape(seqs, pages * rows * ff_rows // span, span),
        ],
        axis=1,
    )
    turned = to_near(sent)
    part_qkv = turned[:, : 3 * rows].reshape(seqs, 3, rows, span).transpose(1, 0, 2, 3)
    extras = turned[:, 3 * rows : 3 * rows + extra.shape[0]]
    part_up = turned[:, 3 * rows + extra.shape[0] :].reshape(seqs * rows, ff_here)
    digits = extras[:, small_rows : small_rows + 2 * page_count, :row_count].astype(jnp.int32)
    cells_all = digits[:, :page_count] * 16 + digits[:, page_count:]
    cells_all = jnp.stack(reorder([cells_all[k] for k in range(seqs)], seq_index), axis=1)
    cells_all = cells_all.reshape(page_count, slots)

    part_mix = w_out.astype(LOW).reshape(rows, width // span, span).transpose(1, 0, 2)
    part_small = extras[:, :small_rows, :lanes].transpose(1, 0, 2).reshape(small_rows, seqs * lanes)
    part_small = jnp.pad(part_small, ((0, -small_rows % 16), (0, span - seqs * lanes)))
    block = seqs * rows
    part_both = jnp.concatenate(
        [part_qkv.reshape(3 * block, span), part_mix.reshape(-1, span), part_small], axis=0
    )
    split = low_page[1:3][::-1]
    stack, rels = part_both[None], [0]
    for bit in low_page[:0:-1][: len(low_page) - 1 - len(split)]:
        stack = jnp.concatenate([stack, swap(stack, "page", pages, bit)], axis=0)
        rels = rels + [rel | bit for rel in rels]
    jumps = [0]
    for bit in split:
        jumps = jumps + [jump | bit for jump in jumps]
    across = [swap(stack, "page", pages, jump) for jump in jumps[1:]]
    beside = [swap(stack, "page", pages, 1)]
    x_near = [tokens]
    x_far = swap(after(tokens, part_both), "seq", seqs, low_seq[-1])
    *across, part_up, first_beside, x_far, w_down_low, x_own = fence(
        *across, part_up, beside[0], x_far, w_down.astype(LOW), tokens
    )
    beside = [first_beside] + [swap(array, "page", pages, 1) for array in across]
    both_pieces = [(array, [rel ^ jump for rel in rels]) for array, jump in zip([stack] + across, jumps)]
    both_pieces += [(array, [rel ^ jump ^ 1 for rel in rels]) for array, jump in zip(beside, jumps)]
    inputs = {0: x_own, low_seq[-1]: x_far}
    for bit in low_seq[:-1][::-1]:
        for rel in list(inputs):
            inputs[rel | bit] = swap(inputs[rel], "seq", seqs, bit)
    inputs = [inputs[rel] for rel in range(seqs)]
    feed_both = lax.all_gather(jnp.concatenate([part_up, w_down_low], axis=0), "page", axis=0, tiled=False)
    w_expand = feed_both[:, :block].reshape(width, ff_here)
    w_reduce = feed_both[:, block:].reshape(ff_here, width)
    fenced = fence(*[array for array, _ in both_pieces], *inputs)
    inputs = list(fenced[len(both_pieces) :])
    both_pieces = [(array, rel) for array, (_, rel) in zip(fenced[: len(both_pieces)], both_pieces)]
    both_rels = [rel for _, rel_list in both_pieces for rel in rel_list]
    vectors = jnp.concatenate([array[:, 4 * block :, :] for array, _ in both_pieces], axis=0)
    vectors = page_order(vectors[:, :small_rows, : seqs * lanes], both_rels, page_index)
    vectors = vectors.reshape(pages, small_rows, seqs * lanes).transpose(1, 0, 2)
    vectors = vectors.reshape(small_rows, width).astype(WIDE)
    hidden_bias = vectors[6:10].reshape(pages, seqs, ff_rows)
    hidden_bias = lax.dynamic_index_in_dim(hidden_bias, seq_index, 1, keepdims=False).reshape(1, ff_here)

    position = lax.broadcasted_iota(jnp.int32, (1, slots), 1)
    position = ((position // row_count) ^ seq_index) * row_count + position % row_count
    mask = jnp.where(position < lengths[:, None], 0.0, -1e30).astype(WIDE)[:, None, :]
    column, row = cells_all[:, :, None], cells_all[:, None, :]
    own_bias = lax.dynamic_slice_in_dim(cell_bias, seq_index * heads_here, heads_here)
    mix_part = jnp.concatenate([array[:, 3 * block : 4 * block, :] for array, _ in both_pieces], axis=0)
    mix_far = swap(mix_part, "seq", seqs, low_seq[-1])
    qkv, lse, w_proj, contexts = attend(
        [(after(array, mix_part), rel_list) for array, rel_list in both_pieces],
        block,
        spot,
        own_bias,
        inputs,
        vectors,
        column,
        row,
        mask,
        heads_here,
        depth,
    )
    contexts, mix_part, mix_far, qkv, lse, w_proj = fence(contexts, mix_part, mix_far, qkv, lse, w_proj)
    mix_near = {0: mix_part, low_seq[-1]: mix_far}
    for bit in low_seq[:-1][::-1]:
        for rel in list(mix_near):
            mix_near[rel | bit] = swap(mix_near[rel], "seq", seqs, bit)
    contexts = to_near(contexts).reshape(seqs, flat, span)
    w_mix = assemble_mix([mix_near[rel] for rel in range(seqs)], both_rels, spot, rows, width)

    flat_inputs = tokens.reshape(flat, width)
    normed, normed_low, hat, rstd = mix(spot, contexts, w_mix, flat_inputs, vectors)
    hidden, active, parts = [], [], []

    def feed(pieces):
        for piece in pieces:
            value = jnp.dot(piece, w_expand, preferred_element_type=WIDE) + hidden_bias
            low = gelu_exact(value).astype(LOW)
            part = jnp.dot(low, w_reduce, preferred_element_type=WIDE)
            part = part.astype(LOW) if len(parts) % 2 else part
            hidden.append(value)
            active.append(low)
            parts.append(part)
        return tuple(parts)

    normed_all = gather_near(normed_low, seqs, feed)
    feed(normed_all[seqs // 2 :])
    keep, close, far, ready = scatter_near(parts[0::2], parts[1::2])
    slopes = [
        0.5 * (1.0 + lax.erf(u * 0.7071067811865476)) + u * jnp.exp(-0.5 * u * u) * 0.3989422804014327
        for u in after(hidden, ready)
    ]
    far, slopes = lax.optimization_barrier((far, slopes))
    output, grad_second, second_low, sums_two = second_norm(
        normed, keep, close, far, vectors, cotangent.reshape(flat, width)
    )

    expanded, parts, totals = [], [], []

    def feed_back(pieces):
        for piece in pieces:
            slope = slopes[len(parts)]
            value = jnp.einsum("td,fd->tf", piece, w_reduce, preferred_element_type=WIDE) * slope
            low = value.astype(LOW)
            part = jnp.einsum("tf,df->td", low, w_expand, preferred_element_type=WIDE)
            part = part.astype(LOW) if len(parts) % 2 else part
            expanded.append(low)
            totals.append(jnp.sum(value, axis=0))
            parts.append(part)
        return tuple(parts)

    second_all = gather_near(second_low, seqs, feed_back)
    feed_back(second_all[seqs // 2 :])
    keep, close, far, ready = scatter_near(parts[0::2], parts[1::2])
    down_keep, down_send = weight_grad(spot, after(active, ready), second_all, pages, True)
    up_keep, up_send = weight_grad(spot, after(normed_all, down_send), expanded, pages, True)
    far, down_send, up_send = lax.optimization_barrier((far, down_send, up_send))
    down_got = scatter_first(down_send, pages)
    grad_first, first_low, sums_one, grad_contexts = first_norm_back(
        spot, grad_second, keep, close, far, hat, rstd, vectors, w_mix, seqs
    )
    grad_contexts = to_near(grad_contexts)
    context = jnp.concatenate([contexts[k] for k in range(seqs)], axis=1)
    grad_mix = jnp.einsum("tc,td->cd", context, first_low, preferred_element_type=WIDE)
    grad_mix = scatter_bits(grad_mix.reshape(pages, seqs, rows, width), "seq", seqs, 1, low_seq[:1])
    grad_contexts, grad_mix, down_got, down_keep, up_send = fence(
        grad_contexts, grad_mix, down_got, down_keep, up_send
    )
    down_sum = Sum(down_keep + down_got.astype(WIDE), pages)
    up_got = scatter_first(up_send, pages)
    mix_keep, mix_parts = scatter_start(grad_mix, "seq", seqs, 1, low_seq[1])
    grad_contexts = after(grad_contexts, down_sum.ready)
    grad_contexts = grad_contexts.reshape(seqs, page_count, row_count, span)
    grad_proj, sums_proj, cells_grad, proj_keep, proj_send = attend_back(
        spot, own_bias, qkv, lse, grad_contexts, inputs, column, row, mask, heads_here, depth, pages
    )
    down_parts = down_sum.parts
    fenced = fence(
        grad_proj, sums_proj, cells_grad, proj_keep, proj_send, up_keep, up_got, mix_keep, mix_parts, *down_parts
    )
    grad_proj, sums_proj, cells_grad, proj_keep, proj_send, up_keep, up_got, mix_keep, mix_parts = fenced[:9]
    down_sum.parts = list(fenced[9:])
    proj_got = scatter_first(proj_send, pages)
    up_sum = Sum(up_keep + up_got.astype(WIDE), pages)
    grad_mix = mix_keep + mix_parts.astype(WIDE)
    mix_keep, mix_parts = scatter_start(grad_mix.reshape(pages, rows, width), "page", pages, 0, 1)
    fenced = fence(proj_got, proj_keep, mix_keep, mix_parts, grad_proj, sums_proj, cells_grad, *up_sum.parts)
    proj_got, proj_keep, mix_keep, mix_parts, grad_proj, sums_proj, cells_grad = fenced[:7]
    up_sum.parts = list(fenced[7:])
    proj_sum = Sum(proj_keep + proj_got.astype(WIDE), pages)
    small_sums = small_table(after(sums_proj, proj_sum.ready), after(cells_grad, proj_sum.ready))
    grad_mix = after(mix_keep, proj_sum.ready) + mix_parts.astype(WIDE)
    mix_keep, mix_parts = scatter_start(grad_mix, "page", pages, 0, 2)
    parts = input_grad(after(grad_proj, proj_sum.ready), w_proj, seqs)
    near_parts = [swap(part, "seq", seqs, 1) for part in parts[1::2]]
    grad_expand = up_sum.finish(proj_sum.ready)
    fenced = fence(small_sums, mix_keep, mix_parts, grad_expand, *proj_sum.parts, *near_parts)
    small_sums, mix_keep, mix_parts, grad_expand = fenced[:4]
    proj_sum.parts = list(fenced[4 : 4 + len(proj_sum.parts)])
    near_parts = list(fenced[4 + len(proj_sum.parts) :])
    grad_qkv = proj_sum.finish()
    grad_reduce = down_sum.finish(grad_qkv)
    grad_mix = mix_keep + mix_parts.astype(WIDE)
    grad_mix = scatter_bits(grad_mix, "page", pages, 0, low_page[2:]).reshape(rows, width)
    keep, close, far = scatter_far(parts[0::2], near_parts)
    sent = jnp.concatenate(
        [
            grad_qkv.reshape(seqs, rows, 3, span).transpose(0, 2, 1, 3).reshape(seqs, 3 * rows, span),
            grad_expand.reshape(seqs, -1, span),
        ],
        axis=1,
    ).astype(LOW)
    turned = to_near(sent)
    grad_qkv = turned[:, : 3 * rows].reshape(seqs, 3, rows, span).transpose(2, 1, 0, 3)
    grad_qkv = grad_qkv.reshape(rows, 3 * width).astype(WIDE)
    grad_expand = turned[:, 3 * rows :].reshape(seqs, rows, pages, ff_rows).transpose(1, 2, 0, 3)
    grad_expand = grad_expand.reshape(rows, seqs * ff_here).astype(WIDE)
    grad_inputs = grad_first.reshape(page_count, row_count, width) + (
        keep + close.astype(WIDE) + far.astype(WIDE)
    )

    summed = jnp.sum(small_sums, axis=0)
    return (
        output.reshape(page_count, row_count, width),
        grad_inputs,
        grad_qkv,
        grad_mix,
        grad_expand,
        grad_reduce,
        summed[:10],
        summed[10:12],
        summed[12:].reshape(-1)[:heads],
    )


def solution(mesh):
    counts = (mesh.shape["page"], mesh.shape["seq"])
    placed = (
        P("page", "seq", None),
        P("page", "seq"),
        P("page"),
        P("page", "seq", None),
        P(("page", "seq"), None),
        P(("page", "seq"), None),
        P(("page", "seq"), None),
        P(("page", "seq"), None),
        P(None, ("page", "seq")),
        P(None, ("page", "seq")),
        P(),
    )

    def step(*args):
        return local(counts, *args)

    return jax.shard_map(
        step,
        mesh=mesh,
        in_specs=placed,
        out_specs=(
            P("page", "seq", None),
            P("page", "seq", None),
            P(("page", "seq"), None),
            P(("page", "seq"), None),
            P(("page", "seq"), None),
            P(("page", "seq"), None),
            P(None, ("page", "seq")),
            P(None, ("page", "seq")),
            P(),
        ),
        check_vma=False,
    )
```

```python
import functools

import jax
import jax.numpy as jnp
from jax import lax
from jax.experimental import pallas as pl
from jax.experimental.pallas import tpu as pltpu
from jax.sharding import PartitionSpec as P

LOW = jnp.bfloat16
WIDE = jnp.float32


def gelu_exact(values):
    return 0.5 * values * (1.0 + lax.erf(values * 0.7071067811865476))


NT = (((1,), (1,)), ((), ()))
TN = (((0,), (0,)), ((), ()))
NN = (((1,), (0,)), ((), ()))
ONCE = pl.Buffered(1)


def mul(left, right, dims=NN):
    return lax.dot_general(left, right, dims, preferred_element_type=WIDE)


def shaped(shape, dtype):
    return pltpu.HBM(shape, dtype)


def kept(shape, dtype):
    return pltpu.VMEM(shape, dtype)


def fixed(shape):
    zeros = (0,) * len(shape)
    return pl.BlockSpec(shape, lambda *_: zeros, pipeline_mode=ONCE)


def scalars():
    return pl.BlockSpec(memory_space=pltpu.SMEM)


def remote():
    return pl.BlockSpec(memory_space=pltpu.HBM)


def outside(values):
    return [pltpu.with_memory_space_constraint(value, pltpu.HBM) for value in values]


def inside(values):
    return [pltpu.with_memory_space_constraint(value, pltpu.VMEM) for value in values]


def near():
    return pl.BlockSpec(memory_space=pltpu.VMEM)


def bring(pairs, sems):
    copies = []
    for source, target in pairs:
        copy = pltpu.make_async_copy(source, target, sems.at[len(copies)])
        copy.start()
        copies.append(copy)
    return copies


def params(megabytes):
    return pltpu.CompilerParams(vmem_limit_bytes=megabytes * 1024 * 1024)


def cost(flops, moved, extra=0):
    return pl.CostEstimate(flops=int(flops), bytes_accessed=int(moved), transcendentals=int(extra))


def swap(values, axis, count, mask):
    return lax.ppermute(values, axis, [(i, i ^ mask) for i in range(count)])


def bits_of(count):
    return [1 << k for k in range(count.bit_length() - 1)]


def gather_near(values, seqs, between=None, wait=()):
    top = bits_of(seqs)[-1]
    far = swap(values, "seq", seqs, top)
    pieces = {0: after(values, *wait) if wait else values}
    for mask in bits_of(top)[::-1]:
        for rel in list(pieces):
            pieces[rel | mask] = swap(pieces[rel], "seq", seqs, mask)
    if between is not None:
        far = after(far, between([pieces[rel] for rel in range(top)]))
    pieces[top] = far
    for mask in bits_of(top)[::-1]:
        for rel in [rel for rel in pieces if rel & top]:
            pieces[rel | mask] = swap(pieces[rel], "seq", seqs, mask)
    return [pieces[rel] for rel in range(seqs)]


def gather_pages(values, pages, hold=None):
    stack, rels = values[None], [0]
    masks = bits_of(pages)[::-1]
    low, high = masks[-1], masks[:-1]
    split = high[-2:]
    for mask in high[:-2]:
        stack = jnp.concatenate([stack, swap(stack, "page", pages, mask)], axis=0)
        rels = rels + [rel | mask for rel in rels]
    found = [(stack, rels)]
    jumps = [0]
    for mask in split:
        jumps = jumps + [jump | mask for jump in jumps]
    for jump in jumps[1:]:
        found.append((swap(stack, "page", pages, jump), [rel ^ jump for rel in rels]))

    def finish(*others):
        first = swap(stack, "page", pages, low)
        more = [(first, [rel ^ low for rel in rels])]
        for array, rels_of in found[1:]:
            array = after(array, first, *others)
            more.append((swap(array, "page", pages, low), [rel ^ low for rel in rels_of]))
        return found + more

    return [array for array, _ in found[1:]], finish


def scatter_first(send, pages):
    return swap(send, "page", pages, 1)


def scatter_rest(keep, got, pages, direct):
    return scatter_last(keep + got.astype(WIDE), pages, 1, direct)


class Sum:
    def __init__(self, total, pages):
        self.pages = pages
        self.total = total
        if pages == 8:
            lows = [self.total[k].astype(LOW) for k in range(1, pages // 2)]
            self.ready = lows[0]
            self.parts = [swap(low, "page", pages, 2 * (k + 1)) for k, low in enumerate(lows)]
        else:
            self.ready = self.total
            self.parts = []

    def arrive(self, *others):
        if self.pages == 8:
            self.parts = [after(part, *others) for part in self.parts]
        else:
            self.parts = []

    def finish(self, *others):
        if self.pages != 8:
            return scatter_last(self.total, self.pages, 1, False)
        final = after(self.total[0], *others)
        for part in self.parts:
            final = final + part.astype(WIDE)
        return final


def scatter_last(total, pages, level, direct):
    left = pages >> level
    mask = 1 << level
    if direct and left == 4:
        lows = [total[k].astype(LOW) for k in range(1, left)]
        parts = [swap(low, "page", pages, 2 * (k + 1)) for k, low in enumerate(lows)]
        final = total[0]
        for part in parts:
            final = final + part.astype(WIDE)
        return final
    while left > 1:
        total = total.reshape((left // 2, 2) + total.shape[1:])
        got = swap(total[:, 1].astype(LOW), "page", pages, mask)
        total = total[:, 0] + got.astype(WIDE)
        left //= 2
        mask *= 2
    return total[0]


def scatter_bits(values, axis, count, dim, order):
    index = lax.axis_index(axis)
    for mask in order:
        shape = values.shape
        values = values.reshape(shape[:dim] + (shape[dim] // 2, 2) + shape[dim + 1 :])
        bit = (index // mask) % 2
        keep = lax.dynamic_index_in_dim(values, bit, dim + 1, keepdims=False)
        send = lax.dynamic_index_in_dim(values, 1 - bit, dim + 1, keepdims=False)
        values = keep.astype(WIDE) + swap(send.astype(LOW), axis, count, mask).astype(WIDE)
    return values


def scatter_start(values, axis, count, dim, mask):
    index = lax.axis_index(axis)
    shape = values.shape
    values = values.reshape(shape[:dim] + (shape[dim] // 2, 2) + shape[dim + 1 :])
    bit = (index // mask) % 2
    keep = lax.dynamic_index_in_dim(values, bit, dim + 1, keepdims=False)
    send = lax.dynamic_index_in_dim(values, 1 - bit, dim + 1, keepdims=False)
    return keep.astype(WIDE), swap(send.astype(LOW), axis, count, mask)


def reorder(pieces, index):
    count = len(pieces)
    out = []
    for k in range(count):
        value = pieces[0]
        for rel in range(1, count):
            value = jnp.where(index ^ k == rel, pieces[rel], value)
        out.append(value)
    return out


def turn(values, seqs, index):
    mine = [lax.dynamic_index_in_dim(values, index ^ rel, 0, keepdims=False) for rel in range(seqs)]
    return [mine[0]] + [swap(mine[rel], "seq", seqs, rel) for rel in range(1, seqs)]


def after(values, *others):
    return lax.optimization_barrier((values, others))[0]


def exchange(pieces):
    seqs = len(pieces)
    return [pieces[0]] + [swap(pieces[rel], "seq", seqs, rel) for rel in range(1, seqs)]


def fence(*values):
    return lax.optimization_barrier(values)


def to_all(values):
    return lax.all_to_all(values, ("page", "seq"), 0, 0)


def head_scores(qkv, h, span, depth, bias, same, mask):
    group = (h * depth) // 128
    lanes = lax.broadcasted_iota(jnp.int32, (1, 128), 1)
    mine = (lanes // depth) == (h % (128 // depth))
    q = qkv[:, group * 128 : group * 128 + 128]
    k = qkv[:, span + group * 128 : span + group * 128 + 128]
    raw = mul(jnp.where(mine, q, jnp.zeros_like(q)), k, NT)
    return raw * 0.125 + jnp.where(same, bias, 0.0) + mask, mine, group


def attend(pieces, block, spot, own_bias, inputs, vectors, column, row, mask, heads, depth):
    page_count, rows, width = inputs[0].shape
    seqs = len(inputs)
    slots = seqs * rows
    span = heads * depth
    arrays = [array for array, _ in pieces]
    rels = [rel for _, rel in pieces]
    n_arrays = len(arrays)

    blocks = sum(len(rel) for rel in rels)

    def body(spot_ref, bias_ref, *refs):
        weights = refs[:n_arrays]
        xs = refs[n_arrays : n_arrays + seqs]
        vec_ref, col_ref, row_ref, mask_ref = refs[n_arrays + seqs : n_arrays + seqs + 4]
        qkv_ref, lse_ref, full_ref = refs[n_arrays + seqs + 4 : n_arrays + seqs + 7]
        ctx_refs = refs[n_arrays + seqs + 7 : n_arrays + 2 * seqs + 7]
        x_all, sems = refs[n_arrays + 2 * seqs + 7 :]
        page = spot_ref[0]
        step = pl.program_id(0)

        @pl.when(step == 0)
        def _():
            pairs = [(xs[r], x_all.at[r]) for r in range(seqs)]
            for ref, rel_list in zip(weights, rels):
                for k, rel in enumerate(rel_list):
                    start = pl.multiple_of((page ^ rel) * block, block)
                    for t in range(3):
                        source = ref.at[k, pl.ds(t * block, block), :]
                        pairs.append((source, full_ref.at[pl.ds(start, block), pl.ds(t * span, span)]))
            for copy in bring(pairs, sems):
                copy.wait()

        at_q = pl.multiple_of(spot_ref[1] * span, span)
        row_bias = jnp.concatenate(
            [vec_ref[0:1, pl.ds(at_q, span)], jnp.zeros((1, span), WIDE), vec_ref[1:2, pl.ds(at_q, span)]],
            axis=1,
        )
        for r in range(seqs):
            part = mul(x_all[r, step], full_ref[...]) + row_bias
            qkv_ref[0, r * rows : (r + 1) * rows, :] = part.astype(LOW)
        qkv = qkv_ref[0]
        same = col_ref[0] == row_ref[0]
        key_mask = mask_ref[0]
        lane = lax.broadcasted_iota(jnp.int32, (1, 128), 1)
        lse = jnp.zeros((slots, 128), WIDE)
        context = [None] * (span // 128)
        for h in range(heads):
            scores, mine, group = head_scores(qkv, h, span, depth, bias_ref[h], same, key_mask)
            peak = jnp.max(scores, axis=-1, keepdims=True)
            exponent = jnp.exp(scores - peak)
            total = jnp.sum(exponent, axis=-1, keepdims=True)
            lse = jnp.where(lane == h, peak + jnp.log(total), lse)
            low = (exponent * (1.0 / total)).astype(LOW)
            v = qkv[:, 2 * span + group * 128 : 2 * span + group * 128 + 128]
            out = mul(low, v)
            context[group] = out if context[group] is None else jnp.where(mine, out, context[group])
        lse_ref[0] = lse
        for group, value in enumerate(context):
            value = value.astype(LOW)
            for r in range(seqs):
                ctx_refs[r][0, :, group * 128 : group * 128 + 128] = value[r * rows : (r + 1) * rows]

    def per_page(shape):
        zeros = (0,) * len(shape)
        return pl.BlockSpec((1,) + shape, lambda i: (i,) + zeros)

    flops = page_count * (2 * slots * width * 3 * span + 8 * heads * slots * slots * depth)
    return pl.pallas_call(
        body,
        grid=(page_count,),
        out_shape=[
            shaped((page_count, slots, 3 * span), LOW),
            shaped((page_count, slots, 128), WIDE),
            shaped((width, 3 * span), LOW),
        ]
        + [shaped((page_count, rows, span), LOW)] * seqs,
        in_specs=[scalars(), scalars()]
        + [remote()] * (n_arrays + seqs)
        + [fixed(vectors.shape), per_page((slots, 1)), per_page((1, slots)), per_page((1, slots))],
        out_specs=[per_page((slots, 3 * span)), per_page((slots, 128)), fixed((width, 3 * span))]
        + [per_page((rows, span))] * seqs,
        scratch_shapes=[
            pltpu.VMEM((seqs, page_count, rows, width), LOW),
            pltpu.SemaphoreType.DMA((seqs + 3 * blocks,)),
        ],
        compiler_params=params(24),
        cost_estimate=cost(flops, 10 << 20, page_count * heads * slots * slots),
        name="attend",
    )(spot, own_bias, *outside(arrays), *outside(inputs), vectors, column, row, mask)


def attend_back(spot, own_bias, qkv, lse, grads, inputs, column, row, mask, heads, depth, pages):
    page_count, slots, triple = qkv.shape
    span = triple // 3
    seqs = len(grads)
    rows = slots // seqs
    groups = span // 128
    width = inputs[0].shape[2]
    block = width // pages
    tile = 256 if width % 256 == 0 else width

    def body(spot_ref, bias_ref, qkv_ref, lse_ref, *refs):
        grad_refs, x_refs = refs[:seqs], refs[seqs : 2 * seqs]
        col_ref, row_ref, mask_ref, out_ref, sum_ref, cell_ref, keep, send = refs[2 * seqs : 2 * seqs + 8]
        full, x_all, g_all, sems = refs[2 * seqs + 8 :]
        step = pl.program_id(0)

        @pl.when(step == 0)
        def _():
            pairs = [(grad_refs[r], g_all.at[:, pl.ds(r * rows, rows), :]) for r in range(seqs)]
            pairs += [(x_refs[r], x_all.at[:, pl.ds(r * rows, rows), :]) for r in range(seqs)]
            for copy in bring(pairs, sems):
                copy.wait()

        page = spot_ref[0]
        qkv = qkv_ref[0]
        same = col_ref[0] == row_ref[0]
        key_mask = mask_ref[0]
        lane = lax.broadcasted_iota(jnp.int32, (1, 128), 1)
        sub = lax.broadcasted_iota(jnp.int32, (128, 1), 0)
        lse = lse_ref[0]
        grad = g_all[step]
        cell = jnp.zeros((1, 128), WIDE)
        dq, dk, dv = [None] * groups, [None] * groups, [None] * groups
        for h in range(heads):
            scores, mine, group = head_scores(qkv, h, span, depth, bias_ref[h], same, key_mask)
            mine_sub = (sub // depth) == (h % (128 // depth))
            at = group * 128
            q = qkv[:, at : at + 128]
            k = qkv[:, span + at : span + at + 128]
            v = qkv[:, 2 * span + at : 2 * span + at + 128]
            g = grad[:, at : at + 128]
            weights = jnp.exp(scores - lse[:, h : h + 1])
            slope = mul(jnp.where(mine, g, jnp.zeros_like(g)), v, NT)
            inner = jnp.sum(weights * slope, axis=-1, keepdims=True)
            ds = weights * (slope - inner)
            same_sum = jnp.sum(jnp.where(same, ds, 0.0), axis=0, keepdims=True)
            cell = jnp.where(lane == h, jnp.sum(same_sum, axis=1, keepdims=True), cell)
            ds_low = ds.astype(LOW)
            part_q = mul(ds_low, k)
            part_k = mul(q, ds_low, TN)
            part_v = mul(g, weights.astype(LOW), TN)
            dq[group] = part_q if dq[group] is None else jnp.where(mine, part_q, dq[group])
            dk[group] = part_k if dk[group] is None else jnp.where(mine_sub, part_k, dk[group])
            dv[group] = part_v if dv[group] is None else jnp.where(mine_sub, part_v, dv[group])
        cell_ref[0] = jnp.broadcast_to(cell, (8, 128))
        for group in range(groups):
            at = group * 128
            value_q = dq[group] * 0.125
            value_v = dv[group].T
            out_ref[0, :, at : at + 128] = value_q.astype(LOW)
            out_ref[0, :, span + at : span + at + 128] = (dk[group] * 0.125).T.astype(LOW)
            out_ref[0, :, 2 * span + at : 2 * span + at + 128] = value_v.astype(LOW)
            sum_ref[0, 0:1, at : at + 128] = jnp.sum(value_q, axis=0, keepdims=True)
            sum_ref[0, 0:1, span + at : span + at + 128] = jnp.sum(value_v, axis=0, keepdims=True)
        grad_proj = out_ref[0]

        @pl.when(step == 0)
        def _():
            for at in range(0, width, tile):
                full[at : at + tile, :] = mul(x_all[step, :, at : at + tile], grad_proj, TN)

        @pl.when(step > 0)
        def _():
            for at in range(0, width, tile):
                full[at : at + tile, :] += mul(x_all[step, :, at : at + tile], grad_proj, TN)

        @pl.when(step == page_count - 1)
        def _():
            low = page % 2
            for k in range(pages // 2):
                keep[k] = full[pl.ds(pl.multiple_of((2 * k + low) * block, block), block), :]
                start = pl.multiple_of((2 * k + 1 - low) * block, block)
                send[k] = full[pl.ds(start, block), :].astype(LOW)

    def per_page(shape):
        zeros = (0,) * len(shape)
        return pl.BlockSpec((1,) + shape, lambda i: (i,) + zeros)

    flops = page_count * (20 * heads * slots * slots * depth + 2 * slots * width * triple)
    return pl.pallas_call(
        body,
        grid=(page_count,),
        out_shape=[
            shaped((page_count, slots, triple), LOW),
            shaped((page_count, 8, 2 * span), WIDE),
            shaped((page_count, 8, 128), WIDE),
            shaped((pages // 2, block, triple), WIDE),
            shaped((pages // 2, block, triple), LOW),
        ],
        in_specs=[scalars(), scalars(), per_page((slots, triple)), per_page((slots, 128))]
        + [remote()] * (2 * seqs)
        + [per_page((slots, 1)), per_page((1, slots)), per_page((1, slots))],
        out_specs=[
            per_page((slots, triple)),
            per_page((8, 2 * span)),
            per_page((8, 128)),
            fixed((pages // 2, block, triple)),
            fixed((pages // 2, block, triple)),
        ],
        scratch_shapes=[
            pltpu.VMEM((width, triple), WIDE),
            pltpu.VMEM((page_count, slots, width), LOW),
            pltpu.VMEM((page_count, slots, span), LOW),
            pltpu.SemaphoreType.DMA((2 * seqs,)),
        ],
        compiler_params=params(28),
        cost_estimate=cost(flops, 10 << 20, page_count * heads * slots * slots),
        name="attend_back",
    )(spot, own_bias, *outside([qkv, lse]), *outside(grads), *outside(inputs), column, row, mask)


def page_order(values, rels, page_index):
    pages = len(rels)
    shape = values.shape
    if rels != sorted(rels):
        values = jnp.stack([values[rels.index(rel)] for rel in range(pages)])
    for bit in bits_of(pages):
        folded = values.reshape((pages // (2 * bit), 2, bit) + shape[1:])
        values = jnp.where((page_index // bit) % 2 == 0, folded, folded[:, ::-1])
    return values.reshape(shape)


def assemble_mix(near_blocks, rels, spot, rows, width):
    seqs = len(near_blocks)
    span = near_blocks[0].shape[2]
    if rows % 16:
        ordered = reorder([array.reshape(len(rels), -1, rows, span) for array in near_blocks], spot[1])
        ordered = jnp.stack([array.transpose(0, 2, 1, 3).reshape(len(rels), rows, width) for array in ordered], axis=1)
        return page_order(ordered, rels, spot[0]).reshape(width, width)

    def body(spot_ref, *refs):
        out, held, sems = refs[-3:]
        page, seq = spot_ref[0], spot_ref[1]
        for copy in bring([(refs[r], held.at[r]) for r in range(seqs)], sems):
            copy.wait()
        for r in range(seqs):
            for k, rel in enumerate(rels):
                start = pl.multiple_of(((page ^ rel) * seqs + (seq ^ r)) * rows, rows)
                for t in range(width // span):
                    out[pl.ds(start, rows), t * span : (t + 1) * span] = held[r, k, t * rows : (t + 1) * rows, :]

    return pl.pallas_call(
        body,
        out_shape=kept((width, width), LOW),
        in_specs=[scalars()] + [remote()] * seqs,
        out_specs=near(),
        scratch_shapes=[pltpu.VMEM((seqs,) + near_blocks[0].shape, LOW), pltpu.SemaphoreType.DMA((seqs,))],
        compiler_params=params(8),
        cost_estimate=cost(0, 4 * width * width),
        name="assemble_mix",
    )(spot, *outside(near_blocks))


def mix(spot, contexts, w_mix, inputs, vectors):
    flat, width = inputs.shape
    seqs = len(contexts)
    span = width // seqs

    def body(spot_ref, *refs):
        c_refs = refs[:seqs]
        w_ref, x_ref, vec_ref, wide_ref, low_ref, hat_ref, rstd_ref, c_all, x_here, sems = refs[seqs:]
        copies = bring([(c_refs[r], c_all.at[r]) for r in range(seqs)] + [(x_ref, x_here)], sems)
        for copy in copies:
            copy.wait()
        total = x_here[...].astype(WIDE) + vec_ref[2:3, :]
        for r in range(seqs):
            start = pl.multiple_of((spot_ref[1] ^ r) * span, span)
            total = total + mul(c_all[r], w_ref[pl.ds(start, span), :])
        center = total - jnp.mean(total, axis=-1, keepdims=True)
        spread = jnp.mean(center * center, axis=-1, keepdims=True)
        rstd = lax.rsqrt(spread + 1e-05)
        hat = center * rstd
        normed = hat * vec_ref[10:11, :] + vec_ref[4:5, :]
        wide_ref[...] = normed
        low_ref[...] = normed.astype(LOW)
        hat_ref[...] = hat
        rstd_ref[...] = jnp.broadcast_to(rstd, (flat, 128))

    return pl.pallas_call(
        body,
        out_shape=[
            kept((flat, width), WIDE),
            shaped((flat, width), LOW),
            shaped((flat, width), WIDE),
            shaped((flat, 128), WIDE),
        ],
        in_specs=[scalars()] + [remote()] * seqs + [near(), remote(), near()],
        out_specs=[near()] * 4,
        scratch_shapes=[
            pltpu.VMEM((seqs, flat, span), LOW),
            pltpu.VMEM((flat, width), LOW),
            pltpu.SemaphoreType.DMA((seqs + 1,)),
        ],
        compiler_params=params(12),
        cost_estimate=cost(2 * flat * width * width, 8 << 20),
        name="mix",
    )(spot, *outside(contexts), *inside([w_mix]), *outside([inputs]), vectors)


def second_norm(normed, keep, close, far, vectors, cotangent):
    flat, width = normed.shape

    def body(h_ref, k_ref, n_ref, f_ref, vec_ref, cot_ref, out, wide, low, sums, n_here, f_here, c_here, sems):
        for copy in bring([(n_ref, n_here), (f_ref, f_here), (cot_ref, c_here)], sems):
            copy.wait()
        total = h_ref[...] + (k_ref[...] + n_here[...].astype(WIDE) + f_here[...].astype(WIDE)) + vec_ref[3:4, :]
        center = total - jnp.mean(total, axis=-1, keepdims=True)
        spread = jnp.mean(center * center, axis=-1, keepdims=True)
        rstd = lax.rsqrt(spread + 1e-05)
        hat = center * rstd
        out[...] = (hat * vec_ref[11:12, :] + vec_ref[5:6, :]).astype(LOW)
        cot = c_here[...].astype(WIDE)
        slope = cot * vec_ref[11:12, :]
        first = jnp.mean(slope, axis=-1, keepdims=True)
        second = jnp.mean(slope * hat, axis=-1, keepdims=True)
        grad = rstd * (slope - first - hat * second)
        wide[...] = grad
        low[...] = grad.astype(LOW)
        sums[0:1, :] = jnp.sum(cot * hat, axis=0, keepdims=True)
        sums[1:2, :] = jnp.sum(cot, axis=0, keepdims=True)
        sums[2:3, :] = jnp.sum(grad, axis=0, keepdims=True)

    return pl.pallas_call(
        body,
        out_shape=[
            shaped((flat, width), LOW),
            kept((flat, width), WIDE),
            shaped((flat, width), LOW),
            shaped((8, width), WIDE),
        ],
        in_specs=[near(), near(), remote(), remote(), near(), remote()],
        out_specs=[near()] * 4,
        scratch_shapes=[pltpu.VMEM((flat, width), LOW)] * 3 + [pltpu.SemaphoreType.DMA((3,))],
        compiler_params=params(12),
        cost_estimate=cost(flat * width * 30, 7 << 20),
        name="second_norm",
    )(*inside([normed]), keep, *outside([close, far]), vectors, *outside([cotangent]))


def first_norm_back(spot, grad_second, keep, close, far, hat, rstd, vectors, w_mix, contexts, pages):
    flat, width = grad_second.shape
    seqs = len(contexts)
    span = width // seqs
    rows = width // (pages * seqs)
    with_mix = rows % 16 == 0

    def body(spot_ref, d_ref, k_ref, n_ref, f_ref, hat_ref, rstd_ref, vec_ref, w_ref, *refs):
        c_refs, (wide, low, sums) = refs[:seqs], refs[seqs : seqs + 3]
        outs, rest = refs[seqs + 3 : 2 * seqs + 3], refs[2 * seqs + 3 :]
        if with_mix:
            mix_keep, mix_send, n_here, f_here, c_here, hat_here, full, sems = rest
        else:
            n_here, f_here, c_here, hat_here, full, sems = rest
        pairs = [(n_ref, n_here), (f_ref, f_here), (hat_ref, hat_here)]
        copies = bring(pairs + [(c_refs[r], c_here.at[r]) for r in range(seqs)], sems)
        copies[0].wait()
        copies[1].wait()
        copies[2].wait()
        grad = d_ref[...] + (k_ref[...] + n_here[...].astype(WIDE) + f_here[...].astype(WIDE))
        hat = hat_here[...]
        slope = grad * vec_ref[10:11, :]
        first = jnp.mean(slope, axis=-1, keepdims=True)
        second = jnp.mean(slope * hat, axis=-1, keepdims=True)
        result = rstd_ref[:, 0:1] * (slope - first - hat * second)
        wide[...] = result
        result_low = result.astype(LOW)
        low[...] = result_low
        for r in range(seqs):
            start = pl.multiple_of((spot_ref[1] ^ r) * span, span)
            outs[r][...] = mul(result_low, w_ref[pl.ds(start, span), :], NT).astype(LOW)
        sums[0:1, :] = jnp.sum(grad * hat, axis=0, keepdims=True)
        sums[1:2, :] = jnp.sum(grad, axis=0, keepdims=True)
        sums[2:3, :] = jnp.sum(result, axis=0, keepdims=True)
        for copy in copies[3:]:
            copy.wait()
        if with_mix:
            for r in range(seqs):
                start = pl.multiple_of((spot_ref[1] ^ r) * span, span)
                full[pl.ds(start, span), :] = mul(c_here[r], result_low, TN)
            bit = spot_ref[1] % 2
            for p in range(pages):
                for k in range(seqs // 2):
                    start = pl.multiple_of((p * seqs + 2 * k + bit) * rows, rows)
                    mix_keep[p, k] = full[pl.ds(start, rows), :]
                    start = pl.multiple_of((p * seqs + 2 * k + 1 - bit) * rows, rows)
                    mix_send[p, k] = full[pl.ds(start, rows), :].astype(LOW)

    mix_shape = (pages, seqs // 2, rows, width)
    return pl.pallas_call(
        body,
        out_shape=[
            shaped((flat, width), WIDE),
            shaped((flat, width), LOW),
            shaped((8, width), WIDE),
        ]
        + [shaped((flat, span), LOW)] * seqs
        + ([shaped(mix_shape, WIDE), shaped(mix_shape, LOW)] if with_mix else []),
        in_specs=[scalars(), near(), near(), remote(), remote(), remote()] + [near()] * 3 + [remote()] * seqs,
        out_specs=[near()] * (3 + seqs + 2 * with_mix),
        scratch_shapes=[pltpu.VMEM((flat, width), LOW)] * 2
        + [
            pltpu.VMEM((seqs, flat, span), LOW),
            pltpu.VMEM((flat, width), WIDE),
            pltpu.VMEM((width, width), WIDE),
            pltpu.SemaphoreType.DMA((3 + seqs,)),
        ],
        compiler_params=params(20),
        cost_estimate=cost(2 * flat * width * width, 8 << 20),
        name="first_norm_back",
    )(
        spot,
        *inside([grad_second]),
        keep,
        *outside([close, far]),
        *outside([hat, rstd]),
        vectors,
        *inside([w_mix]),
        *outside(contexts),
    )


def weight_grad(spot, lefts, rights, pages, split, base=None):
    count = len(lefts)
    tokens, height = lefts[0].shape
    width = rights[0].shape[1]
    rows = height // pages
    tile = 256 if height % 256 == 0 else height

    def body(spot_ref, *refs):
        left, right = refs[:count], refs[count : 2 * count]
        base_ref = refs[2 * count] if base is not None else None
        outs = refs[2 * count + (base is not None) : -4]
        full, l_all, r_all, sems = refs[-4:]
        page = spot_ref[0]
        pairs = []
        for k in range(count):
            pairs.append((left[k], l_all.at[pl.ds(k * tokens, tokens), :]))
            pairs.append((right[k], r_all.at[pl.ds(k * tokens, tokens), :]))
        for copy in bring(pairs, sems):
            copy.wait()
        for at in range(0, height, tile):
            value = mul(l_all[:, at : at + tile], r_all[...], TN)
            if base is not None:
                value = value + base_ref[at : at + tile, :]
            (full if split else outs[0])[at : at + tile, :] = value
        if split:
            low = page % 2
            for k in range(pages // 2):
                outs[0][k] = full[pl.ds(pl.multiple_of((2 * k + low) * rows, rows), rows), :]
                start = pl.multiple_of((2 * k + 1 - low) * rows, rows)
                outs[1][k] = full[pl.ds(start, rows), :].astype(LOW)

    if split:
        outs = [shaped((pages // 2, rows, width), WIDE), shaped((pages // 2, rows, width), LOW)]
    else:
        outs = [kept((height, width), WIDE)]
    return pl.pallas_call(
        body,
        out_shape=outs,
        in_specs=[scalars()] + [remote()] * (2 * count) + [near()] * (base is not None),
        out_specs=[near()] * len(outs),
        scratch_shapes=[
            pltpu.VMEM((height, width) if split else (8, 128), WIDE),
            pltpu.VMEM((count * tokens, height), LOW),
            pltpu.VMEM((count * tokens, width), LOW),
            pltpu.SemaphoreType.DMA((2 * count,)),
        ],
        compiler_params=params(18),
        cost_estimate=cost(2 * count * tokens * height * width, 8 << 20),
        name="weight_grad",
    )(spot, *outside(lefts), *outside(rights), *(inside([base]) if base is not None else []))


def widen(values):
    def body(in_ref, out_ref):
        out_ref[...] = in_ref[...].astype(WIDE)

    return pl.pallas_call(
        body,
        out_shape=shaped(values.shape, WIDE),
        in_specs=[near()],
        out_specs=near(),
        compiler_params=params(4),
        cost_estimate=cost(values.size, 6 * values.size),
        name="widen",
    )(values)


def input_grad(grad_proj, w_proj, seqs):
    page_count, slots, triple = grad_proj.shape
    width = w_proj.shape[0]
    rows = slots // seqs

    def body(d_ref, w_ref, *outs):
        for rel in range(seqs):
            value = mul(d_ref[0, rel * rows : (rel + 1) * rows, :], w_ref[...], NT)
            outs[rel][0] = value.astype(outs[rel].dtype)

    per = pl.BlockSpec((1, rows, width), lambda i: (i, 0, 0))
    return pl.pallas_call(
        body,
        grid=(page_count,),
        out_shape=[shaped((page_count, rows, width), WIDE if rel % 2 == 0 else LOW) for rel in range(seqs)],
        in_specs=[pl.BlockSpec((1, slots, triple), lambda i: (i, 0, 0)), fixed(w_proj.shape)],
        out_specs=[per] * seqs,
        compiler_params=params(14),
        cost_estimate=cost(2 * page_count * slots * triple * width, 8 << 20),
        name="input_grad",
    )(*outside([grad_proj, w_proj]))


def local(counts, tokens, cells, lengths, cotangent, w_qkv, w_out, w_up, w_down, biases, gains, cell_bias):
    pages, seqs = counts
    page_count, row_count, width = tokens.shape
    slots = row_count * seqs
    heads = cell_bias.shape[0]
    depth = width // heads
    heads_here = heads // seqs
    span = heads_here * depth
    flat = page_count * row_count
    rows = w_qkv.shape[0]
    ff_rows = w_down.shape[0]
    ff_here = ff_rows * pages
    page_index = lax.axis_index("page")
    seq_index = lax.axis_index("seq")
    spot = jnp.stack([page_index, seq_index]).astype(jnp.int32)
    low_page = bits_of(pages)
    low_seq = bits_of(seqs)

    def scatter_near(keeps, sends):
        near_parts = [swap(send, "seq", seqs, 1) for send in sends]
        *result, sent = scatter_far_sent(keeps, near_parts)
        return (*result, sent)

    def scatter_far(keeps, nears):
        return scatter_far_sent(keeps, nears)[:3]

    def scatter_far_sent(totals, nears):
        far = jnp.zeros_like(nears[0])
        mask = 2
        while mask < seqs:
            half = [k for k in range(len(totals)) if (k * 2) & mask]
            ready = [(totals[k] + nears[k].astype(WIDE)).astype(LOW) for k in half]
            moved = [swap(value, "seq", seqs, mask) for value in ready]
            rest = [k for k in range(len(totals)) if not (k * 2) & mask]
            if mask * 2 >= seqs:
                far = moved[0]
                totals, nears = [totals[0]], [nears[0]]
            else:
                totals = [totals[k] + nears[k].astype(WIDE) for k in rest]
                nears = moved
            mask *= 2
        return totals[0], nears[0], far, ready[0]

    groups = [[page for page in range(pages) if page % 2 == low] for low in range(2)]

    def halved(keep, *got):
        got = jnp.concatenate(got, axis=1) if len(got) > 1 else got[0]
        return (keep + got.astype(WIDE)).astype(LOW).reshape(-1, keep.shape[-1])

    def scatter_same(values):
        return lax.psum_scatter(values, "page", scatter_dimension=0, tiled=True, axis_index_groups=groups)

    def small_table(sums_proj, cells_grad):
        owners = pages * seqs
        here = lax.broadcasted_iota(jnp.int32, (seqs, 1, 1), 0) == seq_index
        sums_proj = jnp.sum(sums_proj[:, 0], axis=0).reshape(2, 1, pages, lanes)

        def own(vector):
            return jnp.where(here, vector, 0.0).reshape(owners, 1, lanes)

        hidden_sum = functools.reduce(jnp.add, totals).reshape(pages, 1, ff_rows)
        hidden_sum = jnp.where(here.reshape(1, seqs, 1), hidden_sum, 0.0)
        hidden_sum = hidden_sum.reshape(-1, owners, lanes).transpose(1, 0, 2)
        cells_grad = jnp.sum(cells_grad[:, 0, :heads_here], axis=0)[None]
        cells_grad = jnp.where(here[:, 0], cells_grad, 0.0).reshape(heads)
        cells_grad = jnp.pad(cells_grad, (0, -heads % lanes)).reshape(1, -1, lanes)

        def row_of(sums, k):
            return sums[k].reshape(owners, 1, lanes)

        return to_all(
            jnp.concatenate(
                [
                    own(sums_proj[0]),
                    own(sums_proj[1]),
                    row_of(sums_one, 2),
                    row_of(sums_two, 2),
                    row_of(sums_one, 1),
                    row_of(sums_two, 1),
                    hidden_sum,
                    row_of(sums_one, 0),
                    row_of(sums_two, 0),
                    jnp.broadcast_to(cells_grad, (owners,) + cells_grad.shape[1:]),
                ],
                axis=1,
            )
        )

    def block_rows(values):
        return values.reshape(values.shape[0], -1, span)

    small = jnp.concatenate([biases, gains], axis=0).astype(LOW)
    small_rows, lanes = small.shape
    digits = jnp.concatenate([cells // 16, cells % 16], axis=0).astype(LOW)
    extra = jnp.concatenate(
        [jnp.pad(small, ((0, 0), (0, span - lanes))), jnp.pad(digits, ((0, 0), (0, span - row_count)))], axis=0
    )
    part_qkv = w_qkv.astype(LOW).reshape(rows, 3, seqs, span).transpose(2, 1, 0, 3)
    part_up = w_up.astype(LOW).reshape(rows, pages, seqs, ff_rows).transpose(2, 0, 1, 3)
    sent = jnp.concatenate(
        [
            part_qkv.reshape(seqs, 3 * rows, span),
            jnp.broadcast_to(extra, (seqs,) + extra.shape),
            part_up.reshape(seqs, pages * rows * ff_rows // span, span),
        ],
        axis=1,
    )
    turned = jnp.stack(reorder(turn(sent, seqs, seq_index), seq_index))
    part_qkv = turned[:, : 3 * rows].reshape(seqs, 3, rows, span).transpose(1, 0, 2, 3)
    extras = turned[:, 3 * rows : 3 * rows + extra.shape[0]]
    part_up = turned[:, 3 * rows + extra.shape[0] :].reshape(seqs * rows, ff_here)
    digits = extras[:, small_rows : small_rows + 2 * page_count, :row_count].astype(jnp.int32)
    cells_all = digits[:, :page_count] * 16 + digits[:, page_count:]
    cells_all = jnp.stack(reorder([cells_all[k] for k in range(seqs)], seq_index), axis=1)
    cells_all = cells_all.reshape(page_count, slots)

    part_mix = w_out.astype(LOW).reshape(rows, width // span, span).transpose(1, 0, 2)
    part_small = extras[:, :small_rows, :lanes].transpose(1, 0, 2).reshape(small_rows, seqs * lanes)
    part_small = jnp.pad(part_small, ((0, -small_rows % 16), (0, span - seqs * lanes)))
    block = seqs * rows
    part_both = jnp.concatenate(
        [part_qkv.reshape(3 * block, span), part_mix.reshape(-1, span), part_small], axis=0
    )
    split = low_page[1:3][::-1]
    stack, rels = part_both[None], [0]
    for bit in low_page[:0:-1][: len(low_page) - 1 - len(split)]:
        stack = jnp.concatenate([stack, swap(stack, "page", pages, bit)], axis=0)
        rels = rels + [rel | bit for rel in rels]
    jumps = [0]
    for bit in split:
        jumps = jumps + [jump | bit for jump in jumps]
    across = [swap(stack, "page", pages, jump) for jump in jumps[1:]]
    beside = [swap(stack, "page", pages, 1)]
    x_near = [tokens]
    x_far = swap(after(tokens, part_both), "seq", seqs, low_seq[-1])
    *across, part_up, first_beside, x_far, w_down_low, x_own = fence(
        *across, part_up, beside[0], x_far, w_down.astype(LOW), tokens
    )
    beside = [first_beside] + [swap(array, "page", pages, 1) for array in across]
    both_pieces = [(array, [rel ^ jump for rel in rels]) for array, jump in zip([stack] + across, jumps)]
    both_pieces += [(array, [rel ^ jump ^ 1 for rel in rels]) for array, jump in zip(beside, jumps)]
    inputs = {0: x_own, low_seq[-1]: x_far}
    for bit in low_seq[:-1][::-1]:
        for rel in list(inputs):
            inputs[rel | bit] = swap(inputs[rel], "seq", seqs, bit)
    inputs = [inputs[rel] for rel in range(seqs)]
    feed_both = lax.all_gather(jnp.concatenate([part_up, w_down_low], axis=0), "page", axis=0, tiled=False)
    w_expand = feed_both[:, :block].reshape(width, ff_here)
    w_reduce = feed_both[:, block:].reshape(ff_here, width)
    fenced = fence(*[array for array, _ in both_pieces], *inputs)
    inputs = list(fenced[len(both_pieces) :])
    both_pieces = [(array, rel) for array, (_, rel) in zip(fenced[: len(both_pieces)], both_pieces)]
    both_rels = [rel for _, rel_list in both_pieces for rel in rel_list]
    vectors = jnp.concatenate([array[:, 4 * block :, :] for array, _ in both_pieces], axis=0)
    vectors = page_order(vectors[:, :small_rows, : seqs * lanes], both_rels, page_index)
    vectors = vectors.reshape(pages, small_rows, seqs * lanes).transpose(1, 0, 2)
    vectors = vectors.reshape(small_rows, width).astype(WIDE)
    hidden_bias = vectors[6:10].reshape(pages, seqs, ff_rows)
    hidden_bias = lax.dynamic_index_in_dim(hidden_bias, seq_index, 1, keepdims=False).reshape(1, ff_here)

    position = lax.broadcasted_iota(jnp.int32, (1, slots), 1)
    position = ((position // row_count) ^ seq_index) * row_count + position % row_count
    mask = jnp.where(position < lengths[:, None], 0.0, -1e30).astype(WIDE)[:, None, :]
    column, row = cells_all[:, :, None], cells_all[:, None, :]
    own_bias = lax.dynamic_slice_in_dim(cell_bias, seq_index * heads_here, heads_here)
    mix_part = jnp.concatenate([array[:, 3 * block : 4 * block, :] for array, _ in both_pieces], axis=0)
    mix_far = swap(mix_part, "seq", seqs, low_seq[-1])
    qkv, lse, w_proj, *contexts = attend(
        [(after(array, mix_part), rel_list) for array, rel_list in both_pieces],
        block,
        spot,
        own_bias,
        inputs,
        vectors,
        column,
        row,
        mask,
        heads_here,
        depth,
    )
    mix_part, mix_far, qkv, lse, w_proj, *contexts = fence(mix_part, mix_far, qkv, lse, w_proj, *contexts)
    mix_near = {0: mix_part, low_seq[-1]: mix_far}
    for bit in low_seq[:-1][::-1]:
        for rel in list(mix_near):
            mix_near[rel | bit] = swap(mix_near[rel], "seq", seqs, bit)
    contexts = exchange([context.reshape(flat, span) for context in contexts])
    w_mix = assemble_mix([mix_near[rel] for rel in range(seqs)], both_rels, spot, rows, width)

    flat_inputs = tokens.reshape(flat, width)
    normed, normed_low, hat, rstd = mix(spot, contexts, w_mix, flat_inputs, vectors)
    hidden, active, parts = {}, {}, {}

    def feed(rels, *others):
        for rel in rels:
            piece = after(normed_all[rel], *others)
            value = jnp.dot(piece, w_expand, preferred_element_type=WIDE) + hidden_bias
            active[rel] = gelu_exact(value).astype(LOW)
            part = jnp.dot(active[rel], w_reduce, preferred_element_type=WIDE)
            parts[rel] = part.astype(LOW) if rel % 2 else part
            hidden[rel] = value

    normed_all = gather_near(normed_low, seqs)
    feed(range(seqs // 2, seqs))
    far_parts = [swap(parts[rel], "seq", seqs, 1) for rel in range(seqs // 2 + 1, seqs, 2)]
    far_sums = [parts[rel] + part.astype(WIDE) for rel, part in zip(range(seqs // 2, seqs, 2), far_parts)]
    ready = far_sums[0].astype(LOW)
    far = swap(ready, "seq", seqs, seqs // 2)
    feed(range(seqs // 2), ready)
    keep, close = parts[0], swap(parts[1], "seq", seqs, 1)
    slopes = [
        0.5 * (1.0 + lax.erf(u * 0.7071067811865476)) + u * jnp.exp(-0.5 * u * u) * 0.3989422804014327
        for u in after([hidden[rel] for rel in range(seqs)], ready)
    ]
    active = [active[rel] for rel in range(seqs)]
    far, slopes = lax.optimization_barrier((far, slopes))
    output, grad_second, second_low, sums_two = second_norm(
        normed, keep, close, far, vectors, cotangent.reshape(flat, width)
    )

    expanded, parts, totals = [], [], []

    def feed_back(pieces):
        for piece in pieces:
            slope = slopes[len(parts)]
            value = jnp.einsum("td,fd->tf", piece, w_reduce, preferred_element_type=WIDE) * slope
            low = value.astype(LOW)
            part = jnp.einsum("tf,df->td", low, w_expand, preferred_element_type=WIDE)
            part = part.astype(LOW) if len(parts) % 2 else part
            expanded.append(low)
            totals.append(jnp.sum(value, axis=0))
            parts.append(part)
        if len(parts) == len(pieces):
            bases.extend(weight_grad(spot, active[: len(pieces)], pieces, pages, False))
        return tuple(parts + bases)

    bases = []
    second_all = gather_near(second_low, seqs, feed_back)
    feed_back(second_all[seqs // 2 :])
    keep, close, far, ready = scatter_near(parts[0::2], parts[1::2])
    half = seqs // 2
    down_keep, down_send = weight_grad(
        spot, after(active[half:], ready), second_all[half:], pages, True, bases[0]
    )
    up_base = weight_grad(spot, after(normed_all[:half], down_send), expanded[:half], pages, False)[0]
    far, up_base = fence(far, up_base)
    down_got = scatter_first(down_send, pages)
    grad_first, first_low, sums_one, *mix_grads = first_norm_back(
        spot, grad_second, keep, close, far, hat, rstd, vectors, w_mix, contexts, pages
    )
    grad_contexts, mix_grads = mix_grads[:seqs], mix_grads[seqs:]
    up_keep, up_send = weight_grad(
        spot, after(normed_all[half:], first_low), expanded[half:], pages, True, up_base
    )
    grad_contexts = exchange(grad_contexts)
    if mix_grads:
        mix_keep, mix_send = mix_grads
        mix_parts = swap(mix_send, "seq", seqs, 1)
    else:
        context = jnp.concatenate(reorder(contexts, seq_index), axis=1)
        grad_mix = jnp.einsum("tc,td->cd", context, first_low, preferred_element_type=WIDE)
        mix_keep, mix_parts = scatter_start(grad_mix.reshape(pages, seqs, rows, width), "seq", seqs, 1, 1)
    mix_keep, mix_parts, down_got, down_keep, *others = fence(
        mix_keep, mix_parts, down_got, down_keep, *grad_contexts, up_send
    )
    grad_contexts, up_send = others[:seqs], others[seqs]
    down_half = halved(down_keep, down_got)
    up_got = scatter_first(up_send, pages)
    mix_total = (mix_keep + mix_parts.astype(WIDE)).reshape(pages, seqs // 2, rows, width)
    mix_keep, mix_parts = scatter_start(mix_total, "seq", seqs, 1, low_seq[1])
    grad_contexts = after(grad_contexts, down_half)
    grad_reduce = scatter_same(down_half)
    grad_contexts = [grad.reshape(page_count, row_count, span) for grad in grad_contexts]
    grad_proj, sums_proj, cells_grad, proj_keep, proj_send = attend_back(
        spot, own_bias, qkv, lse, grad_contexts, inputs, column, row, mask, heads_here, depth, pages
    )
    grad_proj, sums_proj, cells_grad, proj_keep, proj_send, up_keep, mix_keep, mix_parts = fence(
        grad_proj, sums_proj, cells_grad, proj_keep, proj_send, up_keep, mix_keep, mix_parts
    )
    proj_got = scatter_first(proj_send, pages)
    grad_mix = (mix_keep + mix_parts.astype(WIDE)).reshape(pages, rows, width)
    mix_keep, mix_parts = scatter_start(grad_mix, "page", pages, 0, 1)
    grad_expand = scatter_same(halved(up_keep, up_got))
    parts = input_grad(after(grad_proj, proj_send), w_proj, seqs)
    near_parts = [swap(part, "seq", seqs, 1) for part in parts[1::2]]
    proj_got, proj_keep, sums_proj, cells_grad, mix_keep, mix_parts, grad_expand, grad_reduce, *near_parts = fence(
        proj_got, proj_keep, sums_proj, cells_grad, mix_keep, mix_parts, grad_expand, grad_reduce, *near_parts
    )
    proj_half = halved(proj_keep, proj_got)
    grad_qkv = scatter_same(proj_half)
    grad_reduce = widen(after(grad_reduce, proj_half))
    near_parts, sums_proj, cells_grad, mix_keep, mix_parts = after(
        (near_parts, sums_proj, cells_grad, mix_keep, mix_parts), grad_reduce
    )
    keep, close, far = scatter_far(parts[0::2], near_parts)
    small_sums = small_table(sums_proj, cells_grad)
    mix_keep, mix_parts = scatter_start(mix_keep + mix_parts.astype(WIDE), "page", pages, 0, 2)
    grad_qkv, far, small_sums, mix_keep, mix_parts = fence(grad_qkv, far, small_sums, mix_keep, mix_parts)
    grad_mix = mix_keep + mix_parts.astype(WIDE)
    grad_mix = scatter_bits(grad_mix, "page", pages, 0, low_page[2:]).reshape(rows, width)
    sent = jnp.concatenate(
        [
            grad_qkv.reshape(seqs, rows, 3, span).transpose(0, 2, 1, 3).reshape(seqs, 3 * rows, span),
            grad_expand.reshape(seqs, -1, span),
        ],
        axis=1,
    ).astype(LOW)
    turned = jnp.stack(reorder(turn(sent, seqs, seq_index), seq_index))
    grad_qkv = turned[:, : 3 * rows].reshape(seqs, 3, rows, span).transpose(2, 1, 0, 3)
    grad_qkv = grad_qkv.reshape(rows, 3 * width).astype(WIDE)
    grad_expand = turned[:, 3 * rows :].reshape(seqs, rows, pages, ff_rows).transpose(1, 2, 0, 3)
    grad_expand = grad_expand.reshape(rows, seqs * ff_here).astype(WIDE)
    grad_inputs = grad_first.reshape(page_count, row_count, width) + (
        keep + close.astype(WIDE) + far.astype(WIDE)
    )

    summed = jnp.sum(small_sums, axis=0)
    return (
        output.reshape(page_count, row_count, width),
        grad_inputs,
        grad_qkv,
        grad_mix,
        grad_expand,
        grad_reduce,
        summed[:10],
        summed[10:12],
        summed[12:].reshape(-1)[:heads],
    )


def solution(mesh):
    counts = (mesh.shape["page"], mesh.shape["seq"])
    placed = (
        P("page", "seq", None),
        P("page", "seq"),
        P("page"),
        P("page", "seq", None),
        P(("page", "seq"), None),
        P(("page", "seq"), None),
        P(("page", "seq"), None),
        P(("page", "seq"), None),
        P(None, ("page", "seq")),
        P(None, ("page", "seq")),
        P(),
    )

    def step(*args):
        return local(counts, *args)

    return jax.shard_map(
        step,
        mesh=mesh,
        in_specs=placed,
        out_specs=(
            P("page", "seq", None),
            P("page", "seq", None),
            P(("page", "seq"), None),
            P(("page", "seq"), None),
            P(("page", "seq"), None),
            P(("page", "seq"), None),
            P(None, ("page", "seq")),
            P(None, ("page", "seq")),
            P(),
        ),
        check_vma=False,
    )
```

```python
import functools

import jax
import jax.numpy as jnp
from jax import lax
from jax.experimental import pallas as pl
from jax.experimental.pallas import tpu as pltpu
from jax.sharding import PartitionSpec as P

LOW = jnp.bfloat16
WIDE = jnp.float32


def gelu_exact(values):
    return 0.5 * values * (1.0 + lax.erf(values * 0.7071067811865476))


NT = (((1,), (1,)), ((), ()))
TN = (((0,), (0,)), ((), ()))
NN = (((1,), (0,)), ((), ()))
ONCE = pl.Buffered(1)


def mul(left, right, dims=NN):
    return lax.dot_general(left, right, dims, preferred_element_type=WIDE)


def shaped(shape, dtype):
    return pltpu.HBM(shape, dtype)


def kept(shape, dtype):
    return pltpu.VMEM(shape, dtype)


def fixed(shape):
    zeros = (0,) * len(shape)
    return pl.BlockSpec(shape, lambda *_: zeros, pipeline_mode=ONCE)


def scalars():
    return pl.BlockSpec(memory_space=pltpu.SMEM)


def remote():
    return pl.BlockSpec(memory_space=pltpu.HBM)


def outside(values):
    return [pltpu.with_memory_space_constraint(value, pltpu.HBM) for value in values]


def inside(values):
    return [pltpu.with_memory_space_constraint(value, pltpu.VMEM) for value in values]


def near():
    return pl.BlockSpec(memory_space=pltpu.VMEM)


def bring(pairs, sems):
    copies = []
    for source, target in pairs:
        copy = pltpu.make_async_copy(source, target, sems.at[len(copies)])
        copy.start()
        copies.append(copy)
    return copies


def params(megabytes):
    return pltpu.CompilerParams(vmem_limit_bytes=megabytes * 1024 * 1024)


def cost(flops, moved, extra=0):
    return pl.CostEstimate(flops=int(flops), bytes_accessed=int(moved), transcendentals=int(extra))


def swap(values, axis, count, mask):
    return lax.ppermute(values, axis, [(i, i ^ mask) for i in range(count)])


def bits_of(count):
    return [1 << k for k in range(count.bit_length() - 1)]


def gather_near(values, seqs, between=None, wait=()):
    top = bits_of(seqs)[-1]
    far = swap(values, "seq", seqs, top)
    pieces = {0: after(values, *wait) if wait else values}
    for mask in bits_of(top)[::-1]:
        for rel in list(pieces):
            pieces[rel | mask] = swap(pieces[rel], "seq", seqs, mask)
    if between is not None:
        far = after(far, between([pieces[rel] for rel in range(top)]))
    pieces[top] = far
    for mask in bits_of(top)[::-1]:
        for rel in [rel for rel in pieces if rel & top]:
            pieces[rel | mask] = swap(pieces[rel], "seq", seqs, mask)
    return [pieces[rel] for rel in range(seqs)]


def gather_pages(values, pages, hold=None):
    stack, rels = values[None], [0]
    masks = bits_of(pages)[::-1]
    low, high = masks[-1], masks[:-1]
    split = high[-2:]
    for mask in high[:-2]:
        stack = jnp.concatenate([stack, swap(stack, "page", pages, mask)], axis=0)
        rels = rels + [rel | mask for rel in rels]
    found = [(stack, rels)]
    jumps = [0]
    for mask in split:
        jumps = jumps + [jump | mask for jump in jumps]
    for jump in jumps[1:]:
        found.append((swap(stack, "page", pages, jump), [rel ^ jump for rel in rels]))

    def finish(*others):
        first = swap(stack, "page", pages, low)
        more = [(first, [rel ^ low for rel in rels])]
        for array, rels_of in found[1:]:
            array = after(array, first, *others)
            more.append((swap(array, "page", pages, low), [rel ^ low for rel in rels_of]))
        return found + more

    return [array for array, _ in found[1:]], finish


def scatter_first(send, pages):
    return swap(send, "page", pages, 1)


def scatter_rest(keep, got, pages, direct):
    return scatter_last(keep + got.astype(WIDE), pages, 1, direct)


class Sum:
    def __init__(self, total, pages):
        self.pages = pages
        self.total = total
        if pages == 8:
            lows = [self.total[k].astype(LOW) for k in range(1, pages // 2)]
            self.ready = lows[0]
            self.parts = [swap(low, "page", pages, 2 * (k + 1)) for k, low in enumerate(lows)]
        else:
            self.ready = self.total
            self.parts = []

    def arrive(self, *others):
        if self.pages == 8:
            self.parts = [after(part, *others) for part in self.parts]
        else:
            self.parts = []

    def finish(self, *others):
        if self.pages != 8:
            return scatter_last(self.total, self.pages, 1, False)
        final = after(self.total[0], *others)
        for part in self.parts:
            final = final + part.astype(WIDE)
        return final


def scatter_last(total, pages, level, direct):
    left = pages >> level
    mask = 1 << level
    if direct and left == 4:
        lows = [total[k].astype(LOW) for k in range(1, left)]
        parts = [swap(low, "page", pages, 2 * (k + 1)) for k, low in enumerate(lows)]
        final = total[0]
        for part in parts:
            final = final + part.astype(WIDE)
        return final
    while left > 1:
        total = total.reshape((left // 2, 2) + total.shape[1:])
        got = swap(total[:, 1].astype(LOW), "page", pages, mask)
        total = total[:, 0] + got.astype(WIDE)
        left //= 2
        mask *= 2
    return total[0]


def scatter_bits(values, axis, count, dim, order):
    index = lax.axis_index(axis)
    for mask in order:
        shape = values.shape
        values = values.reshape(shape[:dim] + (shape[dim] // 2, 2) + shape[dim + 1 :])
        bit = (index // mask) % 2
        keep = lax.dynamic_index_in_dim(values, bit, dim + 1, keepdims=False)
        send = lax.dynamic_index_in_dim(values, 1 - bit, dim + 1, keepdims=False)
        values = keep.astype(WIDE) + swap(send.astype(LOW), axis, count, mask).astype(WIDE)
    return values


def scatter_start(values, axis, count, dim, mask):
    index = lax.axis_index(axis)
    shape = values.shape
    values = values.reshape(shape[:dim] + (shape[dim] // 2, 2) + shape[dim + 1 :])
    bit = (index // mask) % 2
    keep = lax.dynamic_index_in_dim(values, bit, dim + 1, keepdims=False)
    send = lax.dynamic_index_in_dim(values, 1 - bit, dim + 1, keepdims=False)
    return keep.astype(WIDE), swap(send.astype(LOW), axis, count, mask)


def reorder(pieces, index):
    count = len(pieces)
    out = []
    for k in range(count):
        value = pieces[0]
        for rel in range(1, count):
            value = jnp.where(index ^ k == rel, pieces[rel], value)
        out.append(value)
    return out


def turn(values, seqs, index):
    mine = [lax.dynamic_index_in_dim(values, index ^ rel, 0, keepdims=False) for rel in range(seqs)]
    return [mine[0]] + [swap(mine[rel], "seq", seqs, rel) for rel in range(1, seqs)]


def after(values, *others):
    return lax.optimization_barrier((values, others))[0]


def exchange(pieces):
    seqs = len(pieces)
    return [pieces[0]] + [swap(pieces[rel], "seq", seqs, rel) for rel in range(1, seqs)]


def fence(*values):
    return lax.optimization_barrier(values)


def to_all(values):
    return lax.all_to_all(values, ("page", "seq"), 0, 0)


def head_scores(qkv, h, span, depth, bias, same, mask):
    group = (h * depth) // 128
    lanes = lax.broadcasted_iota(jnp.int32, (1, 128), 1)
    mine = (lanes // depth) == (h % (128 // depth))
    q = qkv[:, group * 128 : group * 128 + 128]
    k = qkv[:, span + group * 128 : span + group * 128 + 128]
    raw = mul(jnp.where(mine, q * 0.125, jnp.zeros_like(q)), k, NT)
    return raw + jnp.where(same, mask + bias, mask), mine, group


def attend(pieces, block, spot, own_bias, inputs, vectors, column, row, mask, heads, depth):
    page_count, rows, width = inputs[0].shape
    seqs = len(inputs)
    slots = seqs * rows
    span = heads * depth
    arrays = [array for array, _ in pieces]
    rels = [rel for _, rel in pieces]
    n_arrays = len(arrays)

    blocks = sum(len(rel) for rel in rels)

    def body(spot_ref, bias_ref, *refs):
        weights = refs[:n_arrays]
        xs = refs[n_arrays : n_arrays + seqs]
        vec_ref, col_ref, row_ref, mask_ref = refs[n_arrays + seqs : n_arrays + seqs + 4]
        qkv_ref, lse_ref, full_ref = refs[n_arrays + seqs + 4 : n_arrays + seqs + 7]
        ctx_refs = refs[n_arrays + seqs + 7 : n_arrays + 2 * seqs + 7]
        x_all, sems = refs[n_arrays + 2 * seqs + 7 :]
        page = spot_ref[0]
        step = pl.program_id(0)

        @pl.when(step == 0)
        def _():
            pairs = [(xs[r], x_all.at[r]) for r in range(seqs)]
            for ref, rel_list in zip(weights, rels):
                for k, rel in enumerate(rel_list):
                    start = pl.multiple_of((page ^ rel) * block, block)
                    for t in range(3):
                        source = ref.at[k, pl.ds(t * block, block), :]
                        pairs.append((source, full_ref.at[pl.ds(start, block), pl.ds(t * span, span)]))
            for copy in bring(pairs, sems):
                copy.wait()

        at_q = pl.multiple_of(spot_ref[1] * span, span)
        row_bias = jnp.concatenate(
            [vec_ref[0:1, pl.ds(at_q, span)], jnp.zeros((1, span), WIDE), vec_ref[1:2, pl.ds(at_q, span)]],
            axis=1,
        )
        for r in range(seqs):
            part = mul(x_all[r, step], full_ref[...]) + row_bias
            qkv_ref[0, r * rows : (r + 1) * rows, :] = part.astype(LOW)
        qkv = qkv_ref[0]
        same = col_ref[0] == row_ref[0]
        key_mask = mask_ref[0]
        lane = lax.broadcasted_iota(jnp.int32, (1, 128), 1)
        lse = jnp.zeros((slots, 128), WIDE)
        context = [None] * (span // 128)
        for h in range(heads):
            scores, mine, group = head_scores(qkv, h, span, depth, bias_ref[h], same, key_mask)
            peak = jnp.max(scores, axis=-1, keepdims=True)
            exponent = jnp.exp(scores - peak)
            total = jnp.sum(exponent, axis=-1, keepdims=True)
            lse = jnp.where(lane == h, peak + jnp.log(total), lse)
            low = (exponent * (1.0 / total)).astype(LOW)
            v = qkv[:, 2 * span + group * 128 : 2 * span + group * 128 + 128]
            out = mul(low, v)
            context[group] = out if context[group] is None else jnp.where(mine, out, context[group])
        lse_ref[0] = lse
        for group, value in enumerate(context):
            value = value.astype(LOW)
            for r in range(seqs):
                ctx_refs[r][0, :, group * 128 : group * 128 + 128] = value[r * rows : (r + 1) * rows]

    def per_page(shape):
        zeros = (0,) * len(shape)
        return pl.BlockSpec((1,) + shape, lambda i: (i,) + zeros)

    flops = page_count * (2 * slots * width * 3 * span + 8 * heads * slots * slots * depth)
    return pl.pallas_call(
        body,
        grid=(page_count,),
        out_shape=[
            shaped((page_count, slots, 3 * span), LOW),
            shaped((page_count, slots, 128), WIDE),
            shaped((width, 3 * span), LOW),
        ]
        + [shaped((page_count, rows, span), LOW)] * seqs,
        in_specs=[scalars(), scalars()]
        + [remote()] * (n_arrays + seqs)
        + [fixed(vectors.shape), per_page((slots, 1)), per_page((1, slots)), per_page((1, slots))],
        out_specs=[per_page((slots, 3 * span)), per_page((slots, 128)), fixed((width, 3 * span))]
        + [per_page((rows, span))] * seqs,
        scratch_shapes=[
            pltpu.VMEM((seqs, page_count, rows, width), LOW),
            pltpu.SemaphoreType.DMA((seqs + 3 * blocks,)),
        ],
        compiler_params=params(24),
        cost_estimate=cost(flops, 10 << 20, page_count * heads * slots * slots),
        name="attend",
    )(spot, own_bias, *outside(arrays), *outside(inputs), vectors, column, row, mask)


def attend_back(spot, own_bias, qkv, lse, grads, inputs, column, row, mask, heads, depth, pages):
    page_count, slots, triple = qkv.shape
    span = triple // 3
    seqs = len(grads)
    rows = slots // seqs
    groups = span // 128
    width = inputs[0].shape[2]
    block = width // pages
    tile = 256 if width % 256 == 0 else width

    def body(spot_ref, bias_ref, qkv_ref, lse_ref, *refs):
        grad_refs, x_refs = refs[:seqs], refs[seqs : 2 * seqs]
        col_ref, row_ref, mask_ref, out_ref, sum_ref, cell_ref, keep, send = refs[2 * seqs : 2 * seqs + 8]
        full, x_all, g_all, sems = refs[2 * seqs + 8 :]
        step = pl.program_id(0)

        @pl.when(step == 0)
        def _():
            pairs = [(grad_refs[r], g_all.at[:, pl.ds(r * rows, rows), :]) for r in range(seqs)]
            pairs += [(x_refs[r], x_all.at[:, pl.ds(r * rows, rows), :]) for r in range(seqs)]
            for copy in bring(pairs, sems):
                copy.wait()

        page = spot_ref[0]
        qkv = qkv_ref[0]
        same = col_ref[0] == row_ref[0]
        key_mask = mask_ref[0]
        lane = lax.broadcasted_iota(jnp.int32, (1, 128), 1)
        sub = lax.broadcasted_iota(jnp.int32, (128, 1), 0)
        lse = lse_ref[0]
        grad = g_all[step]
        cell = jnp.zeros((1, 128), WIDE)
        dq, dk, dv = [None] * groups, [None] * groups, [None] * groups
        for h in range(heads):
            scores, mine, group = head_scores(qkv, h, span, depth, bias_ref[h], same, key_mask)
            mine_sub = (sub // depth) == (h % (128 // depth))
            at = group * 128
            q = qkv[:, at : at + 128]
            k = qkv[:, span + at : span + at + 128]
            v = qkv[:, 2 * span + at : 2 * span + at + 128]
            g = grad[:, at : at + 128]
            weights = jnp.exp(scores - lse[:, h : h + 1])
            slope = mul(jnp.where(mine, g, jnp.zeros_like(g)), v, NT)
            inner = jnp.sum(weights * slope, axis=-1, keepdims=True)
            ds = weights * (slope - inner)
            same_sum = jnp.sum(jnp.where(same, ds, 0.0), axis=0, keepdims=True)
            cell = jnp.where(lane == h, jnp.sum(same_sum, axis=1, keepdims=True), cell)
            ds_low = ds.astype(LOW)
            part_q = mul(ds_low, k)
            part_k = mul(q, ds_low, TN)
            part_v = mul(g, weights.astype(LOW), TN)
            dq[group] = part_q if dq[group] is None else jnp.where(mine, part_q, dq[group])
            dk[group] = part_k if dk[group] is None else jnp.where(mine_sub, part_k, dk[group])
            dv[group] = part_v if dv[group] is None else jnp.where(mine_sub, part_v, dv[group])
        cell_ref[0] = jnp.broadcast_to(cell, (8, 128))
        for group in range(groups):
            at = group * 128
            value_q = dq[group] * 0.125
            value_v = dv[group].T
            out_ref[0, :, at : at + 128] = value_q.astype(LOW)
            out_ref[0, :, span + at : span + at + 128] = (dk[group] * 0.125).T.astype(LOW)
            out_ref[0, :, 2 * span + at : 2 * span + at + 128] = value_v.astype(LOW)
            sum_ref[0, 0:1, at : at + 128] = jnp.sum(value_q, axis=0, keepdims=True)
            sum_ref[0, 0:1, span + at : span + at + 128] = jnp.sum(value_v, axis=0, keepdims=True)
        grad_proj = out_ref[0]

        @pl.when(step == 0)
        def _():
            for at in range(0, width, tile):
                full[at : at + tile, :] = mul(x_all[step, :, at : at + tile], grad_proj, TN)

        @pl.when(step > 0)
        def _():
            for at in range(0, width, tile):
                full[at : at + tile, :] += mul(x_all[step, :, at : at + tile], grad_proj, TN)

        @pl.when(step == page_count - 1)
        def _():
            low = page % 2
            for k in range(pages // 2):
                keep[k] = full[pl.ds(pl.multiple_of((2 * k + low) * block, block), block), :]
                start = pl.multiple_of((2 * k + 1 - low) * block, block)
                send[k] = full[pl.ds(start, block), :].astype(LOW)

    def per_page(shape):
        zeros = (0,) * len(shape)
        return pl.BlockSpec((1,) + shape, lambda i: (i,) + zeros)

    flops = page_count * (20 * heads * slots * slots * depth + 2 * slots * width * triple)
    return pl.pallas_call(
        body,
        grid=(page_count,),
        out_shape=[
            shaped((page_count, slots, triple), LOW),
            shaped((page_count, 8, 2 * span), WIDE),
            shaped((page_count, 8, 128), WIDE),
            shaped((pages // 2, block, triple), WIDE),
            shaped((pages // 2, block, triple), LOW),
        ],
        in_specs=[scalars(), scalars(), per_page((slots, triple)), per_page((slots, 128))]
        + [remote()] * (2 * seqs)
        + [per_page((slots, 1)), per_page((1, slots)), per_page((1, slots))],
        out_specs=[
            per_page((slots, triple)),
            per_page((8, 2 * span)),
            per_page((8, 128)),
            fixed((pages // 2, block, triple)),
            fixed((pages // 2, block, triple)),
        ],
        scratch_shapes=[
            pltpu.VMEM((width, triple), WIDE),
            pltpu.VMEM((page_count, slots, width), LOW),
            pltpu.VMEM((page_count, slots, span), LOW),
            pltpu.SemaphoreType.DMA((2 * seqs,)),
        ],
        compiler_params=params(28),
        cost_estimate=cost(flops, 10 << 20, page_count * heads * slots * slots),
        name="attend_back",
    )(spot, own_bias, *outside([qkv, lse]), *outside(grads), *outside(inputs), column, row, mask)


def page_order(values, rels, page_index):
    pages = len(rels)
    shape = values.shape
    if rels != sorted(rels):
        values = jnp.stack([values[rels.index(rel)] for rel in range(pages)])
    for bit in bits_of(pages):
        folded = values.reshape((pages // (2 * bit), 2, bit) + shape[1:])
        values = jnp.where((page_index // bit) % 2 == 0, folded, folded[:, ::-1])
    return values.reshape(shape)


def assemble_mix(near_blocks, rels, spot, rows, width):
    seqs = len(near_blocks)
    span = near_blocks[0].shape[2]
    if rows % 16:
        ordered = reorder([array.reshape(len(rels), -1, rows, span) for array in near_blocks], spot[1])
        ordered = jnp.stack([array.transpose(0, 2, 1, 3).reshape(len(rels), rows, width) for array in ordered], axis=1)
        return page_order(ordered, rels, spot[0]).reshape(width, width)

    def body(spot_ref, *refs):
        out = refs[-1]
        page, seq = spot_ref[0], spot_ref[1]
        for r in range(seqs):
            for k, rel in enumerate(rels):
                start = pl.multiple_of(((page ^ rel) * seqs + (seq ^ r)) * rows, rows)
                for t in range(width // span):
                    out[pl.ds(start, rows), t * span : (t + 1) * span] = refs[r][k, t * rows : (t + 1) * rows, :]

    return pl.pallas_call(
        body,
        out_shape=kept((width, width), LOW),
        in_specs=[scalars()] + [near()] * seqs,
        out_specs=near(),
        compiler_params=params(8),
        cost_estimate=cost(0, 4 * width * width),
        name="assemble_mix",
    )(spot, *inside(near_blocks))


def mix(spot, contexts, w_mix, inputs, vectors):
    flat, width = inputs.shape
    seqs = len(contexts)
    span = width // seqs

    def body(spot_ref, *refs):
        c_refs = refs[:seqs]
        w_ref, x_ref, vec_ref, wide_ref, low_ref, hat_ref, rstd_ref, c_all, x_here, sems = refs[seqs:]
        copies = bring([(c_refs[0], c_all), (x_ref, x_here)], sems)
        for copy in copies:
            copy.wait()
        total = x_here[...].astype(WIDE) + vec_ref[2:3, :]
        for r in range(seqs):
            start = pl.multiple_of((spot_ref[1] ^ r) * span, span)
            total = total + mul((c_refs[r] if r else c_all)[...], w_ref[pl.ds(start, span), :])
        center = total - jnp.mean(total, axis=-1, keepdims=True)
        spread = jnp.mean(center * center, axis=-1, keepdims=True)
        rstd = lax.rsqrt(spread + 1e-05)
        hat = center * rstd
        normed = hat * vec_ref[10:11, :] + vec_ref[4:5, :]
        wide_ref[...] = normed
        low_ref[...] = normed.astype(LOW)
        hat_ref[...] = hat
        rstd_ref[...] = jnp.broadcast_to(rstd, (flat, 128))

    return pl.pallas_call(
        body,
        out_shape=[
            kept((flat, width), WIDE),
            shaped((flat, width), LOW),
            shaped((flat, width), WIDE),
            shaped((flat, 128), WIDE),
        ],
        in_specs=[scalars()] + [remote()] + [near()] * seqs + [remote(), near()],
        out_specs=[near()] * 4,
        scratch_shapes=[
            pltpu.VMEM((flat, span), LOW),
            pltpu.VMEM((flat, width), LOW),
            pltpu.SemaphoreType.DMA((2,)),
        ],
        compiler_params=params(12),
        cost_estimate=cost(2 * flat * width * width, 8 << 20),
        name="mix",
    )(spot, *outside(contexts[:1]), *inside(contexts[1:]), *inside([w_mix]), *outside([inputs]), vectors)


def second_norm(normed, keep, close, far, vectors, cotangent):
    flat, width = normed.shape

    def body(h_ref, k_ref, n_ref, f_ref, vec_ref, cot_ref, out, wide, low, sums, c_here, sems):
        for copy in bring([(cot_ref, c_here)], sems):
            copy.wait()
        total = h_ref[...] + (k_ref[...] + n_ref[...].astype(WIDE) + f_ref[...].astype(WIDE)) + vec_ref[3:4, :]
        center = total - jnp.mean(total, axis=-1, keepdims=True)
        spread = jnp.mean(center * center, axis=-1, keepdims=True)
        rstd = lax.rsqrt(spread + 1e-05)
        hat = center * rstd
        out[...] = (hat * vec_ref[11:12, :] + vec_ref[5:6, :]).astype(LOW)
        cot = c_here[...].astype(WIDE)
        slope = cot * vec_ref[11:12, :]
        first = jnp.mean(slope, axis=-1, keepdims=True)
        second = jnp.mean(slope * hat, axis=-1, keepdims=True)
        grad = rstd * (slope - first - hat * second)
        wide[...] = grad
        low[...] = grad.astype(LOW)
        sums[0:1, :] = jnp.sum(cot * hat, axis=0, keepdims=True)
        sums[1:2, :] = jnp.sum(cot, axis=0, keepdims=True)
        sums[2:3, :] = jnp.sum(grad, axis=0, keepdims=True)

    return pl.pallas_call(
        body,
        out_shape=[
            shaped((flat, width), LOW),
            shaped((flat, width), WIDE),
            shaped((flat, width), LOW),
            shaped((8, width), WIDE),
        ],
        in_specs=[near()] * 5 + [remote()],
        out_specs=[near()] * 4,
        scratch_shapes=[pltpu.VMEM((flat, width), LOW), pltpu.SemaphoreType.DMA((1,))],
        compiler_params=params(12),
        cost_estimate=cost(flat * width * 30, 7 << 20),
        name="second_norm",
    )(*inside([normed]), keep, *inside([close, far]), vectors, *outside([cotangent]))


def first_norm_back(spot, grad_second, keep, close, far, hat, rstd, vectors, w_mix, contexts, pages):
    flat, width = grad_second.shape
    seqs = len(contexts)
    span = width // seqs
    rows = width // (pages * seqs)
    with_mix = rows % 16 == 0

    def body(spot_ref, d_ref, k_ref, n_ref, f_ref, hat_ref, rstd_ref, vec_ref, w_ref, *refs):
        c_refs, (wide, low, sums) = refs[:seqs], refs[seqs : seqs + 3]
        outs, rest = refs[seqs + 3 : 2 * seqs + 3], refs[2 * seqs + 3 :]
        if with_mix:
            mix_keep, mix_send, c_here, hat_here, d_here, n_here, f_here, full, sems = rest
        else:
            c_here, hat_here, d_here, n_here, f_here, full, sems = rest
        pairs = [(d_ref, d_here), (n_ref, n_here), (f_ref, f_here), (hat_ref, hat_here)]
        copies = bring(pairs + [(c_refs[r], c_here.at[r]) for r in range(seqs)], sems)
        for copy in copies[:4]:
            copy.wait()
        grad = d_here[...] + (k_ref[...] + n_here[...].astype(WIDE) + f_here[...].astype(WIDE))
        hat = hat_here[...]
        slope = grad * vec_ref[10:11, :]
        first = jnp.mean(slope, axis=-1, keepdims=True)
        second = jnp.mean(slope * hat, axis=-1, keepdims=True)
        result = rstd_ref[:, 0:1] * (slope - first - hat * second)
        wide[...] = result
        result_low = result.astype(LOW)
        low[...] = result_low
        for r in range(seqs):
            start = pl.multiple_of((spot_ref[1] ^ r) * span, span)
            outs[r][...] = mul(result_low, w_ref[pl.ds(start, span), :], NT).astype(LOW)
        sums[0:1, :] = jnp.sum(grad * hat, axis=0, keepdims=True)
        sums[1:2, :] = jnp.sum(grad, axis=0, keepdims=True)
        sums[2:3, :] = jnp.sum(result, axis=0, keepdims=True)
        for copy in copies[4:]:
            copy.wait()
        if with_mix:
            for r in range(seqs):
                start = pl.multiple_of((spot_ref[1] ^ r) * span, span)
                full[pl.ds(start, span), :] = mul(c_here[r], result_low, TN)
            bit = spot_ref[1] % 2
            for p in range(pages):
                for k in range(seqs // 2):
                    start = pl.multiple_of((p * seqs + 2 * k + bit) * rows, rows)
                    mix_keep[p, k] = full[pl.ds(start, rows), :]
                    start = pl.multiple_of((p * seqs + 2 * k + 1 - bit) * rows, rows)
                    mix_send[p, k] = full[pl.ds(start, rows), :].astype(LOW)

    mix_shape = (pages, seqs // 2, rows, width)
    return pl.pallas_call(
        body,
        out_shape=[
            shaped((flat, width), WIDE),
            shaped((flat, width), LOW),
            shaped((8, width), WIDE),
        ]
        + [shaped((flat, span), LOW)] * seqs
        + ([shaped(mix_shape, WIDE), shaped(mix_shape, LOW)] if with_mix else []),
        in_specs=[scalars(), remote(), near(), remote(), remote(), remote()] + [near()] * 3 + [remote()] * seqs,
        out_specs=[near()] * (3 + seqs + 2 * with_mix),
        scratch_shapes=[
            pltpu.VMEM((seqs, flat, span), LOW),
            pltpu.VMEM((flat, width), WIDE),
            pltpu.VMEM((flat, width), WIDE),
            pltpu.VMEM((flat, width), LOW),
            pltpu.VMEM((flat, width), LOW),
            pltpu.VMEM((width, width), WIDE),
            pltpu.SemaphoreType.DMA((4 + seqs,)),
        ],
        compiler_params=params(20),
        cost_estimate=cost(2 * flat * width * width, 8 << 20),
        name="first_norm_back",
    )(
        spot,
        *outside([grad_second]),
        keep,
        *outside([close, far]),
        *outside([hat, rstd]),
        vectors,
        *inside([w_mix]),
        *outside(contexts),
    )


def weight_grad(spot, lefts, rights, pages, split, base=None):
    count = len(lefts)
    tokens, height = lefts[0].shape
    width = rights[0].shape[1]
    rows = height // pages
    tile = 256 if height % 256 == 0 else height

    def body(spot_ref, *refs):
        left, right = refs[:count], refs[count : 2 * count]
        base_ref = refs[2 * count] if base is not None else None
        outs = refs[2 * count + (base is not None) : -5]
        full, l_all, r_all, base_here, sems = refs[-5:]
        page = spot_ref[0]
        pairs = []
        for k in range(count):
            pairs.append((left[k], l_all.at[pl.ds(k * tokens, tokens), :]))
            pairs.append((right[k], r_all.at[pl.ds(k * tokens, tokens), :]))
        copies = bring(pairs + ([(base_ref, base_here)] if base is not None else []), sems)
        for copy in copies:
            copy.wait()
        for at in range(0, height, tile):
            value = mul(l_all[:, at : at + tile], r_all[...], TN)
            if base is not None:
                value = value + base_here[at : at + tile, :]
            if split:
                full[at : at + tile, :] = value
            else:
                outs[0][at : at + tile, :] = value.astype(outs[0].dtype)
        if split:
            low = page % 2
            for k in range(pages // 2):
                outs[0][k] = full[pl.ds(pl.multiple_of((2 * k + low) * rows, rows), rows), :]
                start = pl.multiple_of((2 * k + 1 - low) * rows, rows)
                outs[1][k] = full[pl.ds(start, rows), :].astype(LOW)

    if split:
        outs = [shaped((pages // 2, rows, width), WIDE), shaped((pages // 2, rows, width), LOW)]
    else:
        outs = [shaped((height, width), WIDE if base is None else LOW)]
    return pl.pallas_call(
        body,
        out_shape=outs,
        in_specs=[scalars()] + [remote()] * (2 * count) + [remote()] * (base is not None),
        out_specs=[near()] * len(outs),
        scratch_shapes=[
            pltpu.VMEM((height, width) if split else (8, 128), WIDE),
            pltpu.VMEM((count * tokens, height), LOW),
            pltpu.VMEM((count * tokens, width), LOW),
            pltpu.VMEM((height, width) if base is not None else (8, 128), WIDE),
            pltpu.SemaphoreType.DMA((2 * count + 1,)),
        ],
        compiler_params=params(22),
        cost_estimate=cost(2 * count * tokens * height * width, 8 << 20),
        name="weight_grad",
    )(spot, *outside(lefts), *outside(rights), *(outside([base]) if base is not None else []))


def weight_grad_pair(first, base, second):
    count = len(first)
    tokens, height = first[0][0].shape
    width = first[0][1].shape[1]
    tile = 256 if height % 256 == 0 else height

    def body(*refs):
        base_ref, out, wide, l_one, r_one, l_two, r_two, base_here, sems = refs[4 * count :]
        pairs = []
        for k in range(count):
            at = pl.ds(k * tokens, tokens)
            pairs += [(refs[2 * k], l_one.at[at, :]), (refs[2 * k + 1], r_one.at[at, :])]
        for k in range(count):
            at = pl.ds(k * tokens, tokens)
            pairs += [(refs[2 * count + 2 * k], l_two.at[at, :]), (refs[2 * count + 2 * k + 1], r_two.at[at, :])]
        pairs.insert(2 * count, (base_ref, base_here))
        copies = bring(pairs, sems)
        for copy in copies[: 2 * count + 1]:
            copy.wait()
        for at in range(0, height, tile):
            value = mul(l_one[:, at : at + tile], r_one[...], TN) + base_here[at : at + tile, :]
            out[at : at + tile, :] = value.astype(LOW)
        for copy in copies[2 * count + 1 :]:
            copy.wait()
        for at in range(0, height, tile):
            wide[at : at + tile, :] = mul(l_two[:, at : at + tile], r_two[...], TN)

    flat = [array for pair in first + second for array in pair]
    return pl.pallas_call(
        body,
        out_shape=[shaped((height, width), LOW), shaped((height, width), WIDE)],
        in_specs=[remote()] * (4 * count + 1),
        out_specs=[near()] * 2,
        scratch_shapes=[pltpu.VMEM((count * tokens, height), LOW), pltpu.VMEM((count * tokens, width), LOW)] * 2
        + [pltpu.VMEM((height, width), WIDE), pltpu.SemaphoreType.DMA((4 * count + 1,))],
        compiler_params=params(20),
        cost_estimate=cost(4 * count * tokens * height * width, 12 << 20),
        name="weight_grad_pair",
    )(*outside(flat), *outside([base]))


def pack_small(spot, sums_proj, cells_grad, sums_one, sums_two, hidden_sum, pages, seqs):
    width = sums_one.shape[1]
    span = sums_proj.shape[2] // 2
    hidden = hidden_sum.shape[1] // pages
    owners = pages * seqs
    lanes = width // owners

    def body(spot_ref, proj_ref, cell_ref, one_ref, two_ref, hid_ref, out, rows):
        seq = spot_ref[1]
        rows[...] = jnp.zeros_like(rows)
        proj = jnp.sum(proj_ref[:, 0, :], axis=0, keepdims=True)
        at = pl.multiple_of(seq * span, span)
        rows[0:1, pl.ds(at, span)] = proj[:, :span]
        rows[1:2, pl.ds(at, span)] = proj[:, span:]
        for row, ref, k in ((2, one_ref, 2), (3, two_ref, 2), (4, one_ref, 1), (5, two_ref, 1), (10, one_ref, 0), (11, two_ref, 0)):
            rows[row : row + 1, :] = ref[k : k + 1, :]
        for p in range(pages):
            first = p * seqs * hidden
            at = pl.multiple_of(first % width + seq * hidden, hidden)
            row = 6 + first // width
            rows[row : row + 1, pl.ds(at, hidden)] = hid_ref[0:1, p * hidden : (p + 1) * hidden]
        cell = jnp.sum(cell_ref[:, 0, :], axis=0, keepdims=True)
        for o in range(owners):
            out[o] = rows[:, o * lanes : (o + 1) * lanes]
            out[o, 12:13, :] = cell[:, :lanes]

    return pl.pallas_call(
        body,
        out_shape=shaped((owners, 16, lanes), WIDE),
        in_specs=[scalars()] + [near()] * 5,
        out_specs=near(),
        scratch_shapes=[pltpu.VMEM((16, width), WIDE)],
        compiler_params=params(6),
        cost_estimate=cost(32 * width, 1 << 20),
        name="pack_small",
    )(spot, sums_proj, cells_grad, sums_one, sums_two, hidden_sum)


def add_wide(keep, got):
    def body(keep_ref, got_ref, out_ref):
        out_ref[...] = keep_ref[...].astype(WIDE) + got_ref[...].astype(WIDE)

    return pl.pallas_call(
        body,
        out_shape=shaped(keep.shape, WIDE),
        in_specs=[near(), near()],
        out_specs=near(),
        compiler_params=params(4),
        cost_estimate=cost(keep.size, 8 * keep.size),
        name="add_wide",
    )(keep, got)


def input_grad(grad_proj, w_proj, seqs):
    page_count, slots, triple = grad_proj.shape
    width = w_proj.shape[0]
    rows = slots // seqs

    def body(d_ref, w_ref, *outs):
        for rel in range(seqs):
            value = mul(d_ref[0, rel * rows : (rel + 1) * rows, :], w_ref[...], NT)
            outs[rel][0] = value.astype(outs[rel].dtype)

    per = pl.BlockSpec((1, rows, width), lambda i: (i, 0, 0))
    return pl.pallas_call(
        body,
        grid=(page_count,),
        out_shape=[shaped((page_count, rows, width), WIDE if rel % 2 == 0 else LOW) for rel in range(seqs)],
        in_specs=[pl.BlockSpec((1, slots, triple), lambda i: (i, 0, 0)), fixed(w_proj.shape)],
        out_specs=[per] * seqs,
        compiler_params=params(14),
        cost_estimate=cost(2 * page_count * slots * triple * width, 8 << 20),
        name="input_grad",
    )(*outside([grad_proj, w_proj]))


def local(counts, tokens, cells, lengths, cotangent, w_qkv, w_out, w_up, w_down, biases, gains, cell_bias):
    pages, seqs = counts
    page_count, row_count, width = tokens.shape
    slots = row_count * seqs
    heads = cell_bias.shape[0]
    depth = width // heads
    heads_here = heads // seqs
    span = heads_here * depth
    flat = page_count * row_count
    rows = w_qkv.shape[0]
    ff_rows = w_down.shape[0]
    ff_here = ff_rows * pages
    page_index = lax.axis_index("page")
    seq_index = lax.axis_index("seq")
    spot = jnp.stack([page_index, seq_index]).astype(jnp.int32)
    low_page = bits_of(pages)
    low_seq = bits_of(seqs)

    def scatter_near(keeps, sends):
        near_parts = [swap(send, "seq", seqs, 1) for send in sends]
        *result, sent = scatter_far_sent(keeps, near_parts)
        return (*result, sent)

    def scatter_far(keeps, nears):
        return scatter_far_sent(keeps, nears)[:3]

    def scatter_far_sent(totals, nears):
        far = jnp.zeros_like(nears[0])
        mask = 2
        while mask < seqs:
            half = [k for k in range(len(totals)) if (k * 2) & mask]
            ready = [(totals[k] + nears[k].astype(WIDE)).astype(LOW) for k in half]
            moved = [swap(value, "seq", seqs, mask) for value in ready]
            rest = [k for k in range(len(totals)) if not (k * 2) & mask]
            if mask * 2 >= seqs:
                far = moved[0]
                totals, nears = [totals[0]], [nears[0]]
            else:
                totals = [totals[k] + nears[k].astype(WIDE) for k in rest]
                nears = moved
            mask *= 2
        return totals[0], nears[0], far, ready[0]

    groups = [[page for page in range(pages) if page % 2 == low] for low in range(2)]

    def halved(keep, *got):
        got = jnp.concatenate(got, axis=1) if len(got) > 1 else got[0]
        return (keep + got.astype(WIDE)).astype(LOW).reshape(-1, keep.shape[-1])

    def scatter_same(values):
        return lax.psum_scatter(values, "page", scatter_dimension=0, tiled=True, axis_index_groups=groups)

    def split_low(values):
        values = values.reshape(2, -1, values.shape[-1])
        low = page_index % 2
        mine = lax.dynamic_index_in_dim(values, low, 0, keepdims=False)
        return mine, swap(lax.dynamic_index_in_dim(values, 1 - low, 0, keepdims=False), "page", pages, 1)

    def small_table(sums_proj, cells_grad):
        owners = pages * seqs
        here = lax.broadcasted_iota(jnp.int32, (seqs, 1, 1), 0) == seq_index
        sums_proj = jnp.sum(sums_proj[:, 0], axis=0).reshape(2, 1, pages, lanes)

        def own(vector):
            return jnp.where(here, vector, 0.0).reshape(owners, 1, lanes)

        hidden_sum = functools.reduce(jnp.add, totals).reshape(pages, 1, ff_rows)
        hidden_sum = jnp.where(here.reshape(1, seqs, 1), hidden_sum, 0.0)
        hidden_sum = hidden_sum.reshape(-1, owners, lanes).transpose(1, 0, 2)
        cells_grad = jnp.sum(cells_grad[:, 0, :heads_here], axis=0)[None]
        cells_grad = jnp.where(here[:, 0], cells_grad, 0.0).reshape(heads)
        cells_grad = jnp.pad(cells_grad, (0, -heads % lanes)).reshape(1, -1, lanes)

        def row_of(sums, k):
            return sums[k].reshape(owners, 1, lanes)

        return to_all(
            jnp.concatenate(
                [
                    own(sums_proj[0]),
                    own(sums_proj[1]),
                    row_of(sums_one, 2),
                    row_of(sums_two, 2),
                    row_of(sums_one, 1),
                    row_of(sums_two, 1),
                    hidden_sum,
                    row_of(sums_one, 0),
                    row_of(sums_two, 0),
                    jnp.broadcast_to(cells_grad, (owners,) + cells_grad.shape[1:]),
                ],
                axis=1,
            )
        )

    def block_rows(values):
        return values.reshape(values.shape[0], -1, span)

    small = jnp.concatenate([biases, gains], axis=0).astype(LOW)
    small_rows, lanes = small.shape
    digits = jnp.concatenate([cells // 16, cells % 16], axis=0).astype(LOW)
    extra = jnp.concatenate(
        [jnp.pad(small, ((0, 0), (0, span - lanes))), jnp.pad(digits, ((0, 0), (0, span - row_count)))], axis=0
    )
    part_qkv = w_qkv.astype(LOW).reshape(rows, 3, seqs, span).transpose(2, 1, 0, 3)
    part_up = w_up.astype(LOW).reshape(rows, pages, seqs, ff_rows).transpose(2, 0, 1, 3)
    sent = jnp.concatenate(
        [
            part_qkv.reshape(seqs, 3 * rows, span),
            jnp.broadcast_to(extra, (seqs,) + extra.shape),
            part_up.reshape(seqs, pages * rows * ff_rows // span, span),
        ],
        axis=1,
    )
    turned = jnp.stack(reorder(turn(sent, seqs, seq_index), seq_index))
    part_qkv = turned[:, : 3 * rows].reshape(seqs, 3, rows, span).transpose(1, 0, 2, 3)
    extras = turned[:, 3 * rows : 3 * rows + extra.shape[0]]
    part_up = turned[:, 3 * rows + extra.shape[0] :].reshape(seqs * rows, ff_here)
    digits = extras[:, small_rows : small_rows + 2 * page_count, :row_count].astype(jnp.int32)
    cells_all = digits[:, :page_count] * 16 + digits[:, page_count:]
    cells_all = jnp.stack(reorder([cells_all[k] for k in range(seqs)], seq_index), axis=1)
    cells_all = cells_all.reshape(page_count, slots)

    part_mix = w_out.astype(LOW).reshape(rows, width // span, span).transpose(1, 0, 2)
    part_small = extras[:, :small_rows, :lanes].transpose(1, 0, 2).reshape(small_rows, seqs * lanes)
    part_small = jnp.pad(part_small, ((0, -small_rows % 16), (0, span - seqs * lanes)))
    block = seqs * rows
    part_both = jnp.concatenate(
        [part_qkv.reshape(3 * block, span), part_mix.reshape(-1, span), part_small], axis=0
    )
    split = low_page[1:3][::-1]
    stack, rels = part_both[None], [0]
    for bit in low_page[:0:-1][: len(low_page) - 1 - len(split)]:
        stack = jnp.concatenate([stack, swap(stack, "page", pages, bit)], axis=0)
        rels = rels + [rel | bit for rel in rels]
    jumps = [0]
    for bit in split:
        jumps = jumps + [jump | bit for jump in jumps]
    across = [swap(stack, "page", pages, jump) for jump in jumps[1:]]
    beside = [swap(stack, "page", pages, 1)]
    x_near = [tokens]
    x_far = swap(after(tokens, part_both), "seq", seqs, low_seq[-1])
    *across, part_up, first_beside, x_far, w_down_low, x_own = fence(
        *across, part_up, beside[0], x_far, w_down.astype(LOW), tokens
    )
    beside = [first_beside] + [swap(array, "page", pages, 1) for array in across]
    both_pieces = [(array, [rel ^ jump for rel in rels]) for array, jump in zip([stack] + across, jumps)]
    both_pieces += [(array, [rel ^ jump ^ 1 for rel in rels]) for array, jump in zip(beside, jumps)]
    inputs = {0: x_own, low_seq[-1]: x_far}
    for bit in low_seq[:-1][::-1]:
        for rel in list(inputs):
            inputs[rel | bit] = swap(inputs[rel], "seq", seqs, bit)
    inputs = [inputs[rel] for rel in range(seqs)]
    feed_both = lax.all_gather(jnp.concatenate([part_up, w_down_low], axis=0), "page", axis=0, tiled=False)
    w_expand = feed_both[:, :block].reshape(width, ff_here)
    w_reduce = feed_both[:, block:].reshape(ff_here, width)
    fenced = fence(*[array for array, _ in both_pieces], *inputs)
    inputs = list(fenced[len(both_pieces) :])
    both_pieces = [(array, rel) for array, (_, rel) in zip(fenced[: len(both_pieces)], both_pieces)]
    both_rels = [rel for _, rel_list in both_pieces for rel in rel_list]
    vectors = jnp.concatenate([array[:, 4 * block :, :] for array, _ in both_pieces], axis=0)
    vectors = page_order(vectors[:, :small_rows, : seqs * lanes], both_rels, page_index)
    vectors = vectors.reshape(pages, small_rows, seqs * lanes).transpose(1, 0, 2)
    vectors = vectors.reshape(small_rows, width).astype(WIDE)
    hidden_bias = vectors[6:10].reshape(pages, seqs, ff_rows)
    hidden_bias = lax.dynamic_index_in_dim(hidden_bias, seq_index, 1, keepdims=False).reshape(1, ff_here)

    position = lax.broadcasted_iota(jnp.int32, (1, slots), 1)
    position = ((position // row_count) ^ seq_index) * row_count + position % row_count
    mask = jnp.where(position < lengths[:, None], 0.0, -1e30).astype(WIDE)[:, None, :]
    column, row = cells_all[:, :, None], cells_all[:, None, :]
    own_bias = lax.dynamic_slice_in_dim(cell_bias, seq_index * heads_here, heads_here)
    mix_part = jnp.concatenate([array[:, 3 * block : 4 * block, :] for array, _ in both_pieces], axis=0)
    mix_far = swap(mix_part, "seq", seqs, low_seq[-1])
    qkv, lse, w_proj, *contexts = attend(
        [(after(array, mix_part), rel_list) for array, rel_list in both_pieces],
        block,
        spot,
        own_bias,
        inputs,
        vectors,
        column,
        row,
        mask,
        heads_here,
        depth,
    )
    mix_part, mix_far, qkv, lse, w_proj, *contexts = fence(mix_part, mix_far, qkv, lse, w_proj, *contexts)
    mix_near = {0: mix_part, low_seq[-1]: mix_far}
    for bit in low_seq[:-1][::-1]:
        for rel in list(mix_near):
            mix_near[rel | bit] = swap(mix_near[rel], "seq", seqs, bit)
    contexts = exchange([context.reshape(flat, span) for context in contexts])
    w_mix = assemble_mix([mix_near[rel] for rel in range(seqs)], both_rels, spot, rows, width)

    flat_inputs = tokens.reshape(flat, width)
    normed, normed_low, hat, rstd = mix(spot, contexts, w_mix, flat_inputs, vectors)
    hidden, active, parts = {}, {}, {}

    def feed(rels, *others):
        for rel in rels:
            piece = after(normed_all[rel], *others)
            value = jnp.dot(piece, w_expand, preferred_element_type=WIDE) + hidden_bias
            active[rel] = gelu_exact(value).astype(LOW)
            part = jnp.dot(active[rel], w_reduce, preferred_element_type=WIDE)
            parts[rel] = part.astype(LOW) if rel % 2 else part
            hidden[rel] = value

    normed_all = gather_near(normed_low, seqs)
    feed(range(seqs // 2, seqs))
    far_parts = [swap(parts[rel], "seq", seqs, 1) for rel in range(seqs // 2 + 1, seqs, 2)]
    far_sums = [parts[rel] + part.astype(WIDE) for rel, part in zip(range(seqs // 2, seqs, 2), far_parts)]
    ready = far_sums[0].astype(LOW)
    far = swap(ready, "seq", seqs, seqs // 2)
    feed(range(seqs // 2), ready)
    keep, close = parts[0], swap(parts[1], "seq", seqs, 1)
    slopes = [
        0.5 * (1.0 + lax.erf(u * 0.7071067811865476)) + u * jnp.exp(-0.5 * u * u) * 0.3989422804014327
        for u in after([hidden[rel] for rel in range(seqs)], ready)
    ]
    active = [active[rel] for rel in range(seqs)]
    far, slopes = lax.optimization_barrier((far, slopes))
    output, grad_second, second_low, sums_two = second_norm(
        normed, keep, close, far, vectors, cotangent.reshape(flat, width)
    )

    expanded, parts, totals = [], [], []

    def feed_back(pieces):
        for piece in pieces:
            slope = slopes[len(parts)]
            value = jnp.einsum("td,fd->tf", piece, w_reduce, preferred_element_type=WIDE) * slope
            low = value.astype(LOW)
            part = jnp.einsum("tf,df->td", low, w_expand, preferred_element_type=WIDE)
            part = part.astype(LOW) if len(parts) % 2 else part
            expanded.append(low)
            totals.append(jnp.sum(value, axis=0))
            parts.append(part)
        if len(parts) == len(pieces):
            bases.extend(weight_grad(spot, active[: len(pieces)], pieces, pages, False))
        return tuple(parts + bases)

    bases = []
    second_all = gather_near(second_low, seqs, feed_back)
    feed_back(second_all[seqs // 2 :])
    keep, close, far, ready = scatter_near(parts[0::2], parts[1::2])
    half = seqs // 2
    if ff_here == width:
        first = list(zip(after(active[half:], ready, close), second_all[half:]))
        down_part, up_base = weight_grad_pair(first, bases[0], list(zip(normed_all[:half], expanded[:half])))
    else:
        down_part = weight_grad(spot, active[half:], second_all[half:], pages, False, bases[0])[0]
        up_base = weight_grad(spot, normed_all[:half], expanded[:half], pages, False)[0]
    far, down_part, up_base = fence(far, down_part, up_base)
    down_sum = scatter_same(down_part)
    grad_first, first_low, sums_one, *mix_grads = first_norm_back(
        spot, grad_second, keep, close, far, hat, rstd, vectors, w_mix, contexts, pages
    )
    grad_contexts, mix_grads = mix_grads[:seqs], mix_grads[seqs:]
    up_keep, up_send = weight_grad(
        spot, after(normed_all[half:], first_low), expanded[half:], pages, True, up_base
    )
    grad_contexts = exchange(grad_contexts)
    if mix_grads:
        mix_keep, mix_send = mix_grads
        mix_parts = swap(mix_send, "seq", seqs, 1)
    else:
        context = jnp.concatenate(reorder(contexts, seq_index), axis=1)
        grad_mix = jnp.einsum("tc,td->cd", context, first_low, preferred_element_type=WIDE)
        mix_keep, mix_parts = scatter_start(grad_mix.reshape(pages, seqs, rows, width), "seq", seqs, 1, 1)
    mix_keep, mix_parts, *others = fence(mix_keep, mix_parts, *grad_contexts, up_send)
    grad_contexts, up_send = others[:seqs], others[seqs]
    up_got = scatter_first(up_send, pages)
    mix_total = (mix_keep + mix_parts.astype(WIDE)).reshape(pages, seqs // 2, rows, width)
    mix_keep, mix_parts = scatter_start(mix_total, "seq", seqs, 1, low_seq[1])
    grad_contexts = [grad.reshape(page_count, row_count, span) for grad in grad_contexts]
    grad_proj, sums_proj, cells_grad, proj_keep, proj_send = attend_back(
        spot, own_bias, qkv, lse, grad_contexts, inputs, column, row, mask, heads_here, depth, pages
    )
    grad_proj, sums_proj, cells_grad, proj_keep, proj_send, up_keep, mix_keep, mix_parts = fence(
        grad_proj, sums_proj, cells_grad, proj_keep, proj_send, up_keep, mix_keep, mix_parts
    )
    proj_got = scatter_first(proj_send, pages)
    up_half = halved(up_keep, after(up_got, down_sum))
    up_sum = scatter_same(up_half)
    parts = input_grad(after(grad_proj, up_half), w_proj, seqs)
    packed = lanes % 32 == 0 and span % 128 == 0 and ff_rows % 128 == 0 and width % (seqs * ff_rows) == 0
    if packed:
        hidden_sum = functools.reduce(jnp.add, totals)[None]
        table = pack_small(
            spot, *after((sums_proj, cells_grad), parts), sums_one, sums_two, hidden_sum, pages, seqs
        )
        small_sums = to_all(table)
    else:
        small_sums = small_table(*after((sums_proj, cells_grad), parts))
    proj_got, proj_keep, mix_keep, mix_parts, small_sums, *parts = fence(
        proj_got, proj_keep, mix_keep, mix_parts, small_sums, *parts
    )
    proj_half = halved(proj_keep, proj_got)
    near_parts = [swap(part, "seq", seqs, 1) for part in after(parts[1::2], proj_half)]
    keep, close, far = scatter_far(parts[0::2], near_parts)
    proj_half = after(proj_half, up_sum)
    proj_sum = scatter_same(proj_half)
    grad_mix = add_wide(after(mix_keep, proj_half), mix_parts).reshape(pages, rows, width)
    up_sum, down_sum = after((up_sum, down_sum), grad_mix)
    mix_keep, mix_parts = scatter_start(grad_mix, "page", pages, 0, 1)
    down_keep, down_got = split_low(down_sum)
    up_rows = turn(up_sum.reshape(seqs, rows, ff_here), seqs, seq_index)
    mix_keep, mix_parts = scatter_start(mix_keep + mix_parts.astype(WIDE), "page", pages, 0, 2)
    grad_reduce = down_keep.astype(WIDE) + down_got.astype(WIDE)
    proj_sum, far, mix_keep, mix_parts, *up_rows = fence(proj_sum, far, mix_keep, mix_parts, *up_rows)
    proj_rows = turn(proj_sum.reshape(seqs, rows, 3 * span), seqs, seq_index)
    grad_expand = jnp.stack(reorder(up_rows, seq_index)).reshape(seqs, rows, pages, ff_rows).transpose(1, 2, 0, 3)
    grad_expand = grad_expand.reshape(rows, seqs * ff_here).astype(WIDE)
    grad_mix = mix_keep + mix_parts.astype(WIDE)
    grad_mix = scatter_bits(grad_mix, "page", pages, 0, low_page[2:]).reshape(rows, width)
    grad_qkv = jnp.stack(reorder(proj_rows, seq_index)).reshape(seqs, rows, 3, span).transpose(1, 2, 0, 3)
    grad_qkv = grad_qkv.reshape(rows, 3 * width).astype(WIDE)
    grad_inputs = grad_first.reshape(page_count, row_count, width) + (
        keep + close.astype(WIDE) + far.astype(WIDE)
    )

    summed = jnp.sum(small_sums, axis=0)
    if packed:
        cell_total = small_sums[:, 12, :heads_here].reshape(pages, seqs, heads_here)
        cell_total = jnp.sum(cell_total, axis=0).reshape(heads)
    else:
        cell_total = summed[12:].reshape(-1)[:heads]
    return (
        output.reshape(page_count, row_count, width),
        grad_inputs,
        grad_qkv,
        grad_mix,
        grad_expand,
        grad_reduce,
        summed[:10],
        summed[10:12],
        cell_total,
    )


def solution(mesh):
    counts = (mesh.shape["page"], mesh.shape["seq"])
    placed = (
        P("page", "seq", None),
        P("page", "seq"),
        P("page"),
        P("page", "seq", None),
        P(("page", "seq"), None),
        P(("page", "seq"), None),
        P(("page", "seq"), None),
        P(("page", "seq"), None),
        P(None, ("page", "seq")),
        P(None, ("page", "seq")),
        P(),
    )

    def step(*args):
        return local(counts, *args)

    return jax.shard_map(
        step,
        mesh=mesh,
        in_specs=placed,
        out_specs=(
            P("page", "seq", None),
            P("page", "seq", None),
            P(("page", "seq"), None),
            P(("page", "seq"), None),
            P(("page", "seq"), None),
            P(("page", "seq"), None),
            P(None, ("page", "seq")),
            P(None, ("page", "seq")),
            P(),
        ),
        check_vma=False,
    )
```

```python
import functools

import jax
import jax.numpy as jnp
from jax import lax
from jax.experimental import pallas as pl
from jax.experimental.pallas import tpu as pltpu
from jax.sharding import PartitionSpec as P

LOW = jnp.bfloat16
WIDE = jnp.float32


def gelu_exact(values):
    return 0.5 * values * (1.0 + lax.erf(values * 0.7071067811865476))


NT = (((1,), (1,)), ((), ()))
TN = (((0,), (0,)), ((), ()))
NN = (((1,), (0,)), ((), ()))
ONCE = pl.Buffered(1)


def mul(left, right, dims=NN):
    return lax.dot_general(left, right, dims, preferred_element_type=WIDE)


def shaped(shape, dtype):
    return pltpu.HBM(shape, dtype)


def kept(shape, dtype):
    return pltpu.VMEM(shape, dtype)


def fixed(shape):
    zeros = (0,) * len(shape)
    return pl.BlockSpec(shape, lambda *_: zeros, pipeline_mode=ONCE)


def scalars():
    return pl.BlockSpec(memory_space=pltpu.SMEM)


def remote():
    return pl.BlockSpec(memory_space=pltpu.HBM)


def outside(values):
    return [pltpu.with_memory_space_constraint(value, pltpu.HBM) for value in values]


def inside(values):
    return [pltpu.with_memory_space_constraint(value, pltpu.VMEM) for value in values]


def near():
    return pl.BlockSpec(memory_space=pltpu.VMEM)


def bring(pairs, sems):
    copies = []
    for source, target in pairs:
        copy = pltpu.make_async_copy(source, target, sems.at[len(copies)])
        copy.start()
        copies.append(copy)
    return copies


def params(megabytes):
    return pltpu.CompilerParams(vmem_limit_bytes=megabytes * 1024 * 1024)


def cost(flops, moved, extra=0):
    return pl.CostEstimate(flops=int(flops), bytes_accessed=int(moved), transcendentals=int(extra))


def swap(values, axis, count, mask):
    return lax.ppermute(values, axis, [(i, i ^ mask) for i in range(count)])


def bits_of(count):
    return [1 << k for k in range(count.bit_length() - 1)]


def gather_near(values, seqs, between=None, wait=()):
    top = bits_of(seqs)[-1]
    far = swap(values, "seq", seqs, top)
    pieces = {0: after(values, *wait) if wait else values}
    for mask in bits_of(top)[::-1]:
        for rel in list(pieces):
            pieces[rel | mask] = swap(pieces[rel], "seq", seqs, mask)
    if between is not None:
        far = after(far, between([pieces[rel] for rel in range(top)]))
    pieces[top] = far
    for mask in bits_of(top)[::-1]:
        for rel in [rel for rel in pieces if rel & top]:
            pieces[rel | mask] = swap(pieces[rel], "seq", seqs, mask)
    return [pieces[rel] for rel in range(seqs)]


def gather_pages(values, pages, hold=None):
    stack, rels = values[None], [0]
    masks = bits_of(pages)[::-1]
    low, high = masks[-1], masks[:-1]
    split = high[-2:]
    for mask in high[:-2]:
        stack = jnp.concatenate([stack, swap(stack, "page", pages, mask)], axis=0)
        rels = rels + [rel | mask for rel in rels]
    found = [(stack, rels)]
    jumps = [0]
    for mask in split:
        jumps = jumps + [jump | mask for jump in jumps]
    for jump in jumps[1:]:
        found.append((swap(stack, "page", pages, jump), [rel ^ jump for rel in rels]))

    def finish(*others):
        first = swap(stack, "page", pages, low)
        more = [(first, [rel ^ low for rel in rels])]
        for array, rels_of in found[1:]:
            array = after(array, first, *others)
            more.append((swap(array, "page", pages, low), [rel ^ low for rel in rels_of]))
        return found + more

    return [array for array, _ in found[1:]], finish


def scatter_first(send, pages):
    return swap(send, "page", pages, 1)


def scatter_rest(keep, got, pages, direct):
    return scatter_last(keep + got.astype(WIDE), pages, 1, direct)


class Sum:
    def __init__(self, total, pages):
        self.pages = pages
        self.total = total
        if pages == 8:
            lows = [self.total[k].astype(LOW) for k in range(1, pages // 2)]
            self.ready = lows[0]
            self.parts = [swap(low, "page", pages, 2 * (k + 1)) for k, low in enumerate(lows)]
        else:
            self.ready = self.total
            self.parts = []

    def arrive(self, *others):
        if self.pages == 8:
            self.parts = [after(part, *others) for part in self.parts]
        else:
            self.parts = []

    def finish(self, *others):
        if self.pages != 8:
            return scatter_last(self.total, self.pages, 1, False)
        final = after(self.total[0], *others)
        for part in self.parts:
            final = final + part.astype(WIDE)
        return final


def scatter_last(total, pages, level, direct):
    left = pages >> level
    mask = 1 << level
    if direct and left == 4:
        lows = [total[k].astype(LOW) for k in range(1, left)]
        parts = [swap(low, "page", pages, 2 * (k + 1)) for k, low in enumerate(lows)]
        final = total[0]
        for part in parts:
            final = final + part.astype(WIDE)
        return final
    while left > 1:
        total = total.reshape((left // 2, 2) + total.shape[1:])
        got = swap(total[:, 1].astype(LOW), "page", pages, mask)
        total = total[:, 0] + got.astype(WIDE)
        left //= 2
        mask *= 2
    return total[0]


def scatter_bits(values, axis, count, dim, order):
    index = lax.axis_index(axis)
    for mask in order:
        shape = values.shape
        values = values.reshape(shape[:dim] + (shape[dim] // 2, 2) + shape[dim + 1 :])
        bit = (index // mask) % 2
        keep = lax.dynamic_index_in_dim(values, bit, dim + 1, keepdims=False)
        send = lax.dynamic_index_in_dim(values, 1 - bit, dim + 1, keepdims=False)
        values = keep.astype(WIDE) + swap(send.astype(LOW), axis, count, mask).astype(WIDE)
    return values


def scatter_start(values, axis, count, dim, mask):
    index = lax.axis_index(axis)
    shape = values.shape
    values = values.reshape(shape[:dim] + (shape[dim] // 2, 2) + shape[dim + 1 :])
    bit = (index // mask) % 2
    keep = lax.dynamic_index_in_dim(values, bit, dim + 1, keepdims=False)
    send = lax.dynamic_index_in_dim(values, 1 - bit, dim + 1, keepdims=False)
    return keep.astype(WIDE), swap(send.astype(LOW), axis, count, mask)


def reorder(pieces, index):
    count = len(pieces)
    out = []
    for k in range(count):
        value = pieces[0]
        for rel in range(1, count):
            value = jnp.where(index ^ k == rel, pieces[rel], value)
        out.append(value)
    return out


def turn(values, seqs, index):
    mine = [lax.dynamic_index_in_dim(values, index ^ rel, 0, keepdims=False) for rel in range(seqs)]
    return [mine[0]] + [swap(mine[rel], "seq", seqs, rel) for rel in range(1, seqs)]


def after(values, *others):
    return lax.optimization_barrier((values, others))[0]


def exchange(pieces):
    seqs = len(pieces)
    return [pieces[0]] + [swap(pieces[rel], "seq", seqs, rel) for rel in range(1, seqs)]


def fence(*values):
    return lax.optimization_barrier(values)


def to_all(values):
    return lax.all_to_all(values, ("page", "seq"), 0, 0)


def head_scores(qkv, h, span, depth, bias, same, mask):
    group = (h * depth) // 128
    lanes = lax.broadcasted_iota(jnp.int32, (1, 128), 1)
    mine = (lanes // depth) == (h % (128 // depth))
    q = qkv[:, group * 128 : group * 128 + 128]
    k = qkv[:, span + group * 128 : span + group * 128 + 128]
    raw = mul(jnp.where(mine, q * 0.125, jnp.zeros_like(q)), k, NT)
    return raw + jnp.where(same, mask + bias, mask), mine, group


def attend(pieces, block, spot, own_bias, inputs, vectors, column, row, mask, heads, depth):
    page_count, rows, width = inputs[0].shape
    seqs = len(inputs)
    slots = seqs * rows
    span = heads * depth
    arrays = [array for array, _ in pieces]
    rels = [rel for _, rel in pieces]
    n_arrays = len(arrays)

    blocks = sum(len(rel) for rel in rels)

    def body(spot_ref, bias_ref, *refs):
        weights = refs[:n_arrays]
        xs = refs[n_arrays : n_arrays + seqs]
        vec_ref, col_ref, row_ref, mask_ref = refs[n_arrays + seqs : n_arrays + seqs + 4]
        qkv_ref, lse_ref, full_ref = refs[n_arrays + seqs + 4 : n_arrays + seqs + 7]
        ctx_refs = refs[n_arrays + seqs + 7 : n_arrays + 2 * seqs + 7]
        x_all, sems = refs[n_arrays + 2 * seqs + 7 :]
        page = spot_ref[0]
        step = pl.program_id(0)

        @pl.when(step == 0)
        def _():
            pairs = [(xs[r], x_all.at[r]) for r in range(seqs)]
            for ref, rel_list in zip(weights, rels):
                for k, rel in enumerate(rel_list):
                    start = pl.multiple_of((page ^ rel) * block, block)
                    for t in range(3):
                        source = ref.at[k, pl.ds(t * block, block), :]
                        pairs.append((source, full_ref.at[pl.ds(start, block), pl.ds(t * span, span)]))
            for copy in bring(pairs, sems):
                copy.wait()

        at_q = pl.multiple_of(spot_ref[1] * span, span)
        row_bias = jnp.concatenate(
            [vec_ref[0:1, pl.ds(at_q, span)], jnp.zeros((1, span), WIDE), vec_ref[1:2, pl.ds(at_q, span)]],
            axis=1,
        )
        for r in range(seqs):
            part = mul(x_all[r, step], full_ref[...]) + row_bias
            qkv_ref[0, r * rows : (r + 1) * rows, :] = part.astype(LOW)
        qkv = qkv_ref[0]
        same = col_ref[0] == row_ref[0]
        key_mask = mask_ref[0]
        lane = lax.broadcasted_iota(jnp.int32, (1, 128), 1)
        lse = jnp.zeros((slots, 128), WIDE)
        context = [None] * (span // 128)
        for h in range(heads):
            scores, mine, group = head_scores(qkv, h, span, depth, bias_ref[h], same, key_mask)
            peak = jnp.max(scores, axis=-1, keepdims=True)
            exponent = jnp.exp(scores - peak)
            total = jnp.sum(exponent, axis=-1, keepdims=True)
            lse = jnp.where(lane == h, peak + jnp.log(total), lse)
            low = (exponent * (1.0 / total)).astype(LOW)
            v = qkv[:, 2 * span + group * 128 : 2 * span + group * 128 + 128]
            out = mul(low, v)
            context[group] = out if context[group] is None else jnp.where(mine, out, context[group])
        lse_ref[0] = lse
        for group, value in enumerate(context):
            value = value.astype(LOW)
            for r in range(seqs):
                ctx_refs[r][0, :, group * 128 : group * 128 + 128] = value[r * rows : (r + 1) * rows]

    def per_page(shape):
        zeros = (0,) * len(shape)
        return pl.BlockSpec((1,) + shape, lambda i: (i,) + zeros)

    flops = page_count * (2 * slots * width * 3 * span + 8 * heads * slots * slots * depth)
    return pl.pallas_call(
        body,
        grid=(page_count,),
        out_shape=[
            shaped((page_count, slots, 3 * span), LOW),
            shaped((page_count, slots, 128), WIDE),
            shaped((width, 3 * span), LOW),
        ]
        + [shaped((page_count, rows, span), LOW)] * seqs,
        in_specs=[scalars(), scalars()]
        + [remote()] * (n_arrays + seqs)
        + [fixed(vectors.shape), per_page((slots, 1)), per_page((1, slots)), per_page((1, slots))],
        out_specs=[per_page((slots, 3 * span)), per_page((slots, 128)), fixed((width, 3 * span))]
        + [per_page((rows, span))] * seqs,
        scratch_shapes=[
            pltpu.VMEM((seqs, page_count, rows, width), LOW),
            pltpu.SemaphoreType.DMA((seqs + 3 * blocks,)),
        ],
        compiler_params=params(24),
        cost_estimate=cost(flops, 10 << 20, page_count * heads * slots * slots),
        name="attend",
    )(spot, own_bias, *outside(arrays), *outside(inputs), vectors, column, row, mask)


def attend_back(spot, own_bias, qkv, lse, grads, inputs, column, row, mask, heads, depth, pages):
    page_count, slots, triple = qkv.shape
    span = triple // 3
    seqs = len(grads)
    rows = slots // seqs
    groups = span // 128
    width = inputs[0].shape[2]
    block = width // pages
    tile = 256 if width % 256 == 0 else width

    def body(spot_ref, bias_ref, qkv_ref, lse_ref, *refs):
        grad_refs, x_refs = refs[:seqs], refs[seqs : 2 * seqs]
        col_ref, row_ref, mask_ref, out_ref, sum_ref, cell_ref, keep, send = refs[2 * seqs : 2 * seqs + 8]
        full, x_all, g_all, sems = refs[2 * seqs + 8 :]
        step = pl.program_id(0)

        @pl.when(step == 0)
        def _():
            pairs = [(grad_refs[r], g_all.at[:, pl.ds(r * rows, rows), :]) for r in range(seqs)]
            pairs += [(x_refs[r], x_all.at[:, pl.ds(r * rows, rows), :]) for r in range(seqs)]
            for copy in bring(pairs, sems):
                copy.wait()

        page = spot_ref[0]
        qkv = qkv_ref[0]
        same = col_ref[0] == row_ref[0]
        key_mask = mask_ref[0]
        lane = lax.broadcasted_iota(jnp.int32, (1, 128), 1)
        sub = lax.broadcasted_iota(jnp.int32, (128, 1), 0)
        lse = lse_ref[0]
        grad = g_all[step]
        cell = jnp.zeros((1, 128), WIDE)
        dq, dk, dv = [None] * groups, [None] * groups, [None] * groups
        for h in range(heads):
            scores, mine, group = head_scores(qkv, h, span, depth, bias_ref[h], same, key_mask)
            mine_sub = (sub // depth) == (h % (128 // depth))
            at = group * 128
            q = qkv[:, at : at + 128]
            k = qkv[:, span + at : span + at + 128]
            v = qkv[:, 2 * span + at : 2 * span + at + 128]
            g = grad[:, at : at + 128]
            weights = jnp.exp(scores - lse[:, h : h + 1])
            slope = mul(jnp.where(mine, g, jnp.zeros_like(g)), v, NT)
            inner = jnp.sum(weights * slope, axis=-1, keepdims=True)
            ds = weights * (slope - inner)
            same_sum = jnp.sum(jnp.where(same, ds, 0.0), axis=0, keepdims=True)
            cell = jnp.where(lane == h, jnp.sum(same_sum, axis=1, keepdims=True), cell)
            ds_low = ds.astype(LOW)
            part_q = mul(ds_low, k)
            part_k = mul(q, ds_low, TN)
            part_v = mul(g, weights.astype(LOW), TN)
            dq[group] = part_q if dq[group] is None else jnp.where(mine, part_q, dq[group])
            dk[group] = part_k if dk[group] is None else jnp.where(mine_sub, part_k, dk[group])
            dv[group] = part_v if dv[group] is None else jnp.where(mine_sub, part_v, dv[group])
        cell_ref[0] = jnp.broadcast_to(cell, (8, 128))
        for group in range(groups):
            at = group * 128
            value_q = dq[group] * 0.125
            value_v = dv[group].T
            out_ref[0, :, at : at + 128] = value_q.astype(LOW)
            out_ref[0, :, span + at : span + at + 128] = (dk[group] * 0.125).T.astype(LOW)
            out_ref[0, :, 2 * span + at : 2 * span + at + 128] = value_v.astype(LOW)
            sum_ref[0, 0:1, at : at + 128] = jnp.sum(value_q, axis=0, keepdims=True)
            sum_ref[0, 0:1, span + at : span + at + 128] = jnp.sum(value_v, axis=0, keepdims=True)
        grad_proj = out_ref[0]

        @pl.when(step == 0)
        def _():
            for at in range(0, width, tile):
                full[at : at + tile, :] = mul(x_all[step, :, at : at + tile], grad_proj, TN)

        @pl.when(step > 0)
        def _():
            for at in range(0, width, tile):
                full[at : at + tile, :] += mul(x_all[step, :, at : at + tile], grad_proj, TN)

        @pl.when(step == page_count - 1)
        def _():
            low = page % 2
            for k in range(pages // 2):
                keep[k] = full[pl.ds(pl.multiple_of((2 * k + low) * block, block), block), :]
                start = pl.multiple_of((2 * k + 1 - low) * block, block)
                send[k] = full[pl.ds(start, block), :].astype(LOW)

    def per_page(shape):
        zeros = (0,) * len(shape)
        return pl.BlockSpec((1,) + shape, lambda i: (i,) + zeros)

    flops = page_count * (20 * heads * slots * slots * depth + 2 * slots * width * triple)
    return pl.pallas_call(
        body,
        grid=(page_count,),
        out_shape=[
            shaped((page_count, slots, triple), LOW),
            shaped((page_count, 8, 2 * span), WIDE),
            shaped((page_count, 8, 128), WIDE),
            shaped((pages // 2, block, triple), WIDE),
            shaped((pages // 2, block, triple), LOW),
        ],
        in_specs=[scalars(), scalars(), per_page((slots, triple)), per_page((slots, 128))]
        + [remote()] * (2 * seqs)
        + [per_page((slots, 1)), per_page((1, slots)), per_page((1, slots))],
        out_specs=[
            per_page((slots, triple)),
            per_page((8, 2 * span)),
            per_page((8, 128)),
            fixed((pages // 2, block, triple)),
            fixed((pages // 2, block, triple)),
        ],
        scratch_shapes=[
            pltpu.VMEM((width, triple), WIDE),
            pltpu.VMEM((page_count, slots, width), LOW),
            pltpu.VMEM((page_count, slots, span), LOW),
            pltpu.SemaphoreType.DMA((2 * seqs,)),
        ],
        compiler_params=params(28),
        cost_estimate=cost(flops, 10 << 20, page_count * heads * slots * slots),
        name="attend_back",
    )(spot, own_bias, *outside([qkv, lse]), *outside(grads), *outside(inputs), column, row, mask)


def page_order(values, rels, page_index):
    pages = len(rels)
    shape = values.shape
    if rels != sorted(rels):
        values = jnp.stack([values[rels.index(rel)] for rel in range(pages)])
    for bit in bits_of(pages):
        folded = values.reshape((pages // (2 * bit), 2, bit) + shape[1:])
        values = jnp.where((page_index // bit) % 2 == 0, folded, folded[:, ::-1])
    return values.reshape(shape)


def assemble_mix(near_blocks, rels, spot, rows, width):
    seqs = len(near_blocks)
    span = near_blocks[0].shape[2]
    if rows % 16:
        ordered = reorder([array.reshape(len(rels), -1, rows, span) for array in near_blocks], spot[1])
        ordered = jnp.stack([array.transpose(0, 2, 1, 3).reshape(len(rels), rows, width) for array in ordered], axis=1)
        return page_order(ordered, rels, spot[0]).reshape(width, width)

    def body(spot_ref, *refs):
        out = refs[-1]
        page, seq = spot_ref[0], spot_ref[1]
        for r in range(seqs):
            for k, rel in enumerate(rels):
                start = pl.multiple_of(((page ^ rel) * seqs + (seq ^ r)) * rows, rows)
                for t in range(width // span):
                    out[pl.ds(start, rows), t * span : (t + 1) * span] = refs[r][k, t * rows : (t + 1) * rows, :]

    return pl.pallas_call(
        body,
        out_shape=kept((width, width), LOW),
        in_specs=[scalars()] + [near()] * seqs,
        out_specs=near(),
        compiler_params=params(8),
        cost_estimate=cost(0, 4 * width * width),
        name="assemble_mix",
    )(spot, *inside(near_blocks))


def mix(spot, contexts, w_mix, inputs, vectors):
    flat, width = inputs.shape
    seqs = len(contexts)
    span = width // seqs

    def body(spot_ref, *refs):
        c_refs = refs[:seqs]
        w_ref, x_ref, vec_ref, wide_ref, low_ref, hat_ref, rstd_ref, c_all, x_here, sems = refs[seqs:]
        copies = bring([(c_refs[0], c_all), (x_ref, x_here)], sems)
        for copy in copies:
            copy.wait()
        total = x_here[...].astype(WIDE) + vec_ref[2:3, :]
        for r in range(seqs):
            start = pl.multiple_of((spot_ref[1] ^ r) * span, span)
            total = total + mul((c_refs[r] if r else c_all)[...], w_ref[pl.ds(start, span), :])
        center = total - jnp.mean(total, axis=-1, keepdims=True)
        spread = jnp.mean(center * center, axis=-1, keepdims=True)
        rstd = lax.rsqrt(spread + 1e-05)
        hat = center * rstd
        normed = hat * vec_ref[10:11, :] + vec_ref[4:5, :]
        wide_ref[...] = normed
        low_ref[...] = normed.astype(LOW)
        hat_ref[...] = hat
        rstd_ref[...] = jnp.broadcast_to(rstd, (flat, 128))

    return pl.pallas_call(
        body,
        out_shape=[
            kept((flat, width), WIDE),
            shaped((flat, width), LOW),
            shaped((flat, width), WIDE),
            shaped((flat, 128), WIDE),
        ],
        in_specs=[scalars()] + [remote()] + [near()] * seqs + [remote(), near()],
        out_specs=[near()] * 4,
        scratch_shapes=[
            pltpu.VMEM((flat, span), LOW),
            pltpu.VMEM((flat, width), LOW),
            pltpu.SemaphoreType.DMA((2,)),
        ],
        compiler_params=params(12),
        cost_estimate=cost(2 * flat * width * width, 8 << 20),
        name="mix",
    )(spot, *outside(contexts[:1]), *inside(contexts[1:]), *inside([w_mix]), *outside([inputs]), vectors)


def second_norm(normed, keep, close, far, vectors, cotangent):
    flat, width = normed.shape

    def body(h_ref, k_ref, n_ref, f_ref, vec_ref, cot_ref, out, wide, low, sums, c_here, sems):
        for copy in bring([(cot_ref, c_here)], sems):
            copy.wait()
        total = h_ref[...] + (k_ref[...] + n_ref[...].astype(WIDE) + f_ref[...].astype(WIDE)) + vec_ref[3:4, :]
        center = total - jnp.mean(total, axis=-1, keepdims=True)
        spread = jnp.mean(center * center, axis=-1, keepdims=True)
        rstd = lax.rsqrt(spread + 1e-05)
        hat = center * rstd
        out[...] = (hat * vec_ref[11:12, :] + vec_ref[5:6, :]).astype(LOW)
        cot = c_here[...].astype(WIDE)
        slope = cot * vec_ref[11:12, :]
        first = jnp.mean(slope, axis=-1, keepdims=True)
        second = jnp.mean(slope * hat, axis=-1, keepdims=True)
        grad = rstd * (slope - first - hat * second)
        wide[...] = grad
        low[...] = grad.astype(LOW)
        sums[0:1, :] = jnp.sum(cot * hat, axis=0, keepdims=True)
        sums[1:2, :] = jnp.sum(cot, axis=0, keepdims=True)
        sums[2:3, :] = jnp.sum(grad, axis=0, keepdims=True)

    return pl.pallas_call(
        body,
        out_shape=[
            shaped((flat, width), LOW),
            shaped((flat, width), WIDE),
            shaped((flat, width), LOW),
            shaped((8, width), WIDE),
        ],
        in_specs=[near()] * 5 + [remote()],
        out_specs=[near()] * 4,
        scratch_shapes=[pltpu.VMEM((flat, width), LOW), pltpu.SemaphoreType.DMA((1,))],
        compiler_params=params(12),
        cost_estimate=cost(flat * width * 30, 7 << 20),
        name="second_norm",
    )(*inside([normed]), keep, *inside([close, far]), vectors, *outside([cotangent]))


def first_norm_back(spot, grad_second, keep, close, far, hat, rstd, vectors, w_mix, contexts, pages):
    flat, width = grad_second.shape
    seqs = len(contexts)
    span = width // seqs
    rows = width // (pages * seqs)
    with_mix = rows % 16 == 0

    def body(spot_ref, d_ref, k_ref, n_ref, f_ref, hat_ref, rstd_ref, vec_ref, w_ref, *refs):
        c_refs, (wide, low, sums) = refs[:seqs], refs[seqs : seqs + 3]
        outs, rest = refs[seqs + 3 : 2 * seqs + 3], refs[2 * seqs + 3 :]
        if with_mix:
            mix_keep, mix_send, c_here, hat_here, d_here, n_here, f_here, full, sems = rest
        else:
            c_here, hat_here, d_here, n_here, f_here, full, sems = rest
        pairs = [(d_ref, d_here), (n_ref, n_here), (f_ref, f_here), (hat_ref, hat_here)]
        copies = bring(pairs + [(c_refs[r], c_here.at[r]) for r in range(seqs)], sems)
        for copy in copies[:4]:
            copy.wait()
        grad = d_here[...] + (k_ref[...] + n_here[...].astype(WIDE) + f_here[...].astype(WIDE))
        hat = hat_here[...]
        slope = grad * vec_ref[10:11, :]
        first = jnp.mean(slope, axis=-1, keepdims=True)
        second = jnp.mean(slope * hat, axis=-1, keepdims=True)
        result = rstd_ref[:, 0:1] * (slope - first - hat * second)
        wide[...] = result
        result_low = result.astype(LOW)
        low[...] = result_low
        for r in range(seqs):
            start = pl.multiple_of((spot_ref[1] ^ r) * span, span)
            outs[r][...] = mul(result_low, w_ref[pl.ds(start, span), :], NT).astype(LOW)
        sums[0:1, :] = jnp.sum(grad * hat, axis=0, keepdims=True)
        sums[1:2, :] = jnp.sum(grad, axis=0, keepdims=True)
        sums[2:3, :] = jnp.sum(result, axis=0, keepdims=True)
        for copy in copies[4:]:
            copy.wait()
        if with_mix:
            for r in range(seqs):
                start = pl.multiple_of((spot_ref[1] ^ r) * span, span)
                full[pl.ds(start, span), :] = mul(c_here[r], result_low, TN)
            bit = spot_ref[1] % 2
            for p in range(pages):
                for k in range(seqs // 2):
                    start = pl.multiple_of((p * seqs + 2 * k + bit) * rows, rows)
                    mix_keep[p, k] = full[pl.ds(start, rows), :]
                    start = pl.multiple_of((p * seqs + 2 * k + 1 - bit) * rows, rows)
                    mix_send[p, k] = full[pl.ds(start, rows), :].astype(LOW)

    mix_shape = (pages, seqs // 2, rows, width)
    return pl.pallas_call(
        body,
        out_shape=[
            shaped((flat, width), WIDE),
            shaped((flat, width), LOW),
            shaped((8, width), WIDE),
        ]
        + [shaped((flat, span), LOW)] * seqs
        + ([shaped(mix_shape, WIDE), shaped(mix_shape, LOW)] if with_mix else []),
        in_specs=[scalars(), remote(), near(), remote(), remote(), remote()] + [near()] * 3 + [remote()] * seqs,
        out_specs=[near()] * (3 + seqs + 2 * with_mix),
        scratch_shapes=[
            pltpu.VMEM((seqs, flat, span), LOW),
            pltpu.VMEM((flat, width), WIDE),
            pltpu.VMEM((flat, width), WIDE),
            pltpu.VMEM((flat, width), LOW),
            pltpu.VMEM((flat, width), LOW),
            pltpu.VMEM((width, width), WIDE),
            pltpu.SemaphoreType.DMA((4 + seqs,)),
        ],
        compiler_params=params(20),
        cost_estimate=cost(2 * flat * width * width, 8 << 20),
        name="first_norm_back",
    )(
        spot,
        *outside([grad_second]),
        keep,
        *outside([close, far]),
        *outside([hat, rstd]),
        vectors,
        *inside([w_mix]),
        *outside(contexts),
    )


def weight_grad(spot, lefts, rights, pages, split, base=None):
    count = len(lefts)
    tokens, height = lefts[0].shape
    width = rights[0].shape[1]
    rows = height // pages
    tile = 256 if height % 256 == 0 else height

    def body(spot_ref, *refs):
        left, right = refs[:count], refs[count : 2 * count]
        base_ref = refs[2 * count] if base is not None else None
        outs = refs[2 * count + (base is not None) : -5]
        full, l_all, r_all, base_here, sems = refs[-5:]
        page = spot_ref[0]
        pairs = []
        for k in range(count):
            pairs.append((left[k], l_all.at[pl.ds(k * tokens, tokens), :]))
            pairs.append((right[k], r_all.at[pl.ds(k * tokens, tokens), :]))
        copies = bring(pairs + ([(base_ref, base_here)] if base is not None else []), sems)
        for copy in copies:
            copy.wait()
        for at in range(0, height, tile):
            value = mul(l_all[:, at : at + tile], r_all[...], TN)
            if base is not None:
                value = value + base_here[at : at + tile, :]
            if split:
                full[at : at + tile, :] = value
            else:
                outs[0][at : at + tile, :] = value.astype(outs[0].dtype)
        if split:
            low = page % 2
            for k in range(pages // 2):
                outs[0][k] = full[pl.ds(pl.multiple_of((2 * k + low) * rows, rows), rows), :]
                start = pl.multiple_of((2 * k + 1 - low) * rows, rows)
                outs[1][k] = full[pl.ds(start, rows), :].astype(LOW)

    if split:
        outs = [shaped((pages // 2, rows, width), WIDE), shaped((pages // 2, rows, width), LOW)]
    else:
        outs = [shaped((height, width), WIDE if base is None else LOW)]
    return pl.pallas_call(
        body,
        out_shape=outs,
        in_specs=[scalars()] + [remote()] * (2 * count) + [remote()] * (base is not None),
        out_specs=[near()] * len(outs),
        scratch_shapes=[
            pltpu.VMEM((height, width) if split else (8, 128), WIDE),
            pltpu.VMEM((count * tokens, height), LOW),
            pltpu.VMEM((count * tokens, width), LOW),
            pltpu.VMEM((height, width) if base is not None else (8, 128), WIDE),
            pltpu.SemaphoreType.DMA((2 * count + 1,)),
        ],
        compiler_params=params(22),
        cost_estimate=cost(2 * count * tokens * height * width, 8 << 20),
        name="weight_grad",
    )(spot, *outside(lefts), *outside(rights), *(outside([base]) if base is not None else []))


def weight_grad_pair(spot, first, base, second, pages):
    one, two = len(first), len(second)
    tokens, height = first[0][0].shape
    width = first[0][1].shape[1]
    rows = height // pages
    tile = 256 if height % 256 == 0 else height
    cut = rows * 3 // 8
    cuts = [(0, rows)] if cut % 16 else [(0, cut), (cut, rows)]
    n_sent = len(cuts)

    def body(spot_ref, *refs):
        blocks = refs[: 2 * (one + two)]
        base_ref, out, keep = refs[2 * (one + two) : 2 * (one + two) + 3]
        sends = refs[2 * (one + two) + 3 : 2 * (one + two) + 3 + n_sent]
        l_one, r_one, l_two, r_two, full, sems = refs[2 * (one + two) + 3 + n_sent :]
        pairs = [(base_ref, full)]
        for count, offset, left, right in ((one, 0, l_one, r_one), (two, 2 * one, l_two, r_two)):
            for k in range(count):
                at = pl.ds(k * tokens, tokens)
                pairs += [(blocks[offset + 2 * k], left.at[at, :]), (blocks[offset + 2 * k + 1], right.at[at, :])]
        copies = bring(pairs, sems)
        for copy in copies[: 2 * one + 1]:
            copy.wait()
        for at in range(0, height, tile):
            value = mul(l_one[:, at : at + tile], r_one[...], TN) + full[at : at + tile, :]
            out[at : at + tile, :] = value.astype(LOW)
        for copy in copies[2 * one + 1 :]:
            copy.wait()
        for at in range(0, height, tile):
            full[at : at + tile, :] = mul(l_two[:, at : at + tile], r_two[...], TN)
        low = spot_ref[0] % 2
        for k in range(pages // 2):
            keep[k] = full[pl.ds(pl.multiple_of((2 * k + low) * rows, rows), rows), :]
            start = pl.multiple_of((2 * k + 1 - low) * rows, rows)
            value = full[pl.ds(start, rows), :].astype(LOW)
            for ref, (begin, end) in zip(sends, cuts):
                ref[k] = value[begin:end]

    flat = [array for pair in first + second for array in pair]
    return pl.pallas_call(
        body,
        out_shape=[
            shaped((height, width), LOW),
            shaped((pages // 2, rows, width), WIDE),
        ]
        + [shaped((pages // 2, end - begin, width), LOW) for begin, end in cuts],
        in_specs=[scalars()] + [remote()] * (2 * (one + two) + 1),
        out_specs=[near()] * (2 + n_sent),
        scratch_shapes=[
            pltpu.VMEM((one * tokens, height), LOW),
            pltpu.VMEM((one * tokens, width), LOW),
            pltpu.VMEM((two * tokens, height), LOW),
            pltpu.VMEM((two * tokens, width), LOW),
            pltpu.VMEM((height, width), WIDE),
            pltpu.SemaphoreType.DMA((2 * (one + two) + 1,)),
        ],
        compiler_params=params(26),
        cost_estimate=cost(2 * (one + two) * tokens * height * width, 16 << 20),
        name="weight_grad_pair",
    )(spot, *outside(flat), *outside([base]))


def pack_small(spot, sums_proj, cells_grad, sums_one, sums_two, hidden_sum, pages, seqs):
    width = sums_one.shape[1]
    span = sums_proj.shape[2] // 2
    hidden = hidden_sum.shape[1] // pages
    owners = pages * seqs
    lanes = width // owners

    def body(spot_ref, proj_ref, cell_ref, one_ref, two_ref, hid_ref, out, rows):
        seq = spot_ref[1]
        rows[...] = jnp.zeros_like(rows)
        proj = jnp.sum(proj_ref[:, 0, :], axis=0, keepdims=True)
        at = pl.multiple_of(seq * span, span)
        rows[0:1, pl.ds(at, span)] = proj[:, :span]
        rows[1:2, pl.ds(at, span)] = proj[:, span:]
        for row, ref, k in ((2, one_ref, 2), (3, two_ref, 2), (4, one_ref, 1), (5, two_ref, 1), (10, one_ref, 0), (11, two_ref, 0)):
            rows[row : row + 1, :] = ref[k : k + 1, :]
        for p in range(pages):
            first = p * seqs * hidden
            at = pl.multiple_of(first % width + seq * hidden, hidden)
            row = 6 + first // width
            rows[row : row + 1, pl.ds(at, hidden)] = hid_ref[0:1, p * hidden : (p + 1) * hidden]
        cell = jnp.sum(cell_ref[:, 0, :], axis=0, keepdims=True)
        for o in range(owners):
            out[o] = rows[:, o * lanes : (o + 1) * lanes]
            out[o, 12:13, :] = cell[:, :lanes]

    return pl.pallas_call(
        body,
        out_shape=shaped((owners, 16, lanes), WIDE),
        in_specs=[scalars()] + [near()] * 5,
        out_specs=near(),
        scratch_shapes=[pltpu.VMEM((16, width), WIDE)],
        compiler_params=params(6),
        cost_estimate=cost(32 * width, 1 << 20),
        name="pack_small",
    )(spot, sums_proj, cells_grad, sums_one, sums_two, hidden_sum)


def add_wide(keep, got):
    def body(keep_ref, got_ref, out_ref):
        out_ref[...] = keep_ref[...].astype(WIDE) + got_ref[...].astype(WIDE)

    return pl.pallas_call(
        body,
        out_shape=shaped(keep.shape, WIDE),
        in_specs=[near(), near()],
        out_specs=near(),
        compiler_params=params(4),
        cost_estimate=cost(keep.size, 8 * keep.size),
        name="add_wide",
    )(keep, got)


def input_grad(grad_proj, w_proj, seqs):
    page_count, slots, triple = grad_proj.shape
    width = w_proj.shape[0]
    rows = slots // seqs

    def body(d_ref, w_ref, *outs):
        for rel in range(seqs):
            value = mul(d_ref[0, rel * rows : (rel + 1) * rows, :], w_ref[...], NT)
            outs[rel][0] = value.astype(outs[rel].dtype)

    per = pl.BlockSpec((1, rows, width), lambda i: (i, 0, 0))
    return pl.pallas_call(
        body,
        grid=(page_count,),
        out_shape=[shaped((page_count, rows, width), WIDE if rel % 2 == 0 else LOW) for rel in range(seqs)],
        in_specs=[pl.BlockSpec((1, slots, triple), lambda i: (i, 0, 0)), fixed(w_proj.shape)],
        out_specs=[per] * seqs,
        compiler_params=params(14),
        cost_estimate=cost(2 * page_count * slots * triple * width, 8 << 20),
        name="input_grad",
    )(*outside([grad_proj, w_proj]))


def local(counts, tokens, cells, lengths, cotangent, w_qkv, w_out, w_up, w_down, biases, gains, cell_bias):
    pages, seqs = counts
    page_count, row_count, width = tokens.shape
    slots = row_count * seqs
    heads = cell_bias.shape[0]
    depth = width // heads
    heads_here = heads // seqs
    span = heads_here * depth
    flat = page_count * row_count
    rows = w_qkv.shape[0]
    ff_rows = w_down.shape[0]
    ff_here = ff_rows * pages
    page_index = lax.axis_index("page")
    seq_index = lax.axis_index("seq")
    spot = jnp.stack([page_index, seq_index]).astype(jnp.int32)
    low_page = bits_of(pages)
    low_seq = bits_of(seqs)

    def scatter_near(keeps, sends):
        near_parts = [swap(send, "seq", seqs, 1) for send in sends]
        *result, sent = scatter_far_sent(keeps, near_parts)
        return (*result, sent)

    def scatter_far(keeps, nears):
        return scatter_far_sent(keeps, nears)[:3]

    def scatter_far_sent(totals, nears):
        far = jnp.zeros_like(nears[0])
        mask = 2
        while mask < seqs:
            half = [k for k in range(len(totals)) if (k * 2) & mask]
            ready = [(totals[k] + nears[k].astype(WIDE)).astype(LOW) for k in half]
            moved = [swap(value, "seq", seqs, mask) for value in ready]
            rest = [k for k in range(len(totals)) if not (k * 2) & mask]
            if mask * 2 >= seqs:
                far = moved[0]
                totals, nears = [totals[0]], [nears[0]]
            else:
                totals = [totals[k] + nears[k].astype(WIDE) for k in rest]
                nears = moved
            mask *= 2
        return totals[0], nears[0], far, ready[0]

    groups = [[page for page in range(pages) if page % 2 == low] for low in range(2)]

    def halved(keep, *got):
        got = jnp.concatenate(got, axis=1) if len(got) > 1 else got[0]
        return (keep + got.astype(WIDE)).astype(LOW).reshape(-1, keep.shape[-1])

    def scatter_same(values):
        return lax.psum_scatter(values, "page", scatter_dimension=0, tiled=True, axis_index_groups=groups)

    def split_low(values):
        values = values.reshape(2, -1, values.shape[-1])
        low = page_index % 2
        mine = lax.dynamic_index_in_dim(values, low, 0, keepdims=False)
        return mine, swap(lax.dynamic_index_in_dim(values, 1 - low, 0, keepdims=False), "page", pages, 1)

    def small_table(sums_proj, cells_grad):
        owners = pages * seqs
        here = lax.broadcasted_iota(jnp.int32, (seqs, 1, 1), 0) == seq_index
        sums_proj = jnp.sum(sums_proj[:, 0], axis=0).reshape(2, 1, pages, lanes)

        def own(vector):
            return jnp.where(here, vector, 0.0).reshape(owners, 1, lanes)

        hidden_sum = functools.reduce(jnp.add, totals).reshape(pages, 1, ff_rows)
        hidden_sum = jnp.where(here.reshape(1, seqs, 1), hidden_sum, 0.0)
        hidden_sum = hidden_sum.reshape(-1, owners, lanes).transpose(1, 0, 2)
        cells_grad = jnp.sum(cells_grad[:, 0, :heads_here], axis=0)[None]
        cells_grad = jnp.where(here[:, 0], cells_grad, 0.0).reshape(heads)
        cells_grad = jnp.pad(cells_grad, (0, -heads % lanes)).reshape(1, -1, lanes)

        def row_of(sums, k):
            return sums[k].reshape(owners, 1, lanes)

        return to_all(
            jnp.concatenate(
                [
                    own(sums_proj[0]),
                    own(sums_proj[1]),
                    row_of(sums_one, 2),
                    row_of(sums_two, 2),
                    row_of(sums_one, 1),
                    row_of(sums_two, 1),
                    hidden_sum,
                    row_of(sums_one, 0),
                    row_of(sums_two, 0),
                    jnp.broadcast_to(cells_grad, (owners,) + cells_grad.shape[1:]),
                ],
                axis=1,
            )
        )

    def block_rows(values):
        return values.reshape(values.shape[0], -1, span)

    small = jnp.concatenate([biases, gains], axis=0).astype(LOW)
    small_rows, lanes = small.shape
    digits = jnp.concatenate([cells // 16, cells % 16], axis=0).astype(LOW)
    extra = jnp.concatenate(
        [jnp.pad(small, ((0, 0), (0, span - lanes))), jnp.pad(digits, ((0, 0), (0, span - row_count)))], axis=0
    )
    part_qkv = w_qkv.astype(LOW).reshape(rows, 3, seqs, span).transpose(2, 1, 0, 3)
    part_up = w_up.astype(LOW).reshape(rows, pages, seqs, ff_rows).transpose(2, 0, 1, 3)
    sent = jnp.concatenate(
        [
            part_qkv.reshape(seqs, 3 * rows, span),
            jnp.broadcast_to(extra, (seqs,) + extra.shape),
            part_up.reshape(seqs, pages * rows * ff_rows // span, span),
        ],
        axis=1,
    )
    turned = jnp.stack(reorder(turn(sent, seqs, seq_index), seq_index))
    part_qkv = turned[:, : 3 * rows].reshape(seqs, 3, rows, span).transpose(1, 0, 2, 3)
    extras = turned[:, 3 * rows : 3 * rows + extra.shape[0]]
    part_up = turned[:, 3 * rows + extra.shape[0] :].reshape(seqs * rows, ff_here)
    digits = extras[:, small_rows : small_rows + 2 * page_count, :row_count].astype(jnp.int32)
    cells_all = digits[:, :page_count] * 16 + digits[:, page_count:]
    cells_all = jnp.stack(reorder([cells_all[k] for k in range(seqs)], seq_index), axis=1)
    cells_all = cells_all.reshape(page_count, slots)

    part_mix = w_out.astype(LOW).reshape(rows, width // span, span).transpose(1, 0, 2)
    part_small = extras[:, :small_rows, :lanes].transpose(1, 0, 2).reshape(small_rows, seqs * lanes)
    part_small = jnp.pad(part_small, ((0, -small_rows % 16), (0, span - seqs * lanes)))
    block = seqs * rows
    part_both = jnp.concatenate(
        [part_qkv.reshape(3 * block, span), part_mix.reshape(-1, span), part_small], axis=0
    )
    split = low_page[1:3][::-1]
    stack, rels = part_both[None], [0]
    for bit in low_page[:0:-1][: len(low_page) - 1 - len(split)]:
        stack = jnp.concatenate([stack, swap(stack, "page", pages, bit)], axis=0)
        rels = rels + [rel | bit for rel in rels]
    jumps = [0]
    for bit in split:
        jumps = jumps + [jump | bit for jump in jumps]
    across = [swap(stack, "page", pages, jump) for jump in jumps[1:]]
    beside = [swap(stack, "page", pages, 1)]
    x_near = [tokens]
    x_far = swap(after(tokens, part_both), "seq", seqs, low_seq[-1])
    *across, part_up, first_beside, x_far, w_down_low, x_own = fence(
        *across, part_up, beside[0], x_far, w_down.astype(LOW), tokens
    )
    beside = [first_beside] + [swap(array, "page", pages, 1) for array in across]
    both_pieces = [(array, [rel ^ jump for rel in rels]) for array, jump in zip([stack] + across, jumps)]
    both_pieces += [(array, [rel ^ jump ^ 1 for rel in rels]) for array, jump in zip(beside, jumps)]
    inputs = {0: x_own, low_seq[-1]: x_far}
    for bit in low_seq[:-1][::-1]:
        for rel in list(inputs):
            inputs[rel | bit] = swap(inputs[rel], "seq", seqs, bit)
    inputs = [inputs[rel] for rel in range(seqs)]
    feed_both = lax.all_gather(jnp.concatenate([part_up, w_down_low], axis=0), "page", axis=0, tiled=False)
    w_expand = feed_both[:, :block].reshape(width, ff_here)
    w_reduce = feed_both[:, block:].reshape(ff_here, width)
    fenced = fence(*[array for array, _ in both_pieces], *inputs)
    inputs = list(fenced[len(both_pieces) :])
    both_pieces = [(array, rel) for array, (_, rel) in zip(fenced[: len(both_pieces)], both_pieces)]
    both_rels = [rel for _, rel_list in both_pieces for rel in rel_list]
    vectors = jnp.concatenate([array[:, 4 * block :, :] for array, _ in both_pieces], axis=0)
    vectors = page_order(vectors[:, :small_rows, : seqs * lanes], both_rels, page_index)
    vectors = vectors.reshape(pages, small_rows, seqs * lanes).transpose(1, 0, 2)
    vectors = vectors.reshape(small_rows, width).astype(WIDE)
    hidden_bias = vectors[6:10].reshape(pages, seqs, ff_rows)
    hidden_bias = lax.dynamic_index_in_dim(hidden_bias, seq_index, 1, keepdims=False).reshape(1, ff_here)

    position = lax.broadcasted_iota(jnp.int32, (1, slots), 1)
    position = ((position // row_count) ^ seq_index) * row_count + position % row_count
    mask = jnp.where(position < lengths[:, None], 0.0, -1e30).astype(WIDE)[:, None, :]
    column, row = cells_all[:, :, None], cells_all[:, None, :]
    own_bias = lax.dynamic_slice_in_dim(cell_bias, seq_index * heads_here, heads_here)
    mix_part = jnp.concatenate([array[:, 3 * block : 4 * block, :] for array, _ in both_pieces], axis=0)
    mix_far = swap(mix_part, "seq", seqs, low_seq[-1])
    qkv, lse, w_proj, *contexts = attend(
        [(after(array, mix_part), rel_list) for array, rel_list in both_pieces],
        block,
        spot,
        own_bias,
        inputs,
        vectors,
        column,
        row,
        mask,
        heads_here,
        depth,
    )
    mix_part, mix_far, qkv, lse, w_proj, *contexts = fence(mix_part, mix_far, qkv, lse, w_proj, *contexts)
    mix_near = {0: mix_part, low_seq[-1]: mix_far}
    for bit in low_seq[:-1][::-1]:
        for rel in list(mix_near):
            mix_near[rel | bit] = swap(mix_near[rel], "seq", seqs, bit)
    contexts = exchange([context.reshape(flat, span) for context in contexts])
    w_mix = assemble_mix([mix_near[rel] for rel in range(seqs)], both_rels, spot, rows, width)

    flat_inputs = tokens.reshape(flat, width)
    normed, normed_low, hat, rstd = mix(spot, contexts, w_mix, flat_inputs, vectors)
    hidden, active, parts = {}, {}, {}

    def feed(rels, *others):
        for rel in rels:
            piece = after(normed_all[rel], *others)
            value = jnp.dot(piece, w_expand, preferred_element_type=WIDE) + hidden_bias
            active[rel] = gelu_exact(value).astype(LOW)
            part = jnp.dot(active[rel], w_reduce, preferred_element_type=WIDE)
            parts[rel] = part.astype(LOW) if rel % 2 else part
            hidden[rel] = value

    normed_all = gather_near(normed_low, seqs)
    feed(range(seqs // 2, seqs))
    far_parts = [swap(parts[rel], "seq", seqs, 1) for rel in range(seqs // 2 + 1, seqs, 2)]
    far_sums = [parts[rel] + part.astype(WIDE) for rel, part in zip(range(seqs // 2, seqs, 2), far_parts)]
    ready = far_sums[0].astype(LOW)
    far = swap(ready, "seq", seqs, seqs // 2)
    feed(range(seqs // 2), ready)
    keep, close = parts[0], swap(parts[1], "seq", seqs, 1)
    slopes = [
        0.5 * (1.0 + lax.erf(u * 0.7071067811865476)) + u * jnp.exp(-0.5 * u * u) * 0.3989422804014327
        for u in after([hidden[rel] for rel in range(seqs)], ready)
    ]
    active = [active[rel] for rel in range(seqs)]
    far, slopes = lax.optimization_barrier((far, slopes))
    output, grad_second, second_low, sums_two = second_norm(
        normed, keep, close, far, vectors, cotangent.reshape(flat, width)
    )

    expanded, parts, totals = [], [], []

    def feed_back(pieces):
        for piece in pieces:
            slope = slopes[len(parts)]
            value = jnp.einsum("td,fd->tf", piece, w_reduce, preferred_element_type=WIDE) * slope
            low = value.astype(LOW)
            part = jnp.einsum("tf,df->td", low, w_expand, preferred_element_type=WIDE)
            part = part.astype(LOW) if len(parts) % 2 else part
            expanded.append(low)
            totals.append(jnp.sum(value, axis=0))
            parts.append(part)
        if len(parts) == len(pieces):
            bases.extend(weight_grad(spot, active[: len(pieces)], pieces, pages, False))
        return tuple(parts + bases)

    bases = []
    second_all = gather_near(second_low, seqs, feed_back)
    feed_back(second_all[seqs // 2 :])
    keep, close, far, ready = scatter_near(parts[0::2], parts[1::2])
    half = seqs // 2
    if ff_here == width:
        first = list(zip(after(active[half:], ready, close), second_all[half:]))
        down_part, up_keep, *up_sends = weight_grad_pair(
            spot, first, bases[0], list(zip(normed_all, expanded)), pages
        )
    else:
        down_part = weight_grad(spot, active[half:], second_all[half:], pages, False, bases[0])[0]
        up_keep, *up_sends = weight_grad(spot, normed_all, expanded, pages, True)
    far, down_part, up_keep, *up_sends = fence(far, down_part, up_keep, *up_sends)
    down_sum = scatter_same(down_part)
    up_early = scatter_first(up_sends[0], pages)
    grad_first, first_low, sums_one, *mix_grads = first_norm_back(
        spot, grad_second, keep, close, far, hat, rstd, vectors, w_mix, contexts, pages
    )
    grad_contexts, mix_grads = mix_grads[:seqs], mix_grads[seqs:]
    grad_contexts = exchange(grad_contexts)
    if mix_grads:
        mix_keep, mix_send = mix_grads
        mix_parts = swap(mix_send, "seq", seqs, 1)
    else:
        context = jnp.concatenate(reorder(contexts, seq_index), axis=1)
        grad_mix = jnp.einsum("tc,td->cd", context, first_low, preferred_element_type=WIDE)
        mix_keep, mix_parts = scatter_start(grad_mix.reshape(pages, seqs, rows, width), "seq", seqs, 1, 1)
    mix_keep, mix_parts, up_early, *grad_contexts = fence(mix_keep, mix_parts, up_early, *grad_contexts)
    up_late = [scatter_first(send, pages) for send in up_sends[1:]]
    mix_total = (mix_keep + mix_parts.astype(WIDE)).reshape(pages, seqs // 2, rows, width)
    mix_keep, mix_parts = scatter_start(mix_total, "seq", seqs, 1, low_seq[1])
    grad_contexts = [grad.reshape(page_count, row_count, span) for grad in grad_contexts]
    grad_proj, sums_proj, cells_grad, proj_keep, proj_send = attend_back(
        spot, own_bias, qkv, lse, grad_contexts, inputs, column, row, mask, heads_here, depth, pages
    )
    grad_proj, sums_proj, cells_grad, proj_keep, proj_send, up_keep, mix_keep, mix_parts = fence(
        grad_proj, sums_proj, cells_grad, proj_keep, proj_send, up_keep, mix_keep, mix_parts
    )
    proj_got = scatter_first(proj_send, pages)
    cut = up_early.shape[1]
    sums = [up_keep[:, :cut] + after(up_early, down_sum).astype(WIDE)]
    sums += [up_keep[:, cut:] + part.astype(WIDE) for part in up_late]
    up_half = jnp.concatenate([part.astype(LOW) for part in sums], axis=1).reshape(-1, ff_here)
    up_sum = scatter_same(up_half)
    parts = input_grad(after(grad_proj, up_half), w_proj, seqs)
    packed = lanes % 32 == 0 and span % 128 == 0 and ff_rows % 128 == 0 and width % (seqs * ff_rows) == 0
    if packed:
        hidden_sum = functools.reduce(jnp.add, totals)[None]
        table = pack_small(
            spot, *after((sums_proj, cells_grad), parts), sums_one, sums_two, hidden_sum, pages, seqs
        )
        small_sums = to_all(table)
    else:
        small_sums = small_table(*after((sums_proj, cells_grad), parts))
    proj_got, proj_keep, mix_keep, mix_parts, small_sums, *parts = fence(
        proj_got, proj_keep, mix_keep, mix_parts, small_sums, *parts
    )
    proj_half = halved(proj_keep, proj_got)
    near_parts = [swap(part, "seq", seqs, 1) for part in after(parts[1::2], proj_half)]
    keep, close, far = scatter_far(parts[0::2], near_parts)
    proj_half = after(proj_half, up_sum)
    proj_sum = scatter_same(proj_half)
    grad_mix = add_wide(after(mix_keep, proj_half), mix_parts).reshape(pages, rows, width)
    up_sum, down_sum = after((up_sum, down_sum), grad_mix)
    mix_keep, mix_parts = scatter_start(grad_mix, "page", pages, 0, 1)
    down_keep, down_got = split_low(down_sum)
    up_rows = turn(up_sum.reshape(seqs, rows, ff_here), seqs, seq_index)
    mix_keep, mix_parts = scatter_start(mix_keep + mix_parts.astype(WIDE), "page", pages, 0, 2)
    grad_reduce = down_keep.astype(WIDE) + down_got.astype(WIDE)
    proj_sum, far, mix_keep, mix_parts, *up_rows = fence(proj_sum, far, mix_keep, mix_parts, *up_rows)
    proj_rows = turn(proj_sum.reshape(seqs, rows, 3 * span), seqs, seq_index)
    grad_expand = jnp.stack(reorder(up_rows, seq_index)).reshape(seqs, rows, pages, ff_rows).transpose(1, 2, 0, 3)
    grad_expand = grad_expand.reshape(rows, seqs * ff_here).astype(WIDE)
    grad_mix = mix_keep + mix_parts.astype(WIDE)
    grad_mix = scatter_bits(grad_mix, "page", pages, 0, low_page[2:]).reshape(rows, width)
    grad_qkv = jnp.stack(reorder(proj_rows, seq_index)).reshape(seqs, rows, 3, span).transpose(1, 2, 0, 3)
    grad_qkv = grad_qkv.reshape(rows, 3 * width).astype(WIDE)
    grad_inputs = grad_first.reshape(page_count, row_count, width) + (
        keep + close.astype(WIDE) + far.astype(WIDE)
    )

    summed = jnp.sum(small_sums, axis=0)
    if packed:
        cell_total = small_sums[:, 12, :heads_here].reshape(pages, seqs, heads_here)
        cell_total = jnp.sum(cell_total, axis=0).reshape(heads)
    else:
        cell_total = summed[12:].reshape(-1)[:heads]
    return (
        output.reshape(page_count, row_count, width),
        grad_inputs,
        grad_qkv,
        grad_mix,
        grad_expand,
        grad_reduce,
        summed[:10],
        summed[10:12],
        cell_total,
    )


def solution(mesh):
    counts = (mesh.shape["page"], mesh.shape["seq"])
    placed = (
        P("page", "seq", None),
        P("page", "seq"),
        P("page"),
        P("page", "seq", None),
        P(("page", "seq"), None),
        P(("page", "seq"), None),
        P(("page", "seq"), None),
        P(("page", "seq"), None),
        P(None, ("page", "seq")),
        P(None, ("page", "seq")),
        P(),
    )

    def step(*args):
        return local(counts, *args)

    return jax.shard_map(
        step,
        mesh=mesh,
        in_specs=placed,
        out_specs=(
            P("page", "seq", None),
            P("page", "seq", None),
            P(("page", "seq"), None),
            P(("page", "seq"), None),
            P(("page", "seq"), None),
            P(("page", "seq"), None),
            P(None, ("page", "seq")),
            P(None, ("page", "seq")),
            P(),
        ),
        check_vma=False,
    )
```
